32 devices in a mesh: space: 32 (over z, y, x, core).
Axes of the slice: x: 2, y: 2, z: 4, core: 2. Of those that a mesh axis runs over, the one named last changes fastest.
Arguments:
- positions: float32 [3, 131072], P(None, 'space'), may hold values from 1 to 128, as said below
- velocity: float32 [3, 131072], P(None, 'space'), may hold values from -5 to 5
- deformation: float32 [9, 131072], P(None, 'space'), may hold values from -0.6 to 1.6
- affine: float32 [9, 131072], P(None, 'space'), may hold values from -3 to 3
- particle_mass: float32 [131072], P('space'), may hold values from 0.05 to 0.3
- volume: float32 [131072], P('space'), may hold values from 0.06 to 0.25
- bin_block: int32 [256], P('space'), may hold values from 0 to 255
- live_count: int32 [32], P('space'), may hold values from 2 to 4, as said below
Outputs:
- displacement: float32 [3, 131072], P(None, 'space')
- new_velocity: float32 [3, 131072], P(None, 'space')
- new_deformation: float32 [9, 131072], P(None, 'space')
- new_affine: float32 [9, 131072], P(None, 'space')
The draws below stay inside these ranges and needn't reach their ends.
Inputs may be any that keep to these rules, and one draw needn't show every extreme that they name: `positions`: each particle lies inside its bin's block: 4 d + 1 to 4 d + 4 along the first dimension for the bins of device d, 4 (bin_block // 16) + 1 to 4 (bin_block // 16) + 4 along the second, 4 (bin_block % 16) + 1 to 4 (bin_block % 16) + 4 along the third. The live bins of device d are its first live_count[d] slots; devices 2 k and 2 k + 1 hold at most 6 live bins together, and some such pair holds exactly 6 in every draw.
All inputs are finite; a program needn't handle non-finite values.
Results may differ from the reference program's by a relative error of at most 0.0003.
Values sent between devices are 32-bit elements; how exact they have to be, the bound alone decides.
No kernel may reach another device: no remote copies, remote signals or barrier semaphores. Data moves between devices by JAX's collectives and lax.ppermute only.
A program may use at most 128 MiB of HBM per device.

```python
import math
import jax
import jax.numpy as jnp
from jax import lax

PPB = 512
BIN_CAP = 8
BY = 16
BZ = 16
STEPS = 3
BINS = 256
NGY = 66
NGZ = 66
N_SPACE = 32


def shared_blocks(key):
    return jax.random.randint(jax.random.fold_in(key, 7), (BINS,), 0, BY * BZ, dtype=jnp.int32)


def draw_bin_block(key, part):
    return shared_blocks(key)


def draw_positions(key, part):
    blocks = shared_blocks(key)
    home_devices = jnp.arange(BINS, dtype=jnp.int32) // BIN_CAP
    anchor = jnp.stack([4 * home_devices, 4 * (blocks // BZ), 4 * (blocks % BZ)]).astype(jnp.float32)
    fraction = jax.random.uniform(jax.random.fold_in(key, 8), (3, BINS, PPB), jnp.float32)
    return (anchor[:, :, None] + 1.0 + 3.0 * fraction).reshape(3, BINS * PPB)


def draw_deformation(key, part):
    identity = jnp.eye(3, dtype=jnp.float32).reshape(9, 1)
    noise_key = jax.random.fold_in(key, 9)
    noise = jnp.clip(0.15 * jax.random.normal(noise_key, (9, BINS * PPB), jnp.float32), -0.6, 0.6)
    return identity + noise


def draw_live_count(key, part):
    pair_total = N_SPACE // 2
    keys = [jax.random.fold_in(key, 20 + number) for number in range(5)]
    totals = jax.random.randint(keys[0], (pair_total,), 4, BIN_CAP - 1, dtype=jnp.int32)
    totals = totals.at[0].set(BIN_CAP - 2)
    lower_share = jnp.maximum(2, totals - (BIN_CAP - 4))
    upper_share = jnp.minimum(totals - 2, BIN_CAP - 4)
    share_span = upper_share - lower_share + 1
    random_picks = [jax.random.randint(keys[1 + number], (pair_total,), 0, 1 << 20, dtype=jnp.int32) % share_span for number in range(3)]
    smaller = lower_share + jnp.minimum(jnp.minimum(random_picks[0], random_picks[1]), random_picks[2])
    larger_share = totals - smaller
    flip_order = jax.random.randint(keys[4], (pair_total,), 0, 2, dtype=jnp.int32)
    first_count = jnp.where(flip_order == 1, smaller, larger_share)
    second_count = totals - first_count
    return jnp.stack([first_count, second_count], axis=1).reshape(N_SPACE).astype(jnp.int32)


def steps_of(key, dims, shards, low, top_value):
    loudness, own = 1.0, jax.random.fold_in(key, 6)
    for dim, parts in shards:
        draws = jnp.exp(jax.random.uniform(jax.random.fold_in(own, dim), (parts,), jnp.float32, low / len(shards), top_value / len(shards)))
        loudness = loudness * jnp.repeat(draws, dims[dim] // parts).reshape([-1 if axis == dim else 1 for axis in range(len(dims))])
    return loudness


def bell_draw(rng, dims, width, bound, shards=(), kind=jnp.bfloat16):
    values = width * jax.random.normal(rng, dims, jnp.float32)
    if shards:
        values = values * steps_of(rng, dims, shards, -0.22, 0.18)
    return jnp.clip(values, -bound, bound).astype(kind)


def setup_inputs(seed: int = 0) -> dict:
    splits = jax.random.split(jax.random.key(seed), 9)
    positions = draw_positions(jax.random.fold_in(splits[8], 71), 0)
    velocity = bell_draw(splits[1], (3, BINS * PPB), 1.0, 5.0, ((1, 32),), jnp.float32)
    deformation = draw_deformation(jax.random.fold_in(splits[8], 71), 0)
    affine = bell_draw(splits[3], (9, BINS * PPB), 0.5, 3.0, ((1, 32),), jnp.float32)
    particle_mass = jnp.clip(jnp.exp(math.log(0.3) - 1.7917595 * jax.random.uniform(splits[4], (BINS * PPB,), jnp.float32) ** steps_of(splits[4], (BINS * PPB,), ((0, 32),), -0.2, 0.2)), 0.05, 0.3)
    volume = jnp.clip(jnp.exp(math.log(0.25) - 1.4271164 * jax.random.uniform(splits[5], (BINS * PPB,), jnp.float32) ** steps_of(splits[5], (BINS * PPB,), ((0, 32),), -0.2, 0.2)), 0.06, 0.25)
    bin_block = draw_bin_block(jax.random.fold_in(splits[8], 71), 0)
    live_count = draw_live_count(jax.random.fold_in(splits[8], 71), 0)
    return dict(positions=positions, velocity=velocity, deformation=deformation, affine=affine, particle_mass=particle_mass, volume=volume, bin_block=bin_block, live_count=live_count)


mu_shear = 4.0
lame_first = 6.0
courant = 0.15
sound_speed = 3.7416573867739413
mass_floor = 0.05
gravity_x = 3.0
gravity_z = -9.0
highest = lax.Precision.HIGHEST

def spline(distance):
    magnitude = jnp.abs(distance)
    inner_part = 0.75 - magnitude * magnitude
    outer_part = 0.5 * (1.5 - magnitude) * (1.5 - magnitude)
    return jnp.where(magnitude < 0.5, inner_part, jnp.where(magnitude < 1.5, outer_part, 0.0 * magnitude))

def node_coords():
    numbers = jnp.arange(216, dtype=jnp.int32)
    return jnp.stack([numbers // 36, numbers // 6 % 6, numbers % 6]).astype(jnp.float32)

def spline_weights(local_coords):
    offsets = jnp.arange(6, dtype=jnp.int32).astype(jnp.float32)
    per_axis = [spline(offsets[None, :, None] - local_coords[number][:, None, :]) for number in range(3)]
    weight_table = per_axis[0][:, :, None, None, :] * per_axis[1][:, None, :, None, :] * per_axis[2][:, None, None, :, :]
    return weight_table.reshape(local_coords.shape[1], 216, local_coords.shape[2])

def block_anchor(home_devices, blocks):
    return jnp.stack([4 * home_devices, 4 * (blocks // BZ), 4 * (blocks % BZ)]).astype(jnp.float32)

def selectors(starts, node_total):
    columns = jnp.arange(node_total, dtype=jnp.int32)
    offsets = jnp.arange(6, dtype=jnp.int32)
    return (columns[None, None, :] == 4 * starts[:, None, None] + offsets[None, :, None]).astype(jnp.float32)

def plane_selector(select_y, select_z):
    joined = select_y[:, :, None, :, None] * select_z[:, None, :, None, :]
    return joined.reshape(select_y.shape[0], 36, select_y.shape[2] * select_z.shape[2])

def kirchhoff(deform):
    entries = [deform[number] for number in range(9)]
    determinant = entries[0] * (entries[4] * entries[8] - entries[5] * entries[7]) - entries[1] * (entries[3] * entries[8] - entries[5] * entries[6]) + entries[2] * (entries[3] * entries[7] - entries[4] * entries[6])
    pressure_term = lame_first * (determinant - 1.0) * determinant
    stress = []
    for outer_index in range(3):
        for inner_index in range(3):
            product = entries[3 * outer_index] * entries[3 * inner_index] + entries[3 * outer_index + 1] * entries[3 * inner_index + 1] + entries[3 * outer_index + 2] * entries[3 * inner_index + 2]
            if outer_index == inner_index:
                stress.append(mu_shear * (product - 1.0) + pressure_term)
            else:
                stress.append(mu_shear * product)
    return stress

def particle_to_grid(working, local_coords, weight_table, time_step):
    stress = kirchhoff(working[6:15])
    masses = working[24]
    volumes = working[25]
    affine_term = [masses * working[15 + number] - 4.0 * time_step * volumes * stress[number] for number in range(9)]
    momentum = []
    for outer_index in range(3):
        shifted = masses * working[3 + outer_index]
        for inner_index in range(3):
            shifted = shifted - affine_term[3 * outer_index + inner_index] * local_coords[inner_index]
        momentum.append(shifted)
    quantities = jnp.stack([masses] + momentum + affine_term)
    summed = jnp.einsum('cbp,bnp->bcn', quantities, weight_table, precision=highest)
    nodes = node_coords()
    moments = []
    for outer_index in range(3):
        total_moment = summed[:, 1 + outer_index]
        for inner_index in range(3):
            total_moment = total_moment + summed[:, 4 + 3 * outer_index + inner_index] * nodes[inner_index][None, :]
        moments.append(total_moment)
    return jnp.stack([summed[:, 0]] + moments, axis=1)

def scatter_tiles(node_tiles, select_y, select_z):
    select_plane = plane_selector(select_y, select_z)
    shaped = node_tiles.reshape(node_tiles.shape[0], 24, 36)
    spread = jnp.einsum('bqn,bnm->qm', shaped, select_plane, precision=highest)
    return spread.reshape(4, 6, select_y.shape[2], select_z.shape[2])

def tile_velocities(slab_velocity, select_y, select_z):
    select_plane = plane_selector(select_y, select_z)
    flat = slab_velocity.reshape(18, select_plane.shape[2])
    gathered = jnp.einsum('qm,bnm->bqn', flat, select_plane, precision=highest)
    return gathered.reshape(gathered.shape[0], 3, 216)

def grid_velocity(owned_planes, device, time_step, plane_total):
    node_mass = jnp.maximum(owned_planes[0], mass_floor)
    planes = 4 * device + jnp.arange(4, dtype=jnp.int32)
    column_y = jnp.arange(owned_planes.shape[2], dtype=jnp.int32)
    column_z = jnp.arange(owned_planes.shape[3], dtype=jnp.int32)
    along_x = owned_planes[1] / node_mass + time_step * gravity_x
    along_y = owned_planes[2] / node_mass
    along_z = owned_planes[3] / node_mass + time_step * gravity_z
    along_x = jnp.where((planes < 2)[:, None, None], jnp.maximum(along_x, 0.0), along_x)
    along_x = jnp.where((planes >= plane_total - 2)[:, None, None], jnp.minimum(along_x, 0.0), along_x)
    along_y = jnp.where((column_y < 2)[None, :, None], jnp.maximum(along_y, 0.0), along_y)
    along_y = jnp.where((column_y >= owned_planes.shape[2] - 2)[None, :, None], jnp.minimum(along_y, 0.0), along_y)
    along_z = jnp.where((column_z < 2)[None, None, :], jnp.maximum(along_z, 0.0), along_z)
    along_z = jnp.where((column_z >= owned_planes.shape[3] - 2)[None, None, :], jnp.minimum(along_z, 0.0), along_z)
    return jnp.stack([along_x, along_y, along_z])

def grid_to_particle(working, local_coords, weight_table, velocity_tiles, time_step):
    nodes = node_coords()
    node_terms = [velocity_tiles[:, number] for number in range(3)]
    for outer_index in range(3):
        for inner_index in range(3):
            node_terms.append(velocity_tiles[:, outer_index] * nodes[inner_index][None, :])
    stacked = jnp.stack(node_terms, axis=1)
    interpolated = jnp.einsum('bcn,bnp->cbp', stacked, weight_table, precision=highest)
    new_motion = interpolated[0:3]
    affine_new = []
    for outer_index in range(3):
        for inner_index in range(3):
            affine_new.append(4.0 * (interpolated[3 + 3 * outer_index + inner_index] - new_motion[outer_index] * local_coords[inner_index]))
    deform = working[6:15]
    deform_new = []
    for outer_index in range(3):
        for inner_index in range(3):
            updated = deform[3 * outer_index + inner_index]
            for middle_index in range(3):
                updated = updated + time_step * affine_new[3 * outer_index + middle_index] * deform[3 * middle_index + inner_index]
            deform_new.append(updated)
    moved = working[0:3] + time_step * new_motion
    travelled = working[26:29] + time_step * new_motion
    return jnp.concatenate([moved, new_motion, jnp.stack(deform_new), jnp.stack(affine_new), working[24:26], travelled])

def prepare(working, device, device_blocks):
    home_devices = jnp.zeros_like(device_blocks) + device
    anchor = block_anchor(home_devices, device_blocks)
    local_coords = working[0:3] - anchor[:, :, None]
    return (local_coords, spline_weights(local_coords))

def reference(positions, velocity, deformation, affine, particle_mass, volume, bin_block, live_count):
    slot_ids = jnp.arange(BIN_CAP, dtype=jnp.int32)
    live_slots = (slot_ids[None, :] < live_count[:, None]).astype(jnp.float32)
    masked_mass = particle_mass.reshape(N_SPACE, BIN_CAP, PPB) * live_slots[:, :, None]
    masked_volume = volume.reshape(N_SPACE, BIN_CAP, PPB) * live_slots[:, :, None]
    grouped = jnp.concatenate([positions, velocity, deformation, affine]).reshape(24, N_SPACE, BIN_CAP, PPB)
    travelled = jnp.zeros((3, N_SPACE, BIN_CAP, PPB), jnp.float32)
    particle_state = jnp.concatenate([grouped, masked_mass[None], masked_volume[None], travelled]).transpose(1, 0, 2, 3)
    blocks = bin_block.reshape(N_SPACE, BIN_CAP)
    devices = jnp.arange(N_SPACE, dtype=jnp.int32)
    plane_total = 4 * N_SPACE
    for iteration in range(STEPS):
        speed_squared = jnp.where(particle_state[:, 24] > 0.0, lax.optimization_barrier(jnp.sum(particle_state[:, 3:6] * particle_state[:, 3:6], axis=1)), 0.0)
        time_step = courant / (jnp.sqrt(jnp.max(speed_squared)) + sound_speed)

        def partial_of(inputs):
            device, working, device_blocks = inputs
            local_coords, weight_table = prepare(working, device, device_blocks)
            node_tiles = particle_to_grid(working, local_coords, weight_table, time_step)
            return scatter_tiles(node_tiles, selectors(device_blocks // BZ, NGY), selectors(device_blocks % BZ, NGZ))
        partials = lax.map(partial_of, (devices, particle_state, blocks))
        incoming = jnp.concatenate([jnp.zeros((1, 4, 2, NGY, NGZ), jnp.float32), partials[:-1, :, 4:6]])
        owned_planes = jnp.concatenate([partials[:, :, 0:2] + incoming, partials[:, :, 2:4]], axis=2)
        motion = jax.vmap(grid_velocity, in_axes=(0, 0, None, None))(owned_planes, devices, time_step, plane_total)
        ghost_planes = jnp.concatenate([motion[1:, :, 0:2], jnp.zeros((1, 3, 2, NGY, NGZ), jnp.float32)])
        slab_velocity = jnp.concatenate([motion, ghost_planes], axis=2)

        def update_of(inputs):
            device, working, device_blocks, device_velocity = inputs
            local_coords, weight_table = prepare(working, device, device_blocks)
            velocity_tiles = tile_velocities(device_velocity, selectors(device_blocks // BZ, NGY), selectors(device_blocks % BZ, NGZ))
            return grid_to_particle(working, local_coords, weight_table, velocity_tiles, time_step)
        particle_state = lax.map(update_of, (devices, particle_state, blocks, slab_velocity))
    finished = jnp.concatenate([particle_state[:, 26:29], particle_state[:, 3:24]], axis=1) * live_slots[:, None, :, None]
    flattened = finished.transpose(1, 0, 2, 3).reshape(24, BINS * PPB)
    return (flattened[0:3], flattened[3:6], flattened[6:15], flattened[15:24])
```

```python
import functools

import jax
import jax.numpy as jnp
from jax import lax
from jax.experimental import pallas as pl
from jax.experimental.pallas import tpu as pltpu
from jax.sharding import PartitionSpec as P

BZ = 16
STEPS = 3
NGY = 66
NGZ = 66

mu_shear = 4.0
lame_first = 6.0
courant = 0.15
sound_speed = 3.7416573867739413
mass_floor = 0.05
gravity_x = 3.0
gravity_z = -9.0

LANES = 128
TILE = 36
PITCH = 40
META = 112
SPEED = 7
BIG = 3.0e38
F32 = jnp.float32
BF16 = jnp.bfloat16
INTERPRET = False

POS, VEL, DEF, AFF, MASS, VOL, TRAV = 0, 3, 6, 15, 24, 25, 26
ROWS = 29


def iota(shape, dim):
    return lax.broadcasted_iota(jnp.int32, shape, dim)


def split(value):
    high = value.astype(BF16)
    low = (value - high.astype(F32)).astype(BF16)
    return high, low


def dot_nt(a, b):
    return lax.dot_general(a, b, (((1,), (1,)), ((), ())), preferred_element_type=F32)


def dot_nn(a, b):
    return lax.dot_general(a, b, (((1,), (0,)), ((), ())), preferred_element_type=F32)


def spline(distance):
    magnitude = jnp.abs(distance)
    outer = jnp.maximum(1.5 - magnitude, 0.0)
    inner = jnp.maximum(0.5 - magnitude, 0.0)
    return 0.5 * outer * outer - 1.5 * inner * inner


def spread(value, bin_index, quarters):
    parts = [
        jnp.broadcast_to(value[row : row + 1, :], (8, LANES))
        for row in range(bin_index * quarters, (bin_index + 1) * quarters)
    ]
    return jnp.concatenate(parts, axis=1)


def bin_weights(local, bin_index, quarters, table):
    along_x, along_y, along_z = [spread(local[axis], bin_index, quarters) for axis in range(3)]
    width = along_x.shape[1]
    first = [spline(float(a) - along_x) for a in range(6)]
    first_moved = [first[a] * (float(a) - along_x) for a in range(6)]
    third_node = iota((8, width), 0)
    third_offset = third_node.astype(F32) - along_z
    third = jnp.where(third_node < 6, spline(third_offset), 0.0)
    third_moved = third * third_offset
    for a in range(6):
        second = spline(float(a) - along_y)
        second_moved = second * (float(a) - along_y)
        table[pl.ds(6 * a, 8), :] = second * third
        table[pl.ds(PITCH + 6 * a, 8), :] = second_moved * third
        table[pl.ds(2 * PITCH + 6 * a, 8), :] = second * third_moved
    return first, first_moved


def clear_pads(table):
    width = table.shape[1]
    for part in range(3):
        table[pl.ds(part * PITCH + PITCH - 8, 8), :] = jnp.zeros((8, width), F32)


def kirchhoff(deform):
    determinant = (
        deform[0] * (deform[4] * deform[8] - deform[5] * deform[7])
        - deform[1] * (deform[3] * deform[8] - deform[5] * deform[6])
        + deform[2] * (deform[3] * deform[7] - deform[4] * deform[6])
    )
    pressure = lame_first * (determinant - 1.0) * determinant
    stress = [None] * 9
    for r in range(3):
        for c in range(r, 3):
            product = (
                deform[3 * r] * deform[3 * c]
                + deform[3 * r + 1] * deform[3 * c + 1]
                + deform[3 * r + 2] * deform[3 * c + 2]
            )
            if r == c:
                stress[3 * r + c] = mu_shear * (product - 1.0) + pressure
            else:
                stress[3 * r + c] = mu_shear * product
                stress[3 * c + r] = stress[3 * r + c]
    return stress


def to_grid(state, local, blocks, device, bins, device_total, table, shuffle, tiles, message):
    rows = state[0].shape[0]
    quarters = rows // bins
    deform = state[DEF : DEF + 9]
    mass, volume = state[MASS], state[VOL]
    velocity = state[VEL : VEL + 3]
    speed = velocity[0] * velocity[0] + velocity[1] * velocity[1] + velocity[2] * velocity[2]
    speed = jnp.max(jnp.where(mass > 0.0, speed, 0.0), axis=0, keepdims=True)
    speed = jnp.max(speed, axis=1, keepdims=True)

    stress = kirchhoff(deform)
    scaled = 4.0 * volume
    span = 8 * rows
    zero = jnp.zeros((rows, LANES), F32)

    def put(matrix, row, value):
        shuffle[pl.ds(matrix * span + row, rows, stride=8), :] = value

    put(0, 0, mass)
    for c in range(3):
        put(0, 1 + c, mass * velocity[c])
        put(0, 4 + c, zero)
    put(0, 7, zero)
    for axis in range(3):
        put(1 + axis, 0, zero)
        put(1 + axis, 7, zero)
        for c in range(3):
            put(1 + axis, 1 + c, mass * state[AFF + 3 * c + axis])
            put(1 + axis, 4 + c, scaled * stress[3 * c + axis])

    for b in range(bins):
        first, first_moved = bin_weights(local, b, quarters, table)

        def channel(matrix):
            begin = matrix * span + 8 * b * quarters
            return jnp.concatenate(
                [shuffle[pl.ds(begin + 8 * q, 8), :] for q in range(quarters)], axis=1
            )

        base, slope_x, slope_y, slope_z = [channel(matrix) for matrix in range(4)]
        lefts = [
            jnp.concatenate([first[a] * base + first_moved[a] * slope_x for a in range(6)], axis=0),
            jnp.concatenate([first[a] * slope_y for a in range(6)], axis=0),
            jnp.concatenate([first[a] * slope_z for a in range(6)], axis=0),
        ]
        total = None
        for part in range(3):
            left_high, left_low = split(lefts[part])
            right_high, right_low = split(table[pl.ds(part * PITCH, PITCH), :])
            product = (
                dot_nt(left_high, right_high)
                + dot_nt(left_high, right_low)
                + dot_nt(left_low, right_high)
            )
            total = product if total is None else total + product
        tiles[:, TILE * b : TILE * (b + 1)] = total[:, 0:TILE]

    lane = iota((1, LANES), 1)
    meta = jnp.where(lane == SPEED, speed, 0.0)
    for b in range(bins):
        meta = jnp.where(lane == b, blocks[b].astype(F32), meta)
    row = iota((8, LANES), 0)
    lanes = iota((8, LANES), 1)
    extra = bins * TILE - LANES

    def packed(plane):
        body = tiles[pl.ds(8 * plane, 8), 0:LANES]
        rest = jnp.where(lanes < extra, tiles[pl.ds(8 * plane, 8), LANES : 2 * LANES], 0.0)
        rest = jnp.where(row == 7, jnp.broadcast_to(meta, (8, LANES)), rest)
        rest = pltpu.roll(rest, 0, 1, stride=extra, stride_axis=0)
        folded = jnp.sum(rest, axis=0, keepdims=True)
        return jnp.where(row == 7, jnp.broadcast_to(folded, (8, LANES)), body)

    low = [packed(0), packed(1)]
    high = [packed(4), packed(5)]

    def send(index, carry):
        message[index, 0:8, :] = low[0]
        message[index, 8:16, :] = low[1]
        return carry

    lax.fori_loop(0, device_total, send, 0)

    @pl.when(device + 1 < device_total)
    def _():
        message[device + 1, 0:8, :] = high[0]
        message[device + 1, 8:16, :] = high[1]


def unpacked(block, bins):
    row = iota((8, LANES), 0)
    lanes = iota((8, LANES), 1)
    extra = bins * TILE - LANES
    folded = jnp.broadcast_to(block[7:8, :], (8, LANES))
    rest = folded
    for bit in (1, 2, 4):
        rest = jnp.where(row & bit > 0, pltpu.roll(rest, LANES - bit * extra, 1), rest)
    rest = jnp.where((lanes < extra) & (row < 7), rest, 0.0)
    body = jnp.where(row < 7, block, 0.0)
    return jnp.concatenate([body, rest], axis=1)


def node_key(block, node):
    block_y = jnp.floor((block + 0.5) * (1.0 / BZ))
    block_z = block - BZ * block_y
    node_y = jnp.floor((node + 0.5) * (1.0 / 6.0))
    node_z = node - 6.0 * node_y
    return 4.0 * block_y + node_y, 4.0 * block_z + node_z


def to_particles(state, local, blocks, device, bins, device_total, tiles, received, table, shuffle, live):
    rows = state[0].shape[0]
    quarters = rows // bins
    width = bins * LANES
    nodes = bins * TILE
    speeds = jnp.max(received[:, 7, :], axis=0, keepdims=True)
    lane = iota((1, LANES), 1)
    fastest = jnp.max(jnp.where(lane == META + SPEED, speeds, 0.0), axis=1, keepdims=True)
    time_step = courant / (jnp.sqrt(fastest) + sound_speed)

    left_index = jnp.maximum(device - 1, 0)
    right_index = jnp.minimum(device + 1, device_total - 1)
    left_live = jnp.where(device > 0, 1.0, 0.0)
    right_live = jnp.where(device + 1 < device_total, 1.0, 0.0)
    left_block = received[left_index]
    right_block = received[right_index]
    left_meta = left_block[7:8, :]
    right_meta = right_block[7:8, :]

    position = iota((1, width), 1)
    column_bin = position // LANES
    column_slot = position - LANES * column_bin
    column_part = jnp.where(column_slot >= 2 * PITCH, 2, jnp.where(column_slot >= PITCH, 1, 0))
    column_node = column_slot - PITCH * column_part
    column_valid = (column_node < TILE) & (column_slot < 3 * PITCH)
    column_block = jnp.zeros((1, width), F32)
    for b in range(bins):
        column_block = jnp.where(column_bin == b, blocks[b].astype(F32), column_block)
    column_y, column_z = node_key(column_block, column_node.astype(F32))
    column_key = jnp.where(column_valid, LANES * column_y + column_z, -1.0)

    source = iota((nodes, 1), 0).astype(F32)
    source_bin = jnp.floor((source + 0.5) * (1.0 / TILE))
    source_node = source - TILE * source_bin

    def placing(values):
        source_block = jnp.zeros((nodes, 1), F32)
        for b in range(bins):
            source_block = jnp.where(source_bin == float(b), values[b], source_block)
        row_y, row_z = node_key(source_block, source_node)
        return jnp.where(LANES * row_y + row_z == column_key, 1.0, 0.0).astype(BF16)

    def meta_values(meta):
        return [
            jnp.max(jnp.where(lane == META + b, meta, 0.0), axis=1, keepdims=True)
            for b in range(bins)
        ]

    def placed(values, selector):
        count = values.shape[0]
        high, low = split(values)
        result = dot_nn(jnp.concatenate([high, low], axis=0), selector)
        return result[0:count] + result[count : 2 * count]

    own = placed(tiles[:, 0:nodes], placing([blocks[b].astype(F32) for b in range(bins)]))
    left_values = jnp.concatenate(
        [unpacked(left_block[0:8, :], bins), unpacked(left_block[8:16, :], bins)], axis=0
    )
    right_values = jnp.concatenate(
        [unpacked(right_block[0:8, :], bins), unpacked(right_block[8:16, :], bins)], axis=0
    )
    left = placed(left_values[:, 0:nodes] * left_live, placing(meta_values(left_meta)))
    right = placed(right_values[:, 0:nodes] * right_live, placing(meta_values(right_meta)))

    sub = iota((8, width), 0)
    wide_y = jnp.broadcast_to(column_y, (8, width))
    wide_z = jnp.broadcast_to(column_z, (8, width))
    wide_valid = jnp.broadcast_to(column_key, (8, width)) >= 0.0
    component = (sub >= 1) & (sub <= 3) & wide_valid
    floor_of = jnp.where(
        ((sub == 2) & (wide_y < 2.0)) | ((sub == 3) & (wide_z < 2.0)), 0.0, -BIG
    )
    roof_of = jnp.where(
        ((sub == 2) & (wide_y >= NGY - 2.0)) | ((sub == 3) & (wide_z >= NGZ - 2.0)), 0.0, BIG
    )
    pull = time_step * jnp.where(
        sub == 1, gravity_x, jnp.where(sub == 3, gravity_z, 0.0)
    )
    plane_total = 4 * device_total
    slot = iota((8, LANES), 1)
    lower_half, upper_half = [], []
    for a in range(6):
        sums = own[8 * a : 8 * a + 8]
        if a < 2:
            sums = sums + left[8 * a : 8 * a + 8]
        if a >= 4:
            sums = sums + right[8 * a - 32 : 8 * a - 24]
        plane = 4 * device + a
        node_mass = jnp.maximum(jnp.broadcast_to(sums[0:1, :], (8, width)), mass_floor)
        per_step = pltpu.roll(sums, 5, 0)
        motion = (sums - time_step * per_step) / node_mass + pull
        lowest = jnp.where(plane < 2, 0.0, -BIG)
        highest = jnp.where(plane >= plane_total - 2, 0.0, BIG)
        motion = jnp.maximum(motion, jnp.where(sub == 1, lowest, floor_of))
        motion = jnp.minimum(motion, jnp.where(sub == 1, highest, roof_of))
        inside = jnp.where(plane < plane_total, 1, 0)
        motion = jnp.where(component & (inside > 0), motion, 0.0)
        moved = pltpu.roll(motion, 3, 0)
        for b in range(bins):
            here = motion[:, LANES * b : LANES * (b + 1)]
            there = moved[:, LANES * b : LANES * (b + 1)]
            lower_half.append(
                jnp.where(slot < PITCH, here, jnp.where(slot < 2 * PITCH, there, 0.0))
            )
            upper_half.append(jnp.where(slot >= 2 * PITCH, here, 0.0))

    span = 8 * rows
    for b in range(bins):
        first, first_moved = bin_weights(local, b, quarters, table)
        motions = jnp.concatenate(
            [half[bins * a + b] for a in range(6) for half in (lower_half, upper_half)], axis=0
        )[:, 0 : 3 * PITCH]
        count = motions.shape[0]
        high, low = split(motions)
        right_high, right_low = split(table[pl.ds(0, 3 * PITCH), :])
        product = dot_nn(jnp.concatenate([high, low], axis=0), right_high)
        product = product[0:count] + product[count : 2 * count] + dot_nn(high, right_low)
        sums = [None, None, None]
        for a in range(6):
            top = product[16 * a : 16 * a + 8]
            bottom = product[16 * a + 8 : 16 * a + 16]
            terms = (first[a] * top, first[a] * bottom, first_moved[a] * top)
            sums = [t if s is None else s + t for s, t in zip(sums, terms)]
        for kind in range(3):
            for q in range(quarters):
                begin = kind * span + 8 * (b * quarters + q)
                shuffle[pl.ds(begin, 8), :] = sums[kind][:, LANES * q : LANES * (q + 1)]

    def take(kind, row):
        return shuffle[pl.ds(kind * span + row, rows, stride=8), :]

    velocity = [take(0, 1 + c) for c in range(3)]
    affine = [None] * 9
    for c in range(3):
        affine[3 * c] = 4.0 * take(2, 1 + c)
        affine[3 * c + 1] = 4.0 * take(0, 4 + c)
        affine[3 * c + 2] = 4.0 * take(1, 1 + c)
    old = state[DEF : DEF + 9]
    deform = []
    for r in range(3):
        for c in range(3):
            change = (
                affine[3 * r] * old[c] + affine[3 * r + 1] * old[3 + c] + affine[3 * r + 2] * old[6 + c]
            )
            deform.append(old[3 * r + c] + time_step * change)
    steps = [time_step * velocity[c] for c in range(3)]
    moved = [local[c] + steps[c] for c in range(3)]
    travelled = [state[TRAV + c] + steps[c] for c in range(3)]
    return moved + velocity + deform + affine + [state[MASS], state[VOL]] + travelled


def read_state(ref, rows):
    return [ref[pl.ds(rows * number, rows), :] for number in range(ROWS)]


def write_state(ref, state):
    rows = state[0].shape[0]
    for number in range(ROWS):
        ref[pl.ds(rows * number, rows), :] = state[number]


def first_kernel(
    bins, device_total, blocks, live, x_ref, v_ref, f_ref, c_ref, m_ref, vol_ref,
    state_ref, tiles, message, table, shuffle, device_of,
):
    device = device_of()
    rows = state_ref.shape[0] // ROWS
    quarters = rows // bins
    begin = 0
    for ref, count in ((x_ref, 3), (v_ref, 3), (f_ref, 9), (c_ref, 9)):
        for number in range(count):
            for s in range(rows):
                target = rows * (begin + number) + s
                state_ref[pl.ds(target, 1), :] = ref[
                    pl.ds(number, 1), pl.ds(LANES * s, LANES)
                ]
        begin += count
    for ref, number in ((m_ref, MASS), (vol_ref, VOL)):
        for b in range(bins):
            alive = jnp.where(b < live[0], 1.0, 0.0)
            for q in range(quarters):
                s = quarters * b + q
                piece = ref[pl.ds(LANES * s, LANES)].reshape(1, LANES)
                state_ref[pl.ds(rows * number + s, 1), :] = piece * alive
    home = jnp.zeros((rows, LANES), F32)
    home_y, home_z = home, home
    row_bin = iota((rows, LANES), 0) // quarters
    for b in range(bins):
        block = blocks[b]
        block_y = block // BZ
        block_z = block - BZ * block_y
        home_y = jnp.where(row_bin == b, (4 * block_y).astype(F32), home_y)
        home_z = jnp.where(row_bin == b, (4 * block_z).astype(F32), home_z)
    anchors = (home + (4 * device).astype(F32), home_y, home_z)
    for axis in range(3):
        place = pl.ds(rows * axis, rows)
        state_ref[place, :] = state_ref[place, :] - anchors[axis]
        state_ref[pl.ds(rows * (TRAV + axis), rows), :] = home
    clear_pads(table)
    state = read_state(state_ref, rows)
    to_grid(
        state, state[0:3], blocks, device, bins, device_total, table, shuffle, tiles, message
    )


def middle_kernel(
    bins, device_total, blocks, live, old_ref, old_tiles, received,
    state_ref, tiles, message, table, shuffle, device_of,
):
    device = device_of()
    rows = state_ref.shape[0] // ROWS
    clear_pads(table)
    state = read_state(old_ref, rows)
    state = to_particles(
        state, state[0:3], blocks, device, bins, device_total, old_tiles, received, table,
        shuffle, live,
    )
    write_state(state_ref, state)
    state = read_state(state_ref, rows)
    to_grid(
        state, state[0:3], blocks, device, bins, device_total, table, shuffle, tiles, message
    )


def last_kernel(
    bins, device_total, blocks, live, old_ref, old_tiles, received,
    d_out, v_out, f_out, c_out, table, shuffle, device_of,
):
    device = device_of()
    rows = old_ref.shape[0] // ROWS
    quarters = rows // bins
    clear_pads(table)
    state = read_state(old_ref, rows)
    state = to_particles(
        state, state[0:3], blocks, device, bins, device_total, old_tiles, received, table,
        shuffle, live,
    )
    row_bin = iota((rows, LANES), 0) // quarters
    alive = row_bin < live[0]
    half = rows * LANES
    for ref, begin, count in ((d_out, TRAV, 3), (v_out, VEL, 3), (f_out, DEF, 9), (c_out, AFF, 9)):
        for number in range(count):
            value = jnp.where(alive, state[begin + number], 0.0)
            for s in range(rows):
                ref[pl.ds(number, 1), pl.ds(LANES * s, LANES)] = value[s : s + 1, :]
        total = ref.shape[1]
        ref[:, pl.ds(half, total - half)] = jnp.zeros((count, total - half), F32)


def local(positions, velocity, deformation, affine, particle_mass, volume, bin_block, live_count):
    slot_total = bin_block.shape[0]
    per_bin = positions.shape[1] // slot_total
    bins = slot_total // 2
    device_total = lax.axis_size("space")
    rows = bins * per_bin // LANES
    half = rows * LANES
    nodes = bins * TILE
    state_shape = jax.ShapeDtypeStruct((ROWS * rows, LANES), F32)
    tiles_shape = jax.ShapeDtypeStruct((48, 2 * LANES), F32)
    message_shape = jax.ShapeDtypeStruct((device_total, 16, LANES), F32)
    smem = pl.BlockSpec(memory_space=pltpu.SMEM)
    vmem = pl.BlockSpec(memory_space=pltpu.VMEM)
    scratch = [
        pltpu.VMEM((3 * PITCH, per_bin), F32),
        pltpu.VMEM((4 * 8 * rows, LANES), F32),
    ]
    me = lax.axis_index("space").astype(jnp.int32).reshape(1)

    def call(body, in_specs, out_shape, out_specs, arguments, grid=None):
        def kernel(blocks, live, me_ref, *refs):
            functools.partial(body, bins, device_total, blocks, live)(
                *refs, device_of=lambda: me_ref[0]
            )

        extra = {} if grid is None else {"grid": grid}
        return pl.pallas_call(
            kernel,
            in_specs=[smem, smem, smem] + in_specs,
            out_shape=out_shape,
            out_specs=out_specs,
            scratch_shapes=scratch,
            interpret=INTERPRET,
            **extra,
        )(bin_block, live_count, me, *arguments)

    def first_half(count):
        return pl.BlockSpec((count, half), lambda i: (0, 0))

    flat_half = pl.BlockSpec((half,), lambda i: (0,))
    middle_shapes = (state_shape, tiles_shape, message_shape)
    state, tiles, message = call(
        first_kernel,
        [first_half(3), first_half(3), first_half(9), first_half(9), flat_half, flat_half],
        middle_shapes,
        tuple(
            pl.BlockSpec(shape.shape, lambda i, rank=len(shape.shape): (0,) * rank)
            for shape in middle_shapes
        ),
        (positions, velocity, deformation, affine, particle_mass, volume),
        grid=(1,),
    )
    for step in range(STEPS):
        received = lax.all_to_all(message, "space", 0, 0, tiled=True)
        if step < STEPS - 1:
            state, tiles, message = call(
                middle_kernel, [vmem, vmem, vmem], middle_shapes, (vmem, vmem, vmem),
                (state, tiles, received),
            )
        else:
            total = positions.shape[1]
            out_shape = tuple(jax.ShapeDtypeStruct((count, total), F32) for count in (3, 3, 9, 9))
            return call(
                last_kernel, [vmem, vmem, vmem], out_shape, (vmem,) * 4, (state, tiles, received)
            )


def solution(mesh):
    in_specs = (
        P(None, "space"),
        P(None, "space"),
        P(None, "space"),
        P(None, "space"),
        P("space"),
        P("space"),
        P("space"),
        P("space"),
    )
    out_specs = (P(None, "space"), P(None, "space"), P(None, "space"), P(None, "space"))
    return jax.shard_map(local, mesh=mesh, in_specs=in_specs, out_specs=out_specs, check_vma=False)
```

```python
import jax
import jax.numpy as jnp
from jax import lax
from jax.experimental import pallas as pl
from jax.experimental.pallas import tpu as pltpu
from jax.sharding import PartitionSpec as P

BZ = 16
STEPS = 3
NGY = 66
NGZ = 66

mu_shear = 4.0
lame_first = 6.0
courant = 0.15
sound_speed = 3.7416573867739413
mass_floor = 0.05
gravity_x = 3.0
gravity_z = -9.0

LANES = 128
TILE = 36
PITCH = 40
META = 112
BIG = 3.0e38
GRANT = 8 * 2**20
F32 = jnp.float32
BF16 = jnp.bfloat16
INTERPRET = False

POS, VEL, DEF, AFF, MASS, VOL, TRAV = 0, 3, 6, 15, 24, 25, 26
ROWS = 29


def iota(shape, dim):
    return lax.broadcasted_iota(jnp.int32, shape, dim)


def split(value):
    high = value.astype(BF16)
    low = (value - high.astype(F32)).astype(BF16)
    return high, low


def dot_nt(a, b):
    return lax.dot_general(a, b, (((1,), (1,)), ((), ())), preferred_element_type=F32)


def dot_nn(a, b):
    return lax.dot_general(a, b, (((1,), (0,)), ((), ())), preferred_element_type=F32)


def spline(distance):
    magnitude = jnp.abs(distance)
    outer = jnp.maximum(1.5 - magnitude, 0.0)
    inner = jnp.maximum(0.5 - magnitude, 0.0)
    return 0.5 * outer * outer - 1.5 * inner * inner


def spread(value, bin_index, quarters):
    parts = [
        jnp.broadcast_to(value[row : row + 1, :], (8, LANES))
        for row in range(bin_index * quarters, (bin_index + 1) * quarters)
    ]
    return jnp.concatenate(parts, axis=1)


def bin_weights(local, bin_index, quarters, table, along):
    along_x, along_y, along_z = [spread(local[axis], bin_index, quarters) for axis in range(3)]
    width = along_x.shape[1]
    first = [spline(float(a) - along_x) for a in range(6)]
    first_moved = [first[a] * (float(a) - along_x) for a in range(6)]
    for a in range(6):
        along[pl.ds(16 * bin_index + a, 1), :] = first[a][0:1, :]
        along[pl.ds(16 * bin_index + 8 + a, 1), :] = first_moved[a][0:1, :]
    third_node = iota((8, width), 0)
    third_offset = third_node.astype(F32) - along_z
    third = jnp.where(third_node < 6, spline(third_offset), 0.0)
    third_moved = third * third_offset
    for a in range(6):
        second = spline(float(a) - along_y)
        second_moved = second * (float(a) - along_y)
        table[pl.ds(6 * a, 8), :] = second * third
        table[pl.ds(PITCH + 6 * a, 8), :] = second_moved * third
        table[pl.ds(2 * PITCH + 6 * a, 8), :] = second * third_moved
    return first, first_moved


def clear_pads(table):
    width = table.shape[1]
    for part in range(3):
        table[pl.ds(part * PITCH + PITCH - 8, 8), :] = jnp.zeros((8, width), F32)


def kirchhoff(deform):
    determinant = (
        deform[0] * (deform[4] * deform[8] - deform[5] * deform[7])
        - deform[1] * (deform[3] * deform[8] - deform[5] * deform[6])
        + deform[2] * (deform[3] * deform[7] - deform[4] * deform[6])
    )
    pressure = lame_first * (determinant - 1.0) * determinant
    stress = [None] * 9
    for r in range(3):
        for c in range(r, 3):
            product = (
                deform[3 * r] * deform[3 * c]
                + deform[3 * r + 1] * deform[3 * c + 1]
                + deform[3 * r + 2] * deform[3 * c + 2]
            )
            if r == c:
                stress[3 * r + c] = mu_shear * (product - 1.0) + pressure
            else:
                stress[3 * r + c] = mu_shear * product
                stress[3 * c + r] = stress[3 * r + c]
    return stress


def send_speed(velocity, mass, speeds):
    speed = velocity[0] * velocity[0] + velocity[1] * velocity[1] + velocity[2] * velocity[2]
    speed = jnp.max(jnp.where(mass > 0.0, speed, 0.0), axis=0, keepdims=True)
    speed = jnp.max(speed, axis=1, keepdims=True)
    speeds[...] = jnp.broadcast_to(speed, speeds.shape)


def to_grid(state, device, bins, meta, tiles, near, far, highs, lows, along, table, shuffle):
    rows = state[0].shape[0]
    quarters = rows // bins
    deform = state[DEF : DEF + 9]
    mass, volume = state[MASS], state[VOL]
    velocity = state[VEL : VEL + 3]
    stress = kirchhoff(deform)
    scaled = 4.0 * volume
    span = 8 * rows
    zero = jnp.zeros((rows, LANES), F32)

    def put(matrix, row, value):
        shuffle[pl.ds(matrix * span + row, rows, stride=8), :] = value

    put(0, 0, mass)
    for c in range(3):
        put(0, 1 + c, mass * velocity[c])
        put(0, 4 + c, zero)
    put(0, 7, zero)
    for axis in range(3):
        put(1 + axis, 0, zero)
        put(1 + axis, 7, zero)
        for c in range(3):
            put(1 + axis, 1 + c, mass * state[AFF + 3 * c + axis])
            put(1 + axis, 4 + c, scaled * stress[3 * c + axis])

    for b in range(bins):
        first, first_moved = bin_weights(state[0:3], b, quarters, table, along)
        factors = split(table[...])
        highs[b], lows[b] = factors

        def channel(matrix):
            begin = matrix * span + 8 * b * quarters
            return jnp.concatenate(
                [shuffle[pl.ds(begin + 8 * q, 8), :] for q in range(quarters)], axis=1
            )

        base, slope_x, slope_y, slope_z = [channel(matrix) for matrix in range(4)]
        lefts = [
            jnp.concatenate([first[a] * base + first_moved[a] * slope_x for a in range(6)], axis=0),
            jnp.concatenate([first[a] * slope_y for a in range(6)], axis=0),
            jnp.concatenate([first[a] * slope_z for a in range(6)], axis=0),
        ]
        total = None
        for part in range(3):
            left_high, left_low = split(lefts[part])
            right_high, right_low = split(table[pl.ds(part * PITCH, PITCH), :])
            product = (
                dot_nt(left_high, right_high)
                + dot_nt(left_high, right_low)
                + dot_nt(left_low, right_high)
            )
            total = product if total is None else total + product
        tiles[:, TILE * b : TILE * (b + 1)] = total[:, 0:TILE]

    row = iota((8, LANES), 0)
    lanes = iota((8, LANES), 1)
    extra = bins * TILE - LANES

    def packed(plane):
        body = tiles[pl.ds(8 * plane, 8), 0:LANES]
        rest = jnp.where(lanes < extra, tiles[pl.ds(8 * plane, 8), LANES : 2 * LANES], 0.0)
        rest = jnp.where(row == 7, jnp.broadcast_to(meta, (8, LANES)), rest)
        rest = pltpu.roll(rest, 0, 1, stride=extra, stride_axis=0)
        folded = jnp.sum(rest, axis=0, keepdims=True)
        return jnp.where(row == 7, jnp.broadcast_to(folded, (8, LANES)), body)

    odd = device % 2 == 1
    for half in range(2):
        low, high = packed(half), packed(4 + half)
        near[pl.ds(8 * half, 8), :] = jnp.where(odd, low, high)
        far[pl.ds(8 * half, 8), :] = jnp.where(odd, high, low)


def unpacked(block, bins):
    row = iota((8, LANES), 0)
    lanes = iota((8, LANES), 1)
    extra = bins * TILE - LANES
    folded = jnp.broadcast_to(block[7:8, :], (8, LANES))
    rest = folded
    for bit in (1, 2, 4):
        rest = jnp.where(row & bit > 0, pltpu.roll(rest, LANES - bit * extra, 1), rest)
    rest = jnp.where((lanes < extra) & (row < 7), rest, 0.0)
    body = jnp.where(row < 7, block, 0.0)
    return jnp.concatenate([body, rest], axis=1)


def node_key(block, node):
    block_y = jnp.floor((block + 0.5) * (1.0 / BZ))
    block_z = block - BZ * block_y
    node_y = jnp.floor((node + 0.5) * (1.0 / 6.0))
    node_z = node - 6.0 * node_y
    return 4.0 * block_y + node_y, 4.0 * block_z + node_z


def placing(source_block, column_key, bins):
    nodes = bins * TILE
    source = iota((nodes, 1), 0).astype(F32)
    source_bin = jnp.floor((source + 0.5) * (1.0 / TILE))
    source_node = source - TILE * source_bin
    block = jnp.zeros((nodes, 1), F32)
    for b in range(bins):
        block = jnp.where(source_bin == float(b), source_block[b], block)
    row_y, row_z = node_key(block, source_node)
    return jnp.where(LANES * row_y + row_z == column_key, 1.0, 0.0).astype(BF16)


def placed(values, selector):
    count = values.shape[0]
    high, low = split(values)
    result = dot_nn(jnp.concatenate([high, low], axis=0), selector)
    return result[0:count] + result[count : 2 * count]


def halos(near, far, device, device_total):
    odd = device % 2 == 1
    near_block, far_block = near[...], far[...]
    left_block = jnp.where(odd, near_block, far_block)
    right_block = jnp.where(odd, far_block, near_block)
    left_block = jnp.where(device > 0, left_block, 0.0)
    right_block = jnp.where(device + 1 < device_total, right_block, 0.0)
    return left_block, right_block


def halo_blocks(block, bins):
    lane = iota((1, LANES), 1)
    return [
        jnp.max(jnp.where(lane == META + b, block[7:8, :], 0.0), axis=1, keepdims=True)
        for b in range(bins)
    ]


def to_particles(
    state, device, bins, device_total, geometry, own, sides, speeds, blocks_around,
    highs, lows, along, shuffle,
):
    rows = state[0].shape[0]
    quarters = rows // bins
    width = bins * LANES
    nodes = bins * TILE
    fastest = jnp.max(speeds[...], axis=0, keepdims=True)
    fastest = jnp.max(fastest, axis=1, keepdims=True)
    time_step = courant / (jnp.sqrt(fastest) + sound_speed)

    around = []
    for side, block in enumerate(blocks_around):
        values = jnp.concatenate(
            [unpacked(block[0:8, :], bins), unpacked(block[8:16, :], bins)], axis=0
        )
        around.append(placed(values[:, 0:nodes], sides[side]))
    left, right = around

    sub = iota((8, width), 0)
    wide_valid = geometry[0:8, :] >= 0.0
    component = (sub >= 1) & (sub <= 3) & wide_valid
    floor_of = geometry[8:16, :]
    roof_of = geometry[16:24, :]
    pull = time_step * jnp.where(sub == 1, gravity_x, jnp.where(sub == 3, gravity_z, 0.0))
    plane_total = 4 * device_total
    slot = iota((8, LANES), 1)
    lower_half, upper_half = [], []
    for a in range(6):
        sums = own[8 * a : 8 * a + 8, :]
        if a < 2:
            sums = sums + left[8 * a : 8 * a + 8]
        if a >= 4:
            sums = sums + right[8 * a - 32 : 8 * a - 24]
        plane = 4 * device + a
        node_mass = jnp.maximum(jnp.broadcast_to(sums[0:1, :], (8, width)), mass_floor)
        per_step = pltpu.roll(sums, 5, 0)
        motion = (sums - time_step * per_step) / node_mass + pull
        lowest = jnp.where(plane < 2, 0.0, -BIG)
        highest = jnp.where(plane >= plane_total - 2, 0.0, BIG)
        motion = jnp.maximum(motion, jnp.where(sub == 1, lowest, floor_of))
        motion = jnp.minimum(motion, jnp.where(sub == 1, highest, roof_of))
        inside = jnp.where(plane < plane_total, 1, 0)
        motion = jnp.where(component & (inside > 0), motion, 0.0)
        moved = pltpu.roll(motion, 3, 0)
        for b in range(bins):
            here = motion[:, LANES * b : LANES * (b + 1)]
            there = moved[:, LANES * b : LANES * (b + 1)]
            lower_half.append(
                jnp.where(slot < PITCH, here, jnp.where(slot < 2 * PITCH, there, 0.0))
            )
            upper_half.append(jnp.where(slot >= 2 * PITCH, here, 0.0))

    span = 8 * rows
    for b in range(bins):
        motions = jnp.concatenate(
            [half[bins * a + b] for a in range(6) for half in (lower_half, upper_half)], axis=0
        )[:, 0 : 3 * PITCH]
        count = motions.shape[0]
        high, low = split(motions)
        product = dot_nn(jnp.concatenate([high, low], axis=0), highs[b])
        product = product[0:count] + product[count : 2 * count] + dot_nn(high, lows[b])
        sums = [None, None, None]
        for a in range(6):
            top = product[16 * a : 16 * a + 8]
            bottom = product[16 * a + 8 : 16 * a + 16]
            weight = jnp.broadcast_to(along[pl.ds(16 * b + a, 1), :], top.shape)
            weight_moved = jnp.broadcast_to(along[pl.ds(16 * b + 8 + a, 1), :], top.shape)
            terms = (weight * top, weight * bottom, weight_moved * top)
            sums = [t if s is None else s + t for s, t in zip(sums, terms)]
        for kind in range(3):
            for q in range(quarters):
                begin = kind * span + 8 * (b * quarters + q)
                shuffle[pl.ds(begin, 8), :] = sums[kind][:, LANES * q : LANES * (q + 1)]

    def take(kind, row):
        return shuffle[pl.ds(kind * span + row, rows, stride=8), :]

    velocity = [take(0, 1 + c) for c in range(3)]
    affine = [None] * 9
    for c in range(3):
        affine[3 * c] = 4.0 * take(2, 1 + c)
        affine[3 * c + 1] = 4.0 * take(0, 4 + c)
        affine[3 * c + 2] = 4.0 * take(1, 1 + c)
    old = state[DEF : DEF + 9]
    deform = []
    for r in range(3):
        for c in range(3):
            change = (
                affine[3 * r] * old[c] + affine[3 * r + 1] * old[3 + c] + affine[3 * r + 2] * old[6 + c]
            )
            deform.append(old[3 * r + c] + time_step * change)
    steps = [time_step * velocity[c] for c in range(3)]
    moved = [state[c] + steps[c] for c in range(3)]
    travelled = [state[TRAV + c] + steps[c] for c in range(3)]
    return moved + velocity + deform + affine + [state[MASS], state[VOL]] + travelled


def read_state(ref, rows):
    return [ref[pl.ds(rows * number, rows), :] for number in range(ROWS)]


def write_state(ref, state):
    rows = state[0].shape[0]
    for number in range(ROWS):
        ref[pl.ds(rows * number, rows), :] = state[number]


def first_kernel(
    bins, device_total, blocks, live, device, x_ref, v_ref, f_ref, c_ref, m_ref, vol_ref,
    state_ref, speeds, tiles, near, far, highs, lows, along, table, shuffle,
):
    rows = state_ref.shape[0] // ROWS
    quarters = rows // bins
    begin = 0
    for ref, count in ((x_ref, 3), (v_ref, 3), (f_ref, 9), (c_ref, 9)):
        for number in range(count):
            for s in range(rows):
                target = rows * (begin + number) + s
                state_ref[pl.ds(target, 1), :] = ref[
                    pl.ds(number, 1), pl.ds(LANES * s, LANES)
                ]
        begin += count
    for ref, number in ((m_ref, MASS), (vol_ref, VOL)):
        for b in range(bins):
            alive = jnp.where(b < live[0], 1.0, 0.0)
            for q in range(quarters):
                s = quarters * b + q
                piece = ref[pl.ds(LANES * s, LANES)].reshape(1, LANES)
                state_ref[pl.ds(rows * number + s, 1), :] = piece * alive
    home = jnp.zeros((rows, LANES), F32)
    home_y, home_z = home, home
    row_bin = iota((rows, LANES), 0) // quarters
    for b in range(bins):
        block = blocks[b]
        block_y = block // BZ
        block_z = block - BZ * block_y
        home_y = jnp.where(row_bin == b, (4 * block_y).astype(F32), home_y)
        home_z = jnp.where(row_bin == b, (4 * block_z).astype(F32), home_z)
    anchors = (home + (4 * device).astype(F32), home_y, home_z)
    for axis in range(3):
        place = pl.ds(rows * axis, rows)
        state_ref[place, :] = state_ref[place, :] - anchors[axis]
        state_ref[pl.ds(rows * (TRAV + axis), rows), :] = home
    clear_pads(table)
    state = read_state(state_ref, rows)
    send_speed(state[VEL : VEL + 3], state[MASS], speeds)
    lane = iota((1, LANES), 1)
    meta = jnp.zeros((1, LANES), F32)
    for b in range(bins):
        meta = jnp.where(lane == b, blocks[b].astype(F32), meta)
    to_grid(
        state, device, bins, meta, tiles, near, far, highs, lows, along, table, shuffle
    )


def first_own_kernel(bins, device_total, blocks, live, device, tiles, own, geometry, home):
    width = bins * LANES
    nodes = bins * TILE
    position = iota((1, width), 1)
    column_bin = position // LANES
    column_slot = position - LANES * column_bin
    column_part = jnp.where(column_slot >= 2 * PITCH, 2, jnp.where(column_slot >= PITCH, 1, 0))
    column_node = column_slot - PITCH * column_part
    column_valid = (column_node < TILE) & (column_slot < 3 * PITCH)
    own_blocks = [blocks[b].astype(F32) for b in range(bins)]
    column_block = jnp.zeros((1, width), F32)
    for b in range(bins):
        column_block = jnp.where(column_bin == b, own_blocks[b], column_block)
    column_y, column_z = node_key(column_block, column_node.astype(F32))
    column_key = jnp.where(column_valid, LANES * column_y + column_z, -1.0)
    selector = placing(own_blocks, column_key, bins)
    home[...] = selector
    own[...] = placed(tiles[:, 0:nodes], selector)
    sub = iota((8, width), 0)
    wide_y = jnp.broadcast_to(column_y, (8, width))
    wide_z = jnp.broadcast_to(column_z, (8, width))
    geometry[0:8, :] = jnp.broadcast_to(column_key, (8, width))
    geometry[8:16, :] = jnp.where(
        ((sub == 2) & (wide_y < 2.0)) | ((sub == 3) & (wide_z < 2.0)), 0.0, -BIG
    )
    geometry[16:24, :] = jnp.where(
        ((sub == 2) & (wide_y >= NGY - 2.0)) | ((sub == 3) & (wide_z >= NGZ - 2.0)), 0.0, BIG
    )


def own_kernel(bins, device_total, live, device, tiles, home, own):
    own[...] = placed(tiles[:, 0 : bins * TILE], home[...])


def second_kernel(
    bins, device_total, live, device, old_ref, speeds, own, geometry, old_highs, old_lows,
    old_along, near, far, state_ref, new_speeds, tiles, new_near, new_far, highs, lows, along,
    sides_ref, table, shuffle,
):
    around = halos(near, far, device, device_total)
    key = geometry[0:1, :]
    sides = [placing(halo_blocks(block, bins), key, bins) for block in around]
    for side in range(2):
        sides_ref[side] = sides[side]
    advance(
        bins, device_total, device, old_ref, speeds, own, geometry, old_highs, old_lows,
        old_along, around, sides, state_ref, new_speeds, tiles, new_near, new_far, highs, lows,
        along, table, shuffle,
    )


def later_kernel(
    bins, device_total, live, device, old_ref, speeds, own, geometry, old_highs, old_lows,
    old_along, near, far, sides_ref, state_ref, new_speeds, tiles, new_near, new_far, highs, lows,
    along, table, shuffle,
):
    around = halos(near, far, device, device_total)
    sides = [sides_ref[0], sides_ref[1]]
    advance(
        bins, device_total, device, old_ref, speeds, own, geometry, old_highs, old_lows,
        old_along, around, sides, state_ref, new_speeds, tiles, new_near, new_far, highs, lows,
        along, table, shuffle,
    )


def advance(
    bins, device_total, device, old_ref, speeds, own, geometry, old_highs, old_lows,
    old_along, around, sides, state_ref, new_speeds, tiles, near, far, highs, lows, along,
    table, shuffle,
):
    rows = state_ref.shape[0] // ROWS
    clear_pads(table)
    state = read_state(old_ref, rows)
    state = to_particles(
        state, device, bins, device_total, geometry, own, sides, speeds, around, old_highs,
        old_lows, old_along, shuffle,
    )
    write_state(state_ref, state)
    send_speed(state[VEL : VEL + 3], state[MASS], new_speeds)
    to_grid(
        state, device, bins, jnp.zeros((1, LANES), F32), tiles, near, far, highs, lows, along,
        table, shuffle,
    )


def last_kernel(
    bins, device_total, live, device, old_ref, speeds, own, geometry, highs, lows, along,
    near, far, sides_ref, d_out, v_out, f_out, c_out, shuffle,
):
    rows = old_ref.shape[0] // ROWS
    quarters = rows // bins
    state = read_state(old_ref, rows)
    state = to_particles(
        state, device, bins, device_total, geometry, own, [sides_ref[0], sides_ref[1]], speeds,
        halos(near, far, device, device_total), highs, lows, along, shuffle,
    )
    row_bin = iota((rows, LANES), 0) // quarters
    alive = row_bin < live[0]
    half = rows * LANES
    for ref, begin, count in ((d_out, TRAV, 3), (v_out, VEL, 3), (f_out, DEF, 9), (c_out, AFF, 9)):
        for number in range(count):
            value = jnp.where(alive, state[begin + number], 0.0)
            for s in range(rows):
                ref[pl.ds(number, 1), pl.ds(LANES * s, LANES)] = value[s : s + 1, :]
        total = ref.shape[1]
        ref[:, pl.ds(half, total - half)] = jnp.zeros((count, total - half), F32)


def local(positions, velocity, deformation, affine, particle_mass, volume, bin_block, live_count):
    slot_total = bin_block.shape[0]
    per_bin = positions.shape[1] // slot_total
    bins = slot_total // 2
    device_total = lax.axis_size("space")
    rows = bins * per_bin // LANES
    half = rows * LANES
    nodes = bins * TILE
    width = bins * LANES
    nodes = bins * TILE
    held = [
        ((ROWS * rows, LANES), F32),
        ((device_total, LANES), F32),
        ((48, 2 * LANES), F32),
        ((16, LANES), F32),
        ((16, LANES), F32),
        ((bins, 3 * PITCH, per_bin), BF16),
        ((bins, 3 * PITCH, per_bin), BF16),
        ((16 * bins, per_bin), F32),
    ]
    own_shape = ((48, width), F32)
    geometry_shape = ((24, width), F32)
    home_shape = ((nodes, width), BF16)
    sides_shape = ((2, nodes, width), BF16)
    smem = pl.BlockSpec(memory_space=pltpu.SMEM)
    vmem = pl.BlockSpec(memory_space=pltpu.VMEM)
    table = pltpu.VMEM((3 * PITCH, per_bin), F32)
    shuffle = pltpu.VMEM((4 * 8 * rows, LANES), F32)
    bin_block = bin_block if INTERPRET else pltpu.with_memory_space_constraint(bin_block, pltpu.HBM)
    me = lax.axis_index("space").astype(jnp.int32).reshape(1)

    def stay(array, space=pltpu.VMEM):
        return array if INTERPRET else pltpu.with_memory_space_constraint(array, space)

    def call(body, scalars, arguments, outputs, scratch, in_specs=None, final=False):
        def kernel(*refs):
            count = len(scalars)
            body(bins, device_total, *refs[: count - 1], refs[count - 1][0], *refs[count:])

        extra = {}
        out_specs = tuple(vmem for _ in outputs)
        if in_specs is None:
            in_specs = [vmem] * len(arguments)
            arguments = [stay(argument) for argument in arguments]
        else:
            arguments = [stay(argument, pltpu.HBM) for argument in arguments]
            out_specs = tuple(
                pl.BlockSpec(shape, lambda i, rank=len(shape): (0,) * rank)
                for shape, _ in outputs
            )
            extra = {"grid": (1,)}
        make = jax.ShapeDtypeStruct if final or INTERPRET else pltpu.VMEM
        return pl.pallas_call(
            kernel,
            in_specs=[smem] * len(scalars) + in_specs,
            out_shape=tuple(make(shape, kind) for shape, kind in outputs),
            out_specs=out_specs,
            scratch_shapes=scratch,
            interpret=INTERPRET,
            compiler_params=pltpu.CompilerParams(vmem_limit_bytes=GRANT),
            **extra,
        )(*scalars, *arguments)

    def first_half(count):
        return pl.BlockSpec((count, half), lambda i: (0, 0))

    flat_half = pl.BlockSpec((half,), lambda i: (0,))
    length = device_total
    swap_pairs = [(i, i ^ 1) for i in range(length)]
    cross_pairs = [(i, i + 1) for i in range(1, length - 1, 2)]
    cross_pairs = cross_pairs + [(j, i) for i, j in cross_pairs]

    def exchange(speeds, near, far):
        far = lax.ppermute(far, "space", cross_pairs)
        speeds = lax.all_to_all(speeds, "space", 0, 0, tiled=True)
        near = lax.ppermute(near, "space", swap_pairs)
        return speeds, near, far

    state, speeds, tiles, near, far, highs, lows, along = call(
        first_kernel,
        (bin_block, live_count, me),
        (positions, velocity, deformation, affine, particle_mass, volume),
        held,
        [table, shuffle],
        [first_half(3), first_half(3), first_half(9), first_half(9), flat_half, flat_half],
    )
    speeds, near, far = exchange(speeds, near, far)
    own, geometry, home = call(
        first_own_kernel,
        (bin_block, live_count, me),
        (tiles,),
        [own_shape, geometry_shape, home_shape],
        [],
    )
    sides = ()
    for step in range(STEPS - 1):
        results = call(
            second_kernel if step == 0 else later_kernel,
            (live_count, me),
            (state, speeds, own, geometry, highs, lows, along, near, far, *sides),
            held + ([sides_shape] if step == 0 else []),
            [table, shuffle],
        )
        state, speeds, tiles, near, far, highs, lows, along = results[:8]
        if step == 0:
            sides = results[8:]
        speeds, near, far = exchange(speeds, near, far)
        (own,) = call(own_kernel, (live_count, me), (tiles, home), [own_shape], [])
    total = positions.shape[1]
    return call(
        last_kernel,
        (live_count, me),
        (state, speeds, own, geometry, highs, lows, along, near, far, *sides),
        [((count, total), F32) for count in (3, 3, 9, 9)],
        [shuffle],
        final=True,
    )


def solution(mesh):
    in_specs = (
        P(None, "space"),
        P(None, "space"),
        P(None, "space"),
        P(None, "space"),
        P("space"),
        P("space"),
        P("space"),
        P("space"),
    )
    out_specs = (P(None, "space"), P(None, "space"), P(None, "space"), P(None, "space"))
    return jax.shard_map(local, mesh=mesh, in_specs=in_specs, out_specs=out_specs, check_vma=False)
```

```python
import jax
import jax.numpy as jnp
from jax import lax
from jax.experimental import pallas as pl
from jax.experimental.pallas import tpu as pltpu
from jax.sharding import PartitionSpec as P


BZ = 16
STEPS = 3
NGY = 66
NGZ = 66

mu_shear = 4.0
lame_first = 6.0
courant = 0.15
sound_speed = 3.7416573867739413
mass_floor = 0.05
gravity_x = 3.0
gravity_z = -9.0

LANES = 128
TILE = 48
SLOT = 64
META = 64
BIG = 3.0e38
GRANT = 8 * 2**20
F32 = jnp.float32
BF16 = jnp.bfloat16
INTERPRET = False

POS, DEF, MASS, VOL, TRAV = 0, 3, 12, 13, 14
ROWS = 17


def iota(shape, dim):
    return lax.broadcasted_iota(jnp.int32, shape, dim)


def split(value):
    high = value.astype(BF16)
    low = (value - high.astype(F32)).astype(BF16)
    return high, low


def dot_nt(a, b):
    return lax.dot_general(a, b, (((1,), (1,)), ((), ())), preferred_element_type=F32)


def dot_nn(a, b):
    return lax.dot_general(a, b, (((1,), (0,)), ((), ())), preferred_element_type=F32)


def spline(distance):
    magnitude = jnp.abs(distance)
    outer = jnp.maximum(1.5 - magnitude, 0.0)
    inner = jnp.maximum(0.5 - magnitude, 0.0)
    return 0.5 * outer * outer - 1.5 * inner * inner


def spread(ref, row, quarters):
    return jnp.concatenate(
        [ref[pl.ds(row + q, 8, stride=0), :] for q in range(quarters)], axis=1
    )


def dense_weights(position, ref):
    rows = position.shape[0]
    for a in range(6):
        offset = float(a) - position
        weight = spline(offset)
        ref[pl.ds(rows * a, rows), :] = weight
        ref[pl.ds(rows * (6 + a), rows), :] = weight * offset


def pair_weights(state_ref, across, row, span):
    rows = across.shape[0] // 12
    along_z = spread(state_ref, 2 * rows + row, span)
    third_node = iota(along_z.shape, 0)
    third_offset = third_node.astype(F32) - along_z
    third = jnp.where(third_node < 6, spline(third_offset), 0.0)
    third_moved = third * third_offset
    plain, moved_y, moved_z = [], [], []
    for a in range(6):
        second = spread(across, rows * a + row, span)
        second_moved = spread(across, rows * (6 + a) + row, span)
        plain.append(second * third)
        moved_y.append(second_moved * third)
        moved_z.append(second * third_moved)
    return [jnp.concatenate(part, axis=0) for part in (plain, moved_y, moved_z)]


def kirchhoff(deform):
    determinant = (
        deform[0] * (deform[4] * deform[8] - deform[5] * deform[7])
        - deform[1] * (deform[3] * deform[8] - deform[5] * deform[6])
        + deform[2] * (deform[3] * deform[7] - deform[4] * deform[6])
    )
    pressure = lame_first * (determinant - 1.0) * determinant
    stress = [None] * 9
    for r in range(3):
        for c in range(r, 3):
            product = (
                deform[3 * r] * deform[3 * c]
                + deform[3 * r + 1] * deform[3 * c + 1]
                + deform[3 * r + 2] * deform[3 * c + 2]
            )
            if r == c:
                stress[3 * r + c] = mu_shear * (product - 1.0) + pressure
            else:
                stress[3 * r + c] = mu_shear * product
                stress[3 * c + r] = stress[3 * r + c]
    return stress


def send_speed(velocity, mass, speeds, outbox, sem):
    speed = velocity[0] * velocity[0] + velocity[1] * velocity[1] + velocity[2] * velocity[2]
    speed = jnp.max(jnp.where(mass > 0.0, speed, 0.0), axis=0, keepdims=True)
    speed = jnp.max(speed, axis=1, keepdims=True)
    outbox[...] = jnp.broadcast_to(speed, outbox.shape)
    copy = pltpu.make_async_copy(outbox, speeds, sem)
    copy.start()
    return copy


def halves(quarters):
    parts = 2 if quarters % 2 == 0 else 1
    span = quarters // parts
    return [(part * span, span, pl.ds(part * span * LANES, span * LANES)) for part in range(parts)]


def plane_sums(planes, row, span, channels, along, tables):
    rows = along.shape[0] // 12

    def channel(matrix):
        begin = 8 * (matrix * rows + row)
        return jnp.concatenate(
            [channels[pl.ds(begin + 8 * q, 8), :] for q in range(span)], axis=1
        )

    base, slope_x, slope_y, slope_z = [channel(matrix) for matrix in range(4)]
    pieces = ([], [], [])
    for a in planes:
        first = spread(along, rows * a + row, span)
        first_moved = spread(along, rows * (6 + a) + row, span)
        pieces[0].append(first * base + first_moved * slope_x)
        pieces[1].append(first * slope_y)
        pieces[2].append(first * slope_z)
    count = 8 * len(planes)
    total = None
    for piece, (right_high, right_low) in zip(pieces, tables):
        left_high, left_low = split(jnp.concatenate(piece, axis=0))
        both = dot_nt(jnp.concatenate([left_high, left_low], axis=0), right_high)
        product = both[0:count] + both[count : 2 * count] + dot_nt(left_high, right_low)
        total = product if total is None else total + product
    return total


def far_planes(device):
    return 4 * (device % 2)


def to_grid(
    state, velocity, affine, state_ref, device, bins, meta, far, highs, lows, along, channels, across
):
    rows = state[0].shape[0]
    quarters = rows // bins
    deform = state[DEF : DEF + 9]
    mass, volume = state[MASS], state[VOL]
    stress = kirchhoff(deform)
    scaled = 4.0 * volume
    span = 8 * rows
    zero = jnp.zeros((rows, LANES), F32)

    def put(matrix, row, value):
        channels[pl.ds(matrix * span + row, rows, stride=8), :] = value

    put(0, 0, mass)
    for c in range(3):
        put(0, 1 + c, mass * velocity[c])
        put(0, 4 + c, zero)
    put(0, 7, zero)
    for axis in range(3):
        put(1 + axis, 0, zero)
        put(1 + axis, 7, zero)
        for c in range(3):
            put(1 + axis, 1 + c, mass * affine[3 * c + axis])
            put(1 + axis, 4 + c, scaled * stress[3 * c + axis])
    dense_weights(state[0], along)
    dense_weights(state[1], across)
    base = far_planes(device)
    for b in range(bins):
        total = None
        for begin, width, lanes in halves(quarters):
            row = b * quarters + begin
            tables = []
            for kind, values in enumerate(pair_weights(state_ref, across, row, width)):
                high, low = split(values)
                highs[b, pl.ds(kind * TILE, TILE), lanes] = high
                lows[b, pl.ds(kind * TILE, TILE), lanes] = low
                tables.append((high, low))
            sums = plane_sums((base, base + 1), row, width, channels, along, tables)
            total = sums if total is None else total + sums
        far[:, TILE * b : TILE * (b + 1)] = total
    nodes = bins * TILE
    width = far.shape[1]
    if meta is None:
        meta = jnp.zeros((1, width), F32)
    far[:, nodes:width] = jnp.broadcast_to(meta, (16, width))[:, nodes:width]


def rest_of_grid(device, bins, meta, far, highs, lows, along, channels, near):
    rows = along.shape[0] // 12
    quarters = rows // bins
    odd = device % 2 == 1
    base = 4 - far_planes(device)
    middle = []
    for b in range(bins):
        total = None
        for begin, width, lanes in halves(quarters):
            row = b * quarters + begin
            tables = [
                (highs[b, pl.ds(kind * TILE, TILE), lanes], lows[b, pl.ds(kind * TILE, TILE), lanes])
                for kind in range(3)
            ]
            sums = plane_sums((base, base + 1, 2, 3), row, width, channels, along, tables)
            total = sums if total is None else total + sums
        near[:, TILE * b : TILE * (b + 1)] = total[0:16]
        middle.append(total[16:32])
    nodes = bins * TILE
    width = near.shape[1]
    if meta is None:
        meta = jnp.zeros((1, width), F32)
    near[:, nodes:width] = jnp.broadcast_to(meta, (16, width))[:, nodes:width]
    near_part, far_part = near[:, 0:nodes], far[:, 0:nodes]
    low = jnp.where(odd, near_part, far_part)
    high = jnp.where(odd, far_part, near_part)
    return low, middle, high


def node_key(block, node):
    block_y = jnp.floor((block + 0.5) * (1.0 / BZ))
    block_z = block - BZ * block_y
    node_y = jnp.floor((node + 0.5) * (1.0 / 8.0))
    node_z = node - 8.0 * node_y
    return 4.0 * block_y + node_y, 4.0 * block_z + node_z


def placing(source_block, column_key, bins):
    nodes = bins * TILE
    source = iota((nodes, 1), 0).astype(F32)
    source_bin = jnp.floor((source + 0.5) * (1.0 / TILE))
    source_node = source - TILE * source_bin
    block = jnp.zeros((nodes, 1), F32)
    for b in range(bins):
        block = jnp.where(source_bin == float(b), source_block[b], block)
    row_y, row_z = node_key(block, source_node)
    row_key = LANES * row_y + row_z
    used = source_node - 8.0 * jnp.floor((source_node + 0.5) * (1.0 / 8.0)) < 6.0
    row_key = jnp.where(used, row_key, -2.0)
    return jnp.where(row_key == column_key, 1.0, 0.0).astype(BF16)


def placed(values, selector):
    count = values.shape[0]
    high, low = split(values)
    result = dot_nn(jnp.concatenate([high, low], axis=0), selector)
    return result[0:count] + result[count : 2 * count]


def halos(near, far, device, device_total):
    odd = device % 2 == 1
    near_block, far_block = near[...], far[...]
    left_block = jnp.where(odd, near_block, far_block)
    right_block = jnp.where(odd, far_block, near_block)
    left_block = jnp.where(device > 0, left_block, 0.0)
    right_block = jnp.where(device + 1 < device_total, right_block, 0.0)
    return left_block, right_block


def halo_blocks(block, bins):
    lane = iota((1, LANES), 1)
    return [
        jnp.max(jnp.where(lane == META + b, block[7:8, LANES : 2 * LANES], 0.0), axis=1, keepdims=True)
        for b in range(bins)
    ]


def to_particles(
    state, device, bins, device_total, geometry, own, sides, speeds, blocks_around,
    highs, lows, along, shuffle,
):
    rows = state[0].shape[0]
    quarters = rows // bins
    width = bins * SLOT
    nodes = bins * TILE
    fastest = jnp.max(speeds[...], axis=0, keepdims=True)
    fastest = jnp.max(fastest, axis=1, keepdims=True)
    time_step = courant / (jnp.sqrt(fastest) + sound_speed)

    around = []
    for side, block in enumerate(blocks_around):
        around.append(placed(block[:, 0:nodes], sides[side]))
    left, right = around

    sub = iota((8, width), 0)
    wide_valid = geometry[0:8, :] >= 0.0
    component = (sub >= 1) & (sub <= 3) & wide_valid
    floor_of = geometry[8:16, :]
    roof_of = geometry[16:24, :]
    pull = time_step * jnp.where(sub == 1, gravity_x, jnp.where(sub == 3, gravity_z, 0.0))
    plane_total = 4 * device_total
    motions = []
    for a in range(6):
        sums = own[8 * a : 8 * a + 8, :]
        if a < 2:
            sums = sums + left[8 * a : 8 * a + 8]
        if a >= 4:
            sums = sums + right[8 * a - 32 : 8 * a - 24]
        plane = 4 * device + a
        node_mass = jnp.maximum(jnp.broadcast_to(sums[0:1, :], (8, width)), mass_floor)
        per_step = pltpu.roll(sums, 5, 0)
        motion = (sums - time_step * per_step) / node_mass + pull
        lowest = jnp.where(plane < 2, 0.0, -BIG)
        highest = jnp.where(plane >= plane_total - 2, 0.0, BIG)
        motion = jnp.maximum(motion, jnp.where(sub == 1, lowest, floor_of))
        motion = jnp.minimum(motion, jnp.where(sub == 1, highest, roof_of))
        inside = jnp.where(plane < plane_total, 1, 0)
        motion = jnp.where(component & (inside > 0), motion, 0.0)
        motions.append(motion)
    paired = jnp.concatenate(
        [motions[2 * g] + pltpu.roll(motions[2 * g + 1], 4, 0) for g in range(3)], axis=0
    )

    span = 8 * rows
    for b in range(bins):
        begin = (b * SLOT) // LANES * LANES
        block = paired[:, begin : begin + LANES]
        if b * SLOT > begin:
            block = pltpu.roll(block, LANES - (b * SLOT - begin), 1)
        block = block[:, 0:TILE]
        count = block.shape[0]
        high = block.astype(BF16)
        kept = high.astype(F32)
        stacked = jnp.concatenate([kept, block - kept], axis=0).astype(BF16)
        for first_quarter, wide, lanes in halves(quarters):
            row = b * quarters + first_quarter
            shape = (8, wide * LANES)
            even = iota(shape, 0) < 4
            weights, weights_moved = [
                [
                    jnp.where(
                        even,
                        spread(along, rows * (begin + 2 * g) + row, wide),
                        spread(along, rows * (begin + 2 * g + 1) + row, wide),
                    )
                    for g in range(3)
                ]
                for begin in (0, 6)
            ]
            sums = []
            for kind in range(3):
                right_high = highs[b, pl.ds(kind * TILE, TILE), lanes]
                right_low = lows[b, pl.ds(kind * TILE, TILE), lanes]
                product = dot_nn(stacked, right_high)
                product = product[0:count] + product[count : 2 * count] + dot_nn(high, right_low)
                groups = [product[8 * g : 8 * g + 8] for g in range(3)]
                sums.append(sum(w * group for w, group in zip(weights, groups)))
                if kind == 0:
                    moved_sum = sum(w * group for w, group in zip(weights_moved, groups))
            sums.append(moved_sum)
            for kind in range(4):
                for q in range(wide):
                    target = kind * span + 8 * (row + q)
                    shuffle[pl.ds(target, 8), :] = sums[kind][:, LANES * q : LANES * (q + 1)]

    def take(kind, c):
        return (
            shuffle[pl.ds(kind * span + 1 + c, rows, stride=8), :]
            + shuffle[pl.ds(kind * span + 5 + c, rows, stride=8), :]
        )

    velocity = [take(0, c) for c in range(3)]
    affine = [None] * 9
    for c in range(3):
        affine[3 * c] = 4.0 * take(3, c)
        affine[3 * c + 1] = 4.0 * take(1, c)
        affine[3 * c + 2] = 4.0 * take(2, c)
    old = state[DEF : DEF + 9]
    deform = []
    for r in range(3):
        for c in range(3):
            change = (
                affine[3 * r] * old[c] + affine[3 * r + 1] * old[3 + c] + affine[3 * r + 2] * old[6 + c]
            )
            deform.append(old[3 * r + c] + time_step * change)
    steps = [time_step * velocity[c] for c in range(3)]
    moved = [state[c] + steps[c] for c in range(3)]
    travelled = [state[TRAV + c] + steps[c] for c in range(3)]
    return moved + deform + [state[MASS], state[VOL]] + travelled, velocity, affine


def read_state(ref, rows):
    return [ref[pl.ds(rows * number, rows), :] for number in range(ROWS)]


def write_state(ref, state):
    rows = state[0].shape[0]
    for number in range(ROWS):
        ref[pl.ds(rows * number, rows), :] = state[number]


def block_row(blocks, bins, width):
    lane = iota((1, width), 1)
    meta = jnp.zeros((1, width), F32)
    for b in range(bins):
        meta = jnp.where(lane == LANES + META + b, blocks[b].astype(F32), meta)
    return meta


def first_kernel(
    bins, device_total, blocks, live, device, x_ref, v_ref, f_ref, c_ref, m_ref, vol_ref,
    state_ref, speeds, far, highs, lows, along, channels, across, outbox, sem, motion_ref,
):
    rows = state_ref.shape[0] // ROWS
    quarters = rows // bins
    for ref, count, kept, begin in (
        (x_ref, 3, state_ref, POS),
        (f_ref, 9, state_ref, DEF),
        (v_ref, 3, motion_ref, 0),
        (c_ref, 9, motion_ref, 3),
    ):
        for number in range(count):
            for s in range(rows):
                target = rows * (begin + number) + s
                kept[pl.ds(target, 1), :] = ref[pl.ds(number, 1), pl.ds(LANES * s, LANES)]
    for ref, number in ((m_ref, MASS), (vol_ref, VOL)):
        for b in range(bins):
            alive = jnp.where(b < live[0], 1.0, 0.0)
            for q in range(quarters):
                s = quarters * b + q
                piece = ref[pl.ds(LANES * s, LANES)].reshape(1, LANES)
                state_ref[pl.ds(rows * number + s, 1), :] = piece * alive
    home = jnp.zeros((rows, LANES), F32)
    home_y, home_z = home, home
    row_bin = iota((rows, LANES), 0) // quarters
    for b in range(bins):
        block = blocks[b]
        block_y = block // BZ
        block_z = block - BZ * block_y
        home_y = jnp.where(row_bin == b, (4 * block_y).astype(F32), home_y)
        home_z = jnp.where(row_bin == b, (4 * block_z).astype(F32), home_z)
    anchors = (home + (4 * device).astype(F32), home_y, home_z)
    for axis in range(3):
        place = pl.ds(rows * axis, rows)
        state_ref[place, :] = state_ref[place, :] - anchors[axis]
        state_ref[pl.ds(rows * (TRAV + axis), rows), :] = home
    state = read_state(state_ref, rows)
    motion = [motion_ref[pl.ds(rows * number, rows), :] for number in range(12)]
    copy = send_speed(motion[0:3], state[MASS], speeds, outbox, sem)
    to_grid(
        state, motion[0:3], motion[3:12], state_ref, device, bins, block_row(blocks, bins, far.shape[1]), far, highs, lows,
        along, channels, across,
    )
    copy.wait()


def place_own(own, low, middle, high, selector):
    own[0:16, :] = placed(low, selector)
    own[16:32, :] = placed(jnp.concatenate(middle, axis=1), selector)
    own[32:48, :] = placed(high, selector)


def first_rest_kernel(
    bins, device_total, blocks, live, device, far, highs, lows, along, channels,
    near, own, geometry, home,
):
    low, middle, high = rest_of_grid(
        device, bins, block_row(blocks, bins, near.shape[1]), far, highs, lows, along, channels,
        near,
    )
    width = bins * SLOT
    position = iota((1, width), 1)
    column_bin = position // SLOT
    column_node = position - SLOT * column_bin
    column_valid = (column_node < TILE) & (column_node % 8 < 6)
    own_blocks = [blocks[b].astype(F32) for b in range(bins)]
    column_block = jnp.zeros((1, width), F32)
    for b in range(bins):
        column_block = jnp.where(column_bin == b, own_blocks[b], column_block)
    column_y, column_z = node_key(column_block, column_node.astype(F32))
    column_key = jnp.where(column_valid, LANES * column_y + column_z, -1.0)
    selector = placing(own_blocks, column_key, bins)
    home[...] = selector
    place_own(own, low, middle, high, selector)
    sub = iota((8, width), 0)
    wide_y = jnp.broadcast_to(column_y, (8, width))
    wide_z = jnp.broadcast_to(column_z, (8, width))
    geometry[0:8, :] = jnp.broadcast_to(column_key, (8, width))
    geometry[8:16, :] = jnp.where(
        ((sub == 2) & (wide_y < 2.0)) | ((sub == 3) & (wide_z < 2.0)), 0.0, -BIG
    )
    geometry[16:24, :] = jnp.where(
        ((sub == 2) & (wide_y >= NGY - 2.0)) | ((sub == 3) & (wide_z >= NGZ - 2.0)), 0.0, BIG
    )


def rest_kernel(
    bins, device_total, live, device, far, highs, lows, along, channels, home, near, own
):
    low, middle, high = rest_of_grid(
        device, bins, None, far, highs, lows, along, channels, near
    )
    place_own(own, low, middle, high, home[...])


def second_kernel(
    bins, device_total, live, device, old_ref, speeds, own, geometry, old_highs, old_lows,
    old_along, near, far, state_ref, new_speeds, new_far, highs, lows, along, channels,
    sides_ref, across, outbox, sem,
):
    around = halos(near, far, device, device_total)
    key = geometry[0:1, :]
    sides = [placing(halo_blocks(block, bins), key, bins) for block in around]
    for side in range(2):
        sides_ref[side] = sides[side]
    advance(
        bins, device_total, device, old_ref, speeds, own, geometry, old_highs, old_lows,
        old_along, around, sides, state_ref, new_speeds, new_far, highs, lows, along, channels,
        across, outbox, sem,
    )


def later_kernel(
    bins, device_total, live, device, old_ref, speeds, own, geometry, old_highs, old_lows,
    old_along, near, far, sides_ref, state_ref, new_speeds, new_far, highs, lows, along, channels,
    across, outbox, sem,
):
    around = halos(near, far, device, device_total)
    sides = [sides_ref[0], sides_ref[1]]
    advance(
        bins, device_total, device, old_ref, speeds, own, geometry, old_highs, old_lows,
        old_along, around, sides, state_ref, new_speeds, new_far, highs, lows, along, channels,
        across, outbox, sem,
    )


def advance(
    bins, device_total, device, old_ref, speeds, own, geometry, old_highs, old_lows,
    old_along, around, sides, state_ref, new_speeds, far, highs, lows, along, channels,
    across, outbox, sem,
):
    rows = state_ref.shape[0] // ROWS
    state = read_state(old_ref, rows)
    state, velocity, affine = to_particles(
        state, device, bins, device_total, geometry, own, sides, speeds, around, old_highs,
        old_lows, old_along, channels,
    )
    write_state(state_ref, state)
    copy = send_speed(velocity, state[MASS], new_speeds, outbox, sem)
    to_grid(
        state, velocity, affine, state_ref, device, bins, None, far, highs, lows, along, channels, across
    )
    copy.wait()


def last_kernel(
    bins, device_total, live, device, old_ref, speeds, own, geometry, highs, lows, along,
    near, far, sides_ref, d_out, v_out, f_out, c_out, shuffle,
):
    rows = old_ref.shape[0] // ROWS
    quarters = rows // bins
    state = read_state(old_ref, rows)
    state, velocity, affine = to_particles(
        state, device, bins, device_total, geometry, own, [sides_ref[0], sides_ref[1]], speeds,
        halos(near, far, device, device_total), highs, lows, along, shuffle,
    )
    row_bin = iota((rows, LANES), 0) // quarters
    alive = row_bin < live[0]
    half = rows * LANES
    results = (
        (d_out, state[TRAV : TRAV + 3]),
        (v_out, velocity),
        (f_out, state[DEF : DEF + 9]),
        (c_out, affine),
    )
    for ref, values in results:
        count = len(values)
        for number in range(count):
            value = jnp.where(alive, values[number], 0.0)
            for s in range(rows):
                ref[pl.ds(number, 1), pl.ds(LANES * s, LANES)] = value[s : s + 1, :]
        total = ref.shape[1]
        ref[:, pl.ds(half, total - half)] = jnp.zeros((count, total - half), F32)


def local(positions, velocity, deformation, affine, particle_mass, volume, bin_block, live_count):
    slot_total = bin_block.shape[0]
    per_bin = positions.shape[1] // slot_total
    bins = slot_total // 2
    device_total = lax.axis_size("space")
    rows = bins * per_bin // LANES
    half = rows * LANES
    nodes = bins * TILE
    width = bins * SLOT
    message = ((16, -(-(nodes + LANES // 2) // LANES) * LANES), F32)
    held = [
        ((ROWS * rows, LANES), F32),
        ((device_total, LANES), F32),
        message,
        ((bins, 3 * TILE, per_bin), BF16),
        ((bins, 3 * TILE, per_bin), BF16),
        ((12 * rows, LANES), F32),
        ((4 * 8 * rows, LANES), F32),
    ]
    speeds_shape = held[1]
    own_shape = ((48, width), F32)
    geometry_shape = ((24, width), F32)
    home_shape = ((nodes, width), BF16)
    sides_shape = ((2, nodes, width), BF16)
    smem = pl.BlockSpec(memory_space=pltpu.SMEM)
    vmem = pl.BlockSpec(memory_space=pltpu.VMEM)
    anywhere = pl.BlockSpec(memory_space=pl.ANY)
    working = [
        pltpu.VMEM((12 * rows, LANES), F32),
        pltpu.VMEM((device_total, LANES), F32),
        pltpu.SemaphoreType.DMA,
    ]
    bin_block = bin_block if INTERPRET else pltpu.with_memory_space_constraint(bin_block, pltpu.HBM)
    me = lax.axis_index("space").astype(jnp.int32).reshape(1)

    def stay(array, space=pltpu.VMEM):
        return array if INTERPRET else pltpu.with_memory_space_constraint(array, space)

    def call(body, scalars, arguments, outputs, scratch, in_specs=None, final=False):
        def kernel(*refs):
            count = len(scalars)
            body(bins, device_total, *refs[: count - 1], refs[count - 1][0], *refs[count:])

        extra = {}
        out_specs = tuple(anywhere if output == speeds_shape else vmem for output in outputs)
        if in_specs is None:
            in_specs = [vmem] * len(arguments)
            arguments = [stay(argument) for argument in arguments]
        else:
            arguments = [stay(argument, pltpu.HBM) for argument in arguments]
            out_specs = tuple(
                anywhere
                if output == speeds_shape
                else pl.BlockSpec(output[0], lambda i, rank=len(output[0]): (0,) * rank)
                for output in outputs
            )
            extra = {"grid": (1,)}
        make = jax.ShapeDtypeStruct if final or INTERPRET else pltpu.VMEM
        return pl.pallas_call(
            kernel,
            in_specs=[smem] * len(scalars) + in_specs,
            out_shape=tuple(
                pltpu.HBM(*output) if output == speeds_shape and not INTERPRET else make(*output)
                for output in outputs
            ),
            out_specs=out_specs,
            scratch_shapes=scratch,
            interpret=INTERPRET,
            compiler_params=pltpu.CompilerParams(vmem_limit_bytes=GRANT),
            **extra,
        )(*scalars, *arguments)

    def first_half(count):
        return pl.BlockSpec((count, half), lambda i: (0, 0))

    flat_half = pl.BlockSpec((half,), lambda i: (0,))
    length = device_total
    swap_pairs = [(i, i ^ 1) for i in range(length)]
    cross_pairs = [(i, i + 1) for i in range(1, length - 1, 2)]
    cross_pairs = cross_pairs + [(j, i) for i, j in cross_pairs]

    results = call(
        first_kernel,
        (bin_block, live_count, me),
        (positions, velocity, deformation, affine, particle_mass, volume),
        held,
        working + [pltpu.VMEM((12 * rows, LANES), F32)],
        [first_half(3), first_half(3), first_half(9), first_half(9), flat_half, flat_half],
    )
    sides = ()
    for step in range(STEPS):
        state, speeds, far, highs, lows, along, channels = results[:7]
        sides = sides + tuple(results[7:])
        speeds = lax.all_to_all(speeds, "space", 0, 0, tiled=True)
        from_far = lax.ppermute(far, "space", cross_pairs)
        arguments = (far, highs, lows, along, channels)
        if step == 0:
            near, own, geometry, home = call(
                first_rest_kernel,
                (bin_block, live_count, me),
                arguments,
                [message, own_shape, geometry_shape, home_shape],
                [],
            )
        else:
            near, own = call(
                rest_kernel, (live_count, me), arguments + (home,), [message, own_shape], []
            )
        from_near = lax.ppermute(near, "space", swap_pairs)
        arguments = (state, speeds, own, geometry, highs, lows, along, from_near, from_far, *sides)
        if step < STEPS - 1:
            results = call(
                second_kernel if step == 0 else later_kernel,
                (live_count, me),
                arguments,
                held + ([sides_shape] if step == 0 else []),
                working,
            )
    total = positions.shape[1]
    return call(
        last_kernel,
        (live_count, me),
        arguments,
        [((count, total), F32) for count in (3, 3, 9, 9)],
        [pltpu.VMEM((4 * 8 * rows, LANES), F32)],
        final=True,
    )


def solution(mesh):
    in_specs = (
        P(None, "space"),
        P(None, "space"),
        P(None, "space"),
        P(None, "space"),
        P("space"),
        P("space"),
        P("space"),
        P("space"),
    )
    out_specs = (P(None, "space"), P(None, "space"), P(None, "space"), P(None, "space"))
    return jax.shard_map(local, mesh=mesh, in_specs=in_specs, out_specs=out_specs, check_vma=False)
```

```python
import jax
import jax.numpy as jnp
from jax import lax
from jax.experimental import pallas as pl
from jax.experimental.pallas import tpu as pltpu
from jax.sharding import PartitionSpec as P


BZ = 16
STEPS = 3
NGY = 66
NGZ = 66

mu_shear = 4.0
lame_first = 6.0
courant = 0.15
sound_speed = 3.7416573867739413
mass_floor = 0.05
gravity_x = 3.0
gravity_z = -9.0

LANES = 128
TILE = 48
SLOT = 64
META = 64
BIG = 3.0e38
GRANT = 8 * 2**20
F32 = jnp.float32
BF16 = jnp.bfloat16
INTERPRET = False

POS, DEF, MASS, VOL, TRAV = 0, 3, 12, 13, 14
ROWS = 17


def iota(shape, dim):
    return lax.broadcasted_iota(jnp.int32, shape, dim)


def split(value):
    high = value.astype(BF16)
    low = (value - high.astype(F32)).astype(BF16)
    return high, low


def dot_nt(a, b):
    return lax.dot_general(a, b, (((1,), (1,)), ((), ())), preferred_element_type=F32)


def dot_nn(a, b):
    return lax.dot_general(a, b, (((1,), (0,)), ((), ())), preferred_element_type=F32)


def spline(distance):
    magnitude = jnp.abs(distance)
    outer = jnp.maximum(1.5 - magnitude, 0.0)
    inner = jnp.maximum(0.5 - magnitude, 0.0)
    return 0.5 * outer * outer - 1.5 * inner * inner


def spread(ref, row, quarters):
    return jnp.concatenate(
        [ref[pl.ds(row + q, 8, stride=0), :] for q in range(quarters)], axis=1
    )


def dense_weights(position, ref):
    rows = position.shape[0]
    for a in range(6):
        offset = float(a) - position
        weight = spline(offset)
        ref[pl.ds(rows * a, rows), :] = weight
        ref[pl.ds(rows * (6 + a), rows), :] = weight * offset


def pair_weights(state_ref, across, row, span):
    rows = across.shape[0] // 12
    along_z = spread(state_ref, 2 * rows + row, span)
    third_node = iota(along_z.shape, 0)
    third_offset = third_node.astype(F32) - along_z
    third = jnp.where(third_node < 6, spline(third_offset), 0.0)
    third_moved = third * third_offset
    plain, moved_y, moved_z = [], [], []
    for a in range(6):
        second = spread(across, rows * a + row, span)
        second_moved = spread(across, rows * (6 + a) + row, span)
        plain.append(second * third)
        moved_y.append(second_moved * third)
        moved_z.append(second * third_moved)
    return [jnp.concatenate(part, axis=0) for part in (plain, moved_y, moved_z)]


def kirchhoff(deform):
    determinant = (
        deform[0] * (deform[4] * deform[8] - deform[5] * deform[7])
        - deform[1] * (deform[3] * deform[8] - deform[5] * deform[6])
        + deform[2] * (deform[3] * deform[7] - deform[4] * deform[6])
    )
    pressure = lame_first * (determinant - 1.0) * determinant
    stress = [None] * 9
    for r in range(3):
        for c in range(r, 3):
            product = (
                deform[3 * r] * deform[3 * c]
                + deform[3 * r + 1] * deform[3 * c + 1]
                + deform[3 * r + 2] * deform[3 * c + 2]
            )
            if r == c:
                stress[3 * r + c] = mu_shear * (product - 1.0) + pressure
            else:
                stress[3 * r + c] = mu_shear * product
                stress[3 * c + r] = stress[3 * r + c]
    return stress


def send_speed(velocity, mass, speeds, outbox, sem):
    speed = velocity[0] * velocity[0] + velocity[1] * velocity[1] + velocity[2] * velocity[2]
    speed = jnp.max(jnp.where(mass > 0.0, speed, 0.0), axis=0, keepdims=True)
    speed = jnp.max(speed, axis=1, keepdims=True)
    outbox[...] = jnp.broadcast_to(speed, outbox.shape)
    copy = pltpu.make_async_copy(outbox, speeds, sem)
    copy.start()
    return copy


def halves(quarters):
    parts = 2 if quarters % 2 == 0 else 1
    span = quarters // parts
    return [(part * span, span, pl.ds(part * span * LANES, span * LANES)) for part in range(parts)]


def plane_sums(planes, row, span, channels, along, tables):
    rows = along.shape[0] // 12

    def channel(matrix):
        begin = 8 * (matrix * rows + row)
        return jnp.concatenate(
            [channels[pl.ds(begin + 8 * q, 8), :] for q in range(span)], axis=1
        )

    base, slope_x, slope_y, slope_z = [channel(matrix) for matrix in range(4)]
    pieces = ([], [], [])
    for a in planes:
        first = spread(along, rows * a + row, span)
        first_moved = spread(along, rows * (6 + a) + row, span)
        pieces[0].append(first * base + first_moved * slope_x)
        pieces[1].append(first * slope_y)
        pieces[2].append(first * slope_z)
    count = 8 * len(planes)
    total = None
    for piece, (right_high, right_low) in zip(pieces, tables):
        left_high, left_low = split(jnp.concatenate(piece, axis=0))
        both = dot_nt(jnp.concatenate([left_high, left_low], axis=0), right_high)
        product = both[0:count] + both[count : 2 * count] + dot_nt(left_high, right_low)
        total = product if total is None else total + product
    return total


def far_planes(device):
    return 4 * (device % 2)


def to_grid(
    state, velocity, affine, state_ref, device, bins, meta, far, highs, lows, along, channels, across
):
    rows = state[0].shape[0]
    quarters = rows // bins
    deform = state[DEF : DEF + 9]
    mass, volume = state[MASS], state[VOL]
    stress = kirchhoff(deform)
    scaled = 4.0 * volume
    span = 8 * rows
    zero = jnp.zeros((rows, LANES), F32)

    def put(matrix, row, value):
        channels[pl.ds(matrix * span + row, rows, stride=8), :] = value

    put(0, 0, mass)
    for c in range(3):
        put(0, 1 + c, mass * velocity[c])
        put(0, 4 + c, zero)
    put(0, 7, zero)
    for axis in range(3):
        put(1 + axis, 0, zero)
        put(1 + axis, 7, zero)
        for c in range(3):
            put(1 + axis, 1 + c, mass * affine[3 * c + axis])
            put(1 + axis, 4 + c, scaled * stress[3 * c + axis])
    dense_weights(state[0], along)
    dense_weights(state[1], across)
    base = far_planes(device)
    for b in range(bins):
        total = None
        for begin, width, lanes in halves(quarters):
            row = b * quarters + begin
            tables = []
            for kind, values in enumerate(pair_weights(state_ref, across, row, width)):
                high, low = split(values)
                highs[b, pl.ds(kind * TILE, TILE), lanes] = high
                lows[b, pl.ds(kind * TILE, TILE), lanes] = low
                tables.append((high, low))
            sums = plane_sums((base, base + 1), row, width, channels, along, tables)
            total = sums if total is None else total + sums
        far[:, TILE * b : TILE * (b + 1)] = total
    nodes = bins * TILE
    width = far.shape[1]
    if meta is None:
        meta = jnp.zeros((1, width), F32)
    far[:, nodes:width] = jnp.broadcast_to(meta, (16, width))[:, nodes:width]


def rest_of_grid(device, bins, meta, far, highs, lows, along, channels, near):
    rows = along.shape[0] // 12
    quarters = rows // bins
    odd = device % 2 == 1
    base = 4 - far_planes(device)
    middle = []
    for b in range(bins):
        total = None
        for begin, width, lanes in halves(quarters):
            row = b * quarters + begin
            tables = [
                (highs[b, pl.ds(kind * TILE, TILE), lanes], lows[b, pl.ds(kind * TILE, TILE), lanes])
                for kind in range(3)
            ]
            sums = plane_sums((base, base + 1, 2, 3), row, width, channels, along, tables)
            total = sums if total is None else total + sums
        near[:, TILE * b : TILE * (b + 1)] = total[0:16]
        middle.append(total[16:32])
    nodes = bins * TILE
    width = near.shape[1]
    if meta is None:
        meta = jnp.zeros((1, width), F32)
    near[:, nodes:width] = jnp.broadcast_to(meta, (16, width))[:, nodes:width]
    near_part, far_part = near[:, 0:nodes], far[:, 0:nodes]
    low = jnp.where(odd, near_part, far_part)
    high = jnp.where(odd, far_part, near_part)
    return low, middle, high


def node_key(block, node):
    block_y = jnp.floor((block + 0.5) * (1.0 / BZ))
    block_z = block - BZ * block_y
    node_y = jnp.floor((node + 0.5) * (1.0 / 8.0))
    node_z = node - 8.0 * node_y
    return 4.0 * block_y + node_y, 4.0 * block_z + node_z


def placing(source_block, column_key, bins):
    nodes = bins * TILE
    source = iota((nodes, 1), 0).astype(F32)
    source_bin = jnp.floor((source + 0.5) * (1.0 / TILE))
    source_node = source - TILE * source_bin
    block = jnp.zeros((nodes, 1), F32)
    for b in range(bins):
        block = jnp.where(source_bin == float(b), source_block[b], block)
    row_y, row_z = node_key(block, source_node)
    row_key = LANES * row_y + row_z
    used = source_node - 8.0 * jnp.floor((source_node + 0.5) * (1.0 / 8.0)) < 6.0
    row_key = jnp.where(used, row_key, -2.0)
    return jnp.where(row_key == column_key, 1.0, 0.0).astype(BF16)


def placed(values, selector):
    count = values.shape[0]
    high, low = split(values)
    result = dot_nn(jnp.concatenate([high, low], axis=0), selector)
    return result[0:count] + result[count : 2 * count]


def halos(near, outer, inner, device, device_total):
    odd = device % 2 == 1
    middle = (device + 1) % 4 >= 2
    near_block = near[...]
    far_block = jnp.where(middle, inner[...], outer[...])
    left_block = jnp.where(odd, near_block, far_block)
    right_block = jnp.where(odd, far_block, near_block)
    left_block = jnp.where(device > 0, left_block, 0.0)
    right_block = jnp.where(device + 1 < device_total, right_block, 0.0)
    return left_block, right_block


def halo_blocks(block, bins):
    lane = iota((1, LANES), 1)
    return [
        jnp.max(jnp.where(lane == META + b, block[7:8, LANES : 2 * LANES], 0.0), axis=1, keepdims=True)
        for b in range(bins)
    ]


def to_particles(
    state, device, bins, device_total, geometry, own, sides, speeds, blocks_around,
    highs, lows, along, shuffle,
):
    rows = state[0].shape[0]
    quarters = rows // bins
    width = bins * SLOT
    nodes = bins * TILE
    fastest = jnp.max(speeds[...], axis=0, keepdims=True)
    fastest = jnp.max(fastest, axis=1, keepdims=True)
    time_step = courant / (jnp.sqrt(fastest) + sound_speed)

    around = []
    for side, block in enumerate(blocks_around):
        around.append(placed(block[:, 0:nodes], sides[side]))
    left, right = around

    sub = iota((8, width), 0)
    wide_valid = geometry[0:8, :] >= 0.0
    component = (sub >= 1) & (sub <= 3) & wide_valid
    floor_of = geometry[8:16, :]
    roof_of = geometry[16:24, :]
    pull = time_step * jnp.where(sub == 1, gravity_x, jnp.where(sub == 3, gravity_z, 0.0))
    plane_total = 4 * device_total
    motions = []
    for a in range(6):
        sums = own[8 * a : 8 * a + 8, :]
        if a < 2:
            sums = sums + left[8 * a : 8 * a + 8]
        if a >= 4:
            sums = sums + right[8 * a - 32 : 8 * a - 24]
        plane = 4 * device + a
        node_mass = jnp.maximum(jnp.broadcast_to(sums[0:1, :], (8, width)), mass_floor)
        per_step = pltpu.roll(sums, 5, 0)
        motion = (sums - time_step * per_step) / node_mass + pull
        lowest = jnp.where(plane < 2, 0.0, -BIG)
        highest = jnp.where(plane >= plane_total - 2, 0.0, BIG)
        motion = jnp.maximum(motion, jnp.where(sub == 1, lowest, floor_of))
        motion = jnp.minimum(motion, jnp.where(sub == 1, highest, roof_of))
        inside = jnp.where(plane < plane_total, 1, 0)
        motion = jnp.where(component & (inside > 0), motion, 0.0)
        motions.append(motion)
    paired = jnp.concatenate(
        [motions[2 * g] + pltpu.roll(motions[2 * g + 1], 4, 0) for g in range(3)], axis=0
    )

    span = 8 * rows
    for b in range(bins):
        begin = (b * SLOT) // LANES * LANES
        block = paired[:, begin : begin + LANES]
        if b * SLOT > begin:
            block = pltpu.roll(block, LANES - (b * SLOT - begin), 1)
        block = block[:, 0:TILE]
        count = block.shape[0]
        high = block.astype(BF16)
        kept = high.astype(F32)
        stacked = jnp.concatenate([kept, block - kept], axis=0).astype(BF16)
        for first_quarter, wide, lanes in halves(quarters):
            row = b * quarters + first_quarter
            shape = (8, wide * LANES)
            even = iota(shape, 0) < 4
            weights, weights_moved = [
                [
                    jnp.where(
                        even,
                        spread(along, rows * (begin + 2 * g) + row, wide),
                        spread(along, rows * (begin + 2 * g + 1) + row, wide),
                    )
                    for g in range(3)
                ]
                for begin in (0, 6)
            ]
            sums = []
            for kind in range(3):
                right_high = highs[b, pl.ds(kind * TILE, TILE), lanes]
                right_low = lows[b, pl.ds(kind * TILE, TILE), lanes]
                product = dot_nn(stacked, right_high)
                product = product[0:count] + product[count : 2 * count] + dot_nn(high, right_low)
                groups = [product[8 * g : 8 * g + 8] for g in range(3)]
                sums.append(sum(w * group for w, group in zip(weights, groups)))
                if kind == 0:
                    moved_sum = sum(w * group for w, group in zip(weights_moved, groups))
            sums.append(moved_sum)
            for kind in range(4):
                for q in range(wide):
                    target = kind * span + 8 * (row + q)
                    shuffle[pl.ds(target, 8), :] = sums[kind][:, LANES * q : LANES * (q + 1)]

    def take(kind, c):
        return (
            shuffle[pl.ds(kind * span + 1 + c, rows, stride=8), :]
            + shuffle[pl.ds(kind * span + 5 + c, rows, stride=8), :]
        )

    velocity = [take(0, c) for c in range(3)]
    affine = [None] * 9
    for c in range(3):
        affine[3 * c] = 4.0 * take(3, c)
        affine[3 * c + 1] = 4.0 * take(1, c)
        affine[3 * c + 2] = 4.0 * take(2, c)
    old = state[DEF : DEF + 9]
    deform = []
    for r in range(3):
        for c in range(3):
            change = (
                affine[3 * r] * old[c] + affine[3 * r + 1] * old[3 + c] + affine[3 * r + 2] * old[6 + c]
            )
            deform.append(old[3 * r + c] + time_step * change)
    steps = [time_step * velocity[c] for c in range(3)]
    moved = [state[c] + steps[c] for c in range(3)]
    travelled = [state[TRAV + c] + steps[c] for c in range(3)]
    return moved + deform + [state[MASS], state[VOL]] + travelled, velocity, affine


def read_state(ref, rows):
    return [ref[pl.ds(rows * number, rows), :] for number in range(ROWS)]


def write_state(ref, state):
    rows = state[0].shape[0]
    for number in range(ROWS):
        ref[pl.ds(rows * number, rows), :] = state[number]


def block_row(blocks, bins, width):
    lane = iota((1, width), 1)
    meta = jnp.zeros((1, width), F32)
    for b in range(bins):
        meta = jnp.where(lane == LANES + META + b, blocks[b].astype(F32), meta)
    return meta


def first_kernel(
    bins, device_total, blocks, live, device, x_ref, v_ref, f_ref, c_ref, m_ref, vol_ref,
    state_ref, speeds, far, highs, lows, along, channels, across, outbox, sem, motion_ref,
):
    rows = state_ref.shape[0] // ROWS
    quarters = rows // bins
    for ref, count, kept, begin in (
        (x_ref, 3, state_ref, POS),
        (f_ref, 9, state_ref, DEF),
        (v_ref, 3, motion_ref, 0),
        (c_ref, 9, motion_ref, 3),
    ):
        for number in range(count):
            for s in range(rows):
                target = rows * (begin + number) + s
                kept[pl.ds(target, 1), :] = ref[pl.ds(number, 1), pl.ds(LANES * s, LANES)]
    for ref, number in ((m_ref, MASS), (vol_ref, VOL)):
        for b in range(bins):
            alive = jnp.where(b < live[0], 1.0, 0.0)
            for q in range(quarters):
                s = quarters * b + q
                piece = ref[pl.ds(LANES * s, LANES)].reshape(1, LANES)
                state_ref[pl.ds(rows * number + s, 1), :] = piece * alive
    home = jnp.zeros((rows, LANES), F32)
    home_y, home_z = home, home
    row_bin = iota((rows, LANES), 0) // quarters
    for b in range(bins):
        block = blocks[b]
        block_y = block // BZ
        block_z = block - BZ * block_y
        home_y = jnp.where(row_bin == b, (4 * block_y).astype(F32), home_y)
        home_z = jnp.where(row_bin == b, (4 * block_z).astype(F32), home_z)
    anchors = (home + (4 * device).astype(F32), home_y, home_z)
    for axis in range(3):
        place = pl.ds(rows * axis, rows)
        state_ref[place, :] = state_ref[place, :] - anchors[axis]
        state_ref[pl.ds(rows * (TRAV + axis), rows), :] = home
    state = read_state(state_ref, rows)
    motion = [motion_ref[pl.ds(rows * number, rows), :] for number in range(12)]
    copy = send_speed(motion[0:3], state[MASS], speeds, outbox, sem)
    to_grid(
        state, motion[0:3], motion[3:12], state_ref, device, bins, block_row(blocks, bins, far.shape[1]), far, highs, lows,
        along, channels, across,
    )
    copy.wait()


def place_own(own, low, middle, high, selector):
    own[0:16, :] = placed(low, selector)
    own[16:32, :] = placed(jnp.concatenate(middle, axis=1), selector)
    own[32:48, :] = placed(high, selector)


def first_rest_kernel(
    bins, device_total, blocks, live, device, far, highs, lows, along, channels,
    near, own, geometry, home,
):
    low, middle, high = rest_of_grid(
        device, bins, block_row(blocks, bins, near.shape[1]), far, highs, lows, along, channels,
        near,
    )
    width = bins * SLOT
    position = iota((1, width), 1)
    column_bin = position // SLOT
    column_node = position - SLOT * column_bin
    column_valid = (column_node < TILE) & (column_node % 8 < 6)
    own_blocks = [blocks[b].astype(F32) for b in range(bins)]
    column_block = jnp.zeros((1, width), F32)
    for b in range(bins):
        column_block = jnp.where(column_bin == b, own_blocks[b], column_block)
    column_y, column_z = node_key(column_block, column_node.astype(F32))
    column_key = jnp.where(column_valid, LANES * column_y + column_z, -1.0)
    selector = placing(own_blocks, column_key, bins)
    home[...] = selector
    place_own(own, low, middle, high, selector)
    sub = iota((8, width), 0)
    wide_y = jnp.broadcast_to(column_y, (8, width))
    wide_z = jnp.broadcast_to(column_z, (8, width))
    geometry[0:8, :] = jnp.broadcast_to(column_key, (8, width))
    geometry[8:16, :] = jnp.where(
        ((sub == 2) & (wide_y < 2.0)) | ((sub == 3) & (wide_z < 2.0)), 0.0, -BIG
    )
    geometry[16:24, :] = jnp.where(
        ((sub == 2) & (wide_y >= NGY - 2.0)) | ((sub == 3) & (wide_z >= NGZ - 2.0)), 0.0, BIG
    )


def rest_kernel(
    bins, device_total, live, device, far, highs, lows, along, channels, home, near, own
):
    low, middle, high = rest_of_grid(
        device, bins, None, far, highs, lows, along, channels, near
    )
    place_own(own, low, middle, high, home[...])


def second_kernel(
    bins, device_total, live, device, old_ref, speeds, own, geometry, old_highs, old_lows,
    old_along, near, outer, inner, state_ref, new_speeds, new_far, highs, lows, along, channels,
    sides_ref, across, outbox, sem,
):
    around = halos(near, outer, inner, device, device_total)
    key = geometry[0:1, :]
    sides = [placing(halo_blocks(block, bins), key, bins) for block in around]
    for side in range(2):
        sides_ref[side] = sides[side]
    advance(
        bins, device_total, device, old_ref, speeds, own, geometry, old_highs, old_lows,
        old_along, around, sides, state_ref, new_speeds, new_far, highs, lows, along, channels,
        across, outbox, sem,
    )


def later_kernel(
    bins, device_total, live, device, old_ref, speeds, own, geometry, old_highs, old_lows,
    old_along, near, outer, inner, sides_ref, state_ref, new_speeds, new_far, highs, lows, along, channels,
    across, outbox, sem,
):
    around = halos(near, outer, inner, device, device_total)
    sides = [sides_ref[0], sides_ref[1]]
    advance(
        bins, device_total, device, old_ref, speeds, own, geometry, old_highs, old_lows,
        old_along, around, sides, state_ref, new_speeds, new_far, highs, lows, along, channels,
        across, outbox, sem,
    )


def advance(
    bins, device_total, device, old_ref, speeds, own, geometry, old_highs, old_lows,
    old_along, around, sides, state_ref, new_speeds, far, highs, lows, along, channels,
    across, outbox, sem,
):
    rows = state_ref.shape[0] // ROWS
    state = read_state(old_ref, rows)
    state, velocity, affine = to_particles(
        state, device, bins, device_total, geometry, own, sides, speeds, around, old_highs,
        old_lows, old_along, channels,
    )
    write_state(state_ref, state)
    copy = send_speed(velocity, state[MASS], new_speeds, outbox, sem)
    to_grid(
        state, velocity, affine, state_ref, device, bins, None, far, highs, lows, along, channels, across
    )
    copy.wait()


def last_kernel(
    bins, device_total, live, device, old_ref, speeds, own, geometry, highs, lows, along,
    near, outer, inner, sides_ref, d_out, v_out, f_out, c_out, shuffle,
):
    rows = old_ref.shape[0] // ROWS
    quarters = rows // bins
    state = read_state(old_ref, rows)
    state, velocity, affine = to_particles(
        state, device, bins, device_total, geometry, own, [sides_ref[0], sides_ref[1]], speeds,
        halos(near, outer, inner, device, device_total), highs, lows, along, shuffle,
    )
    row_bin = iota((rows, LANES), 0) // quarters
    alive = row_bin < live[0]
    half = rows * LANES
    results = (
        (d_out, state[TRAV : TRAV + 3]),
        (v_out, velocity),
        (f_out, state[DEF : DEF + 9]),
        (c_out, affine),
    )
    for ref, values in results:
        count = len(values)
        for number in range(count):
            value = jnp.where(alive, values[number], 0.0)
            for s in range(rows):
                ref[pl.ds(number, 1), pl.ds(LANES * s, LANES)] = value[s : s + 1, :]
        total = ref.shape[1]
        ref[:, pl.ds(half, total - half)] = jnp.zeros((count, total - half), F32)


def local(positions, velocity, deformation, affine, particle_mass, volume, bin_block, live_count):
    slot_total = bin_block.shape[0]
    per_bin = positions.shape[1] // slot_total
    bins = slot_total // 2
    device_total = lax.axis_size("space")
    rows = bins * per_bin // LANES
    half = rows * LANES
    nodes = bins * TILE
    width = bins * SLOT
    message = ((16, -(-(nodes + LANES // 2) // LANES) * LANES), F32)
    held = [
        ((ROWS * rows, LANES), F32),
        ((device_total, LANES), F32),
        message,
        ((bins, 3 * TILE, per_bin), BF16),
        ((bins, 3 * TILE, per_bin), BF16),
        ((12 * rows, LANES), F32),
        ((4 * 8 * rows, LANES), F32),
    ]
    speeds_shape = held[1]
    own_shape = ((48, width), F32)
    geometry_shape = ((24, width), F32)
    home_shape = ((nodes, width), BF16)
    sides_shape = ((2, nodes, width), BF16)
    smem = pl.BlockSpec(memory_space=pltpu.SMEM)
    vmem = pl.BlockSpec(memory_space=pltpu.VMEM)
    anywhere = pl.BlockSpec(memory_space=pl.ANY)
    working = [
        pltpu.VMEM((12 * rows, LANES), F32),
        pltpu.VMEM((device_total, LANES), F32),
        pltpu.SemaphoreType.DMA,
    ]
    bin_block = bin_block if INTERPRET else pltpu.with_memory_space_constraint(bin_block, pltpu.HBM)
    me = lax.axis_index("space").astype(jnp.int32).reshape(1)

    def stay(array, space=pltpu.VMEM):
        return array if INTERPRET else pltpu.with_memory_space_constraint(array, space)

    def call(body, scalars, arguments, outputs, scratch, in_specs=None, final=False):
        def kernel(*refs):
            count = len(scalars)
            body(bins, device_total, *refs[: count - 1], refs[count - 1][0], *refs[count:])

        extra = {}
        out_specs = tuple(anywhere if output == speeds_shape else vmem for output in outputs)
        if in_specs is None:
            in_specs = [vmem] * len(arguments)
            arguments = [stay(argument) for argument in arguments]
        else:
            arguments = [stay(argument, pltpu.HBM) for argument in arguments]
            out_specs = tuple(
                anywhere
                if output == speeds_shape
                else pl.BlockSpec(output[0], lambda i, rank=len(output[0]): (0,) * rank)
                for output in outputs
            )
            extra = {"grid": (1,)}
        make = jax.ShapeDtypeStruct if final or INTERPRET else pltpu.VMEM
        return pl.pallas_call(
            kernel,
            in_specs=[smem] * len(scalars) + in_specs,
            out_shape=tuple(
                pltpu.HBM(*output) if output == speeds_shape and not INTERPRET else make(*output)
                for output in outputs
            ),
            out_specs=out_specs,
            scratch_shapes=scratch,
            interpret=INTERPRET,
            compiler_params=pltpu.CompilerParams(vmem_limit_bytes=GRANT),
            **extra,
        )(*scalars, *arguments)

    def first_half(count):
        return pl.BlockSpec((count, half), lambda i: (0, 0))

    flat_half = pl.BlockSpec((half,), lambda i: (0,))
    length = device_total
    swap_pairs = [(i, i ^ 1) for i in range(length)]
    inner_pairs = [(i, i ^ 3) for i in range(length)]
    outer_pairs = [(i, i + 1) for i in range(3, length - 1, 4)]
    outer_pairs = outer_pairs + [(i, i + 3) for i in range(2, length - 3, 4)]
    outer_pairs = outer_pairs + [(0, 1), (length - 2, length - 1)]
    outer_pairs = outer_pairs + [(j, i) for i, j in outer_pairs]

    results = call(
        first_kernel,
        (bin_block, live_count, me),
        (positions, velocity, deformation, affine, particle_mass, volume),
        held,
        working + [pltpu.VMEM((12 * rows, LANES), F32)],
        [first_half(3), first_half(3), first_half(9), first_half(9), flat_half, flat_half],
    )
    sides = ()
    for step in range(STEPS):
        state, speeds, far, highs, lows, along, channels = results[:7]
        sides = sides + tuple(results[7:])
        speeds = lax.all_to_all(speeds, "space", 0, 0, tiled=True)
        from_outer = lax.ppermute(far, "space", outer_pairs)
        from_inner = lax.ppermute(far, "space", inner_pairs)
        arguments = (far, highs, lows, along, channels)
        if step == 0:
            near, own, geometry, home = call(
                first_rest_kernel,
                (bin_block, live_count, me),
                arguments,
                [message, own_shape, geometry_shape, home_shape],
                [],
            )
        else:
            near, own = call(
                rest_kernel, (live_count, me), arguments + (home,), [message, own_shape], []
            )
        from_near = lax.ppermute(near, "space", swap_pairs)
        arguments = (state, speeds, own, geometry, highs, lows, along, from_near, from_outer, from_inner, *sides)
        if step < STEPS - 1:
            results = call(
                second_kernel if step == 0 else later_kernel,
                (live_count, me),
                arguments,
                held + ([sides_shape] if step == 0 else []),
                working,
            )
    total = positions.shape[1]
    return call(
        last_kernel,
        (live_count, me),
        arguments,
        [((count, total), F32) for count in (3, 3, 9, 9)],
        [pltpu.VMEM((4 * 8 * rows, LANES), F32)],
        final=True,
    )


def solution(mesh):
    in_specs = (
        P(None, "space"),
        P(None, "space"),
        P(None, "space"),
        P(None, "space"),
        P("space"),
        P("space"),
        P("space"),
        P("space"),
    )
    out_specs = (P(None, "space"), P(None, "space"), P(None, "space"), P(None, "space"))
    return jax.shard_map(local, mesh=mesh, in_specs=in_specs, out_specs=out_specs, check_vma=False)
```

```python
import jax
import jax.numpy as jnp
from jax import lax
from jax.experimental import pallas as pl
from jax.experimental.pallas import tpu as pltpu
from jax.sharding import PartitionSpec as P


BZ = 16
STEPS = 3
NGY = 66
NGZ = 66

mu_shear = 4.0
lame_first = 6.0
courant = 0.15
sound_speed = 3.7416573867739413
mass_floor = 0.05
gravity_x = 3.0
gravity_z = -9.0

LANES = 128
TILE = 48
SLOT = 64
META = 64
BIG = 3.0e38
GRANT = 8 * 2**20
F32 = jnp.float32
BF16 = jnp.bfloat16
INTERPRET = False

POS, DEF, MASS, VOL, TRAV = 0, 3, 12, 13, 14
ROWS = 17


def iota(shape, dim):
    return lax.broadcasted_iota(jnp.int32, shape, dim)


def split(value):
    high = value.astype(BF16)
    low = (value - high.astype(F32)).astype(BF16)
    return high, low


def dot_nt(a, b):
    return lax.dot_general(a, b, (((1,), (1,)), ((), ())), preferred_element_type=F32)


def dot_nn(a, b):
    return lax.dot_general(a, b, (((1,), (0,)), ((), ())), preferred_element_type=F32)


def spline(distance):
    magnitude = jnp.abs(distance)
    outer = jnp.maximum(1.5 - magnitude, 0.0)
    inner = jnp.maximum(0.5 - magnitude, 0.0)
    return 0.5 * outer * outer - 1.5 * inner * inner


def spread(ref, row, quarters):
    return jnp.concatenate(
        [ref[pl.ds(row + q, 8, stride=0), :] for q in range(quarters)], axis=1
    )


def dense_weights(position, ref):
    rows = position.shape[0]
    for a in range(6):
        offset = float(a) - position
        weight = spline(offset)
        ref[pl.ds(rows * a, rows), :] = weight
        ref[pl.ds(rows * (6 + a), rows), :] = weight * offset


def pair_weights(state_ref, across, row, span):
    rows = across.shape[0] // 12
    along_z = spread(state_ref, 2 * rows + row, span)
    third_node = iota(along_z.shape, 0)
    third_offset = third_node.astype(F32) - along_z
    third = jnp.where(third_node < 6, spline(third_offset), 0.0)
    third_moved = third * third_offset
    plain, moved_y, moved_z = [], [], []
    for a in range(6):
        second = spread(across, rows * a + row, span)
        second_moved = spread(across, rows * (6 + a) + row, span)
        plain.append(second * third)
        moved_y.append(second_moved * third)
        moved_z.append(second * third_moved)
    return [jnp.concatenate(part, axis=0) for part in (plain, moved_y, moved_z)]


def kirchhoff(deform):
    determinant = (
        deform[0] * (deform[4] * deform[8] - deform[5] * deform[7])
        - deform[1] * (deform[3] * deform[8] - deform[5] * deform[6])
        + deform[2] * (deform[3] * deform[7] - deform[4] * deform[6])
    )
    pressure = lame_first * (determinant - 1.0) * determinant
    stress = [None] * 9
    for r in range(3):
        for c in range(r, 3):
            product = (
                deform[3 * r] * deform[3 * c]
                + deform[3 * r + 1] * deform[3 * c + 1]
                + deform[3 * r + 2] * deform[3 * c + 2]
            )
            if r == c:
                stress[3 * r + c] = mu_shear * (product - 1.0) + pressure
            else:
                stress[3 * r + c] = mu_shear * product
                stress[3 * c + r] = stress[3 * r + c]
    return stress


def send_speed(velocity, mass, speeds, outbox, sem):
    speed = velocity[0] * velocity[0] + velocity[1] * velocity[1] + velocity[2] * velocity[2]
    speed = jnp.max(jnp.where(mass > 0.0, speed, 0.0), axis=0, keepdims=True)
    speed = jnp.max(speed, axis=1, keepdims=True)
    outbox[...] = jnp.broadcast_to(speed, outbox.shape)
    pltpu.make_async_copy(outbox, speeds, sem).start()


def halves(quarters):
    parts = 2 if quarters % 2 == 0 else 1
    span = quarters // parts
    return [(part * span, span, pl.ds(part * span * LANES, span * LANES)) for part in range(parts)]


def plane_sums(planes, row, span, channels, along, tables):
    rows = along.shape[0] // 12

    def channel(matrix):
        begin = 8 * (matrix * rows + row)
        return jnp.concatenate(
            [channels[pl.ds(begin + 8 * q, 8), :] for q in range(span)], axis=1
        )

    base, slope_x, slope_y, slope_z = [channel(matrix) for matrix in range(4)]
    pieces = ([], [], [])
    for a in planes:
        first = spread(along, rows * a + row, span)
        first_moved = spread(along, rows * (6 + a) + row, span)
        pieces[0].append(first * base + first_moved * slope_x)
        pieces[1].append(first * slope_y)
        pieces[2].append(first * slope_z)
    count = 8 * len(planes)
    total = None
    for piece, (right_high, right_low) in zip(pieces, tables):
        left_high, left_low = split(jnp.concatenate(piece, axis=0))
        both = dot_nt(jnp.concatenate([left_high, left_low], axis=0), right_high)
        product = both[0:count] + both[count : 2 * count] + dot_nt(left_high, right_low)
        total = product if total is None else total + product
    return total


def far_planes(device):
    return 4 * (device % 2)


def to_grid(
    state, velocity, affine, state_ref, device, bins, meta, far, highs, lows, along, channels, across
):
    rows = state[0].shape[0]
    quarters = rows // bins
    deform = state[DEF : DEF + 9]
    mass, volume = state[MASS], state[VOL]
    stress = kirchhoff(deform)
    scaled = 4.0 * volume
    span = 8 * rows
    zero = jnp.zeros((rows, LANES), F32)

    def put(matrix, row, value):
        channels[pl.ds(matrix * span + row, rows, stride=8), :] = value

    put(0, 0, mass)
    for c in range(3):
        put(0, 1 + c, mass * velocity[c])
        put(0, 4 + c, zero)
    put(0, 7, zero)
    for axis in range(3):
        put(1 + axis, 0, zero)
        put(1 + axis, 7, zero)
        for c in range(3):
            put(1 + axis, 1 + c, mass * affine[3 * c + axis])
            put(1 + axis, 4 + c, scaled * stress[3 * c + axis])
    dense_weights(state[0], along)
    dense_weights(state[1], across)
    base = far_planes(device)
    for b in range(bins):
        total = None
        for begin, width, lanes in halves(quarters):
            row = b * quarters + begin
            tables = []
            for kind, values in enumerate(pair_weights(state_ref, across, row, width)):
                high, low = split(values)
                highs[b, pl.ds(kind * TILE, TILE), lanes] = high
                lows[b, pl.ds(kind * TILE, TILE), lanes] = low
                tables.append((high, low))
            sums = plane_sums((base, base + 1), row, width, channels, along, tables)
            total = sums if total is None else total + sums
        far[:, TILE * b : TILE * (b + 1)] = total
    nodes = bins * TILE
    width = far.shape[1]
    far[:, nodes:width] = jnp.broadcast_to(meta[0:1, nodes:width], (16, width - nodes))


def rest_of_grid(device, bins, meta, far, highs, lows, along, channels, near):
    rows = along.shape[0] // 12
    quarters = rows // bins
    odd = device % 2 == 1
    base = 4 - far_planes(device)
    middle = []
    for b in range(bins):
        total = None
        for begin, width, lanes in halves(quarters):
            row = b * quarters + begin
            tables = [
                (highs[b, pl.ds(kind * TILE, TILE), lanes], lows[b, pl.ds(kind * TILE, TILE), lanes])
                for kind in range(3)
            ]
            sums = plane_sums((base, base + 1, 2, 3), row, width, channels, along, tables)
            total = sums if total is None else total + sums
        near[:, TILE * b : TILE * (b + 1)] = total[0:16]
        middle.append(total[16:32])
    nodes = bins * TILE
    width = near.shape[1]
    near[:, nodes:width] = jnp.broadcast_to(meta[0:1, nodes:width], (16, width - nodes))
    near_part, far_part = near[:, 0:nodes], far[:, 0:nodes]
    low = jnp.where(odd, near_part, far_part)
    high = jnp.where(odd, far_part, near_part)
    return low, middle, high


def node_key(block, node):
    block_y = jnp.floor((block + 0.5) * (1.0 / BZ))
    block_z = block - BZ * block_y
    node_y = jnp.floor((node + 0.5) * (1.0 / 8.0))
    node_z = node - 8.0 * node_y
    return 4.0 * block_y + node_y, 4.0 * block_z + node_z


def placing(source_block, column_key, bins):
    nodes = bins * TILE
    source = iota((nodes, 1), 0).astype(F32)
    source_bin = jnp.floor((source + 0.5) * (1.0 / TILE))
    source_node = source - TILE * source_bin
    block = jnp.zeros((nodes, 1), F32)
    for b in range(bins):
        block = jnp.where(source_bin == float(b), source_block[b], block)
    row_y, row_z = node_key(block, source_node)
    row_key = LANES * row_y + row_z
    used = source_node - 8.0 * jnp.floor((source_node + 0.5) * (1.0 / 8.0)) < 6.0
    row_key = jnp.where(used, row_key, -2.0)
    return jnp.where(row_key == column_key, 1.0, 0.0).astype(BF16)


def placed(values, selector):
    count = values.shape[0]
    high, low = split(values)
    result = dot_nn(jnp.concatenate([high, low], axis=0), selector)
    return result[0:count] + result[count : 2 * count]


def halos(near, outer, inner, device, device_total):
    odd = device % 2 == 1
    middle = (device + 1) % 4 >= 2
    near_block = near[...]
    far_block = jnp.where(middle, inner[...], outer[...])
    left_block = jnp.where(odd, near_block, far_block)
    right_block = jnp.where(odd, far_block, near_block)
    left_block = jnp.where(device > 0, left_block, 0.0)
    right_block = jnp.where(device + 1 < device_total, right_block, 0.0)
    return left_block, right_block


def block_numbers(row, bins):
    lane = iota((1, LANES), 1)
    return [
        jnp.max(jnp.where(lane == META + b, row[:, LANES : 2 * LANES], 0.0), axis=1, keepdims=True)
        for b in range(bins)
    ]


def to_particles(
    live, old_ref, device, bins, device_total, geometry, own, sides, speeds, blocks_around,
    highs, lows, along, shuffle, started, finish,
):
    rows = old_ref.shape[0] // ROWS
    quarters = rows // bins
    state = read_state(old_ref, rows)
    width = bins * SLOT
    nodes = bins * TILE
    fastest = jnp.max(speeds[...], axis=0, keepdims=True)
    fastest = jnp.max(fastest, axis=1, keepdims=True)
    time_step = courant / (jnp.sqrt(fastest) + sound_speed)

    around = []
    for side, block in enumerate(blocks_around):
        around.append(placed(block[:, 0:nodes], sides[side]))
    left, right = around

    sub = iota((8, width), 0)
    wide_valid = geometry[0:8, :] >= 0.0
    component = (sub >= 1) & (sub <= 3) & wide_valid
    floor_of = geometry[8:16, :]
    roof_of = geometry[16:24, :]
    pull = time_step * jnp.where(sub == 1, gravity_x, jnp.where(sub == 3, gravity_z, 0.0))
    plane_total = 4 * device_total
    motions = []
    for a in range(6):
        sums = own[8 * a : 8 * a + 8, :]
        if a < 2:
            sums = sums + left[8 * a : 8 * a + 8]
        if a >= 4:
            sums = sums + right[8 * a - 32 : 8 * a - 24]
        plane = 4 * device + a
        node_mass = jnp.maximum(jnp.broadcast_to(sums[0:1, :], (8, width)), mass_floor)
        per_step = pltpu.roll(sums, 5, 0)
        motion = (sums - time_step * per_step) / node_mass + pull
        lowest = jnp.where(plane < 2, 0.0, -BIG)
        highest = jnp.where(plane >= plane_total - 2, 0.0, BIG)
        motion = jnp.maximum(motion, jnp.where(sub == 1, lowest, floor_of))
        motion = jnp.minimum(motion, jnp.where(sub == 1, highest, roof_of))
        inside = jnp.where(plane < plane_total, 1, 0)
        motion = jnp.where(component & (inside > 0), motion, 0.0)
        motions.append(motion)
    paired = jnp.concatenate(
        [motions[2 * g] + pltpu.roll(motions[2 * g + 1], 4, 0) for g in range(3)], axis=0
    )

    span = 8 * rows
    blocks = []
    for b in range(bins):
        begin = (b * SLOT) // LANES * LANES
        block = paired[:, begin : begin + LANES]
        if b * SLOT > begin:
            block = pltpu.roll(block, LANES - (b * SLOT - begin), 1)
        block = block[:, 0:TILE]
        high = block.astype(BF16)
        kept = high.astype(F32)
        blocks.append((jnp.concatenate([kept, block - kept], axis=0).astype(BF16), high))

    def gather(kinds):
        for b in range(bins):
            stacked, high = blocks[b]
            count = high.shape[0]
            for first_quarter, wide, lanes in halves(quarters):
                row = b * quarters + first_quarter
                even = iota((8, wide * LANES), 0) < 4

                def pair_weights_of(begin):
                    return [
                        jnp.where(
                            even,
                            spread(along, rows * (begin + 2 * g) + row, wide),
                            spread(along, rows * (begin + 2 * g + 1) + row, wide),
                        )
                        for g in range(3)
                    ]

                weights = pair_weights_of(0)
                for kind in kinds:
                    right_high = highs[b, pl.ds(kind * TILE, TILE), lanes]
                    right_low = lows[b, pl.ds(kind * TILE, TILE), lanes]
                    product = dot_nn(stacked, right_high)
                    product = product[0:count] + product[count : 2 * count]
                    product = product + dot_nn(high, right_low)
                    groups = [product[8 * g : 8 * g + 8] for g in range(3)]
                    sums = [(kind, sum(w * group for w, group in zip(weights, groups)))]
                    if kind == 0:
                        moved = zip(pair_weights_of(6), groups)
                        sums.append((3, sum(w * group for w, group in moved)))
                    for target, value in sums:
                        for q in range(wide):
                            place = target * span + 8 * (row + q)
                            shuffle[pl.ds(place, 8), :] = value[:, LANES * q : LANES * (q + 1)]

    def take(kind, c):
        return (
            shuffle[pl.ds(kind * span + 1 + c, rows, stride=8), :]
            + shuffle[pl.ds(kind * span + 5 + c, rows, stride=8), :]
        )

    gather((0, 1, 2) if live is None else (0,))
    started([take(0, c) for c in range(3)])

    def rest():
        if live is not None:
            gather((1, 2))
        velocity = [take(0, c) for c in range(3)]
        affine = [None] * 9
        for c in range(3):
            affine[3 * c] = 4.0 * take(3, c)
            affine[3 * c + 1] = 4.0 * take(1, c)
            affine[3 * c + 2] = 4.0 * take(2, c)
        old = state[DEF : DEF + 9]
        deform = []
        for r in range(3):
            for c in range(3):
                change = (
                    affine[3 * r] * old[c]
                    + affine[3 * r + 1] * old[3 + c]
                    + affine[3 * r + 2] * old[6 + c]
                )
                deform.append(old[3 * r + c] + time_step * change)
        steps = [time_step * velocity[c] for c in range(3)]
        moved = [state[c] + steps[c] for c in range(3)]
        travelled = [state[TRAV + c] + steps[c] for c in range(3)]
        finish(moved + deform + [state[MASS], state[VOL]] + travelled, velocity, affine)

    if live is None:
        rest()
    else:
        pl.when(live[0] >= 0)(rest)


def read_state(ref, rows):
    return [ref[pl.ds(rows * number, rows), :] for number in range(ROWS)]


def write_state(ref, state):
    rows = state[0].shape[0]
    for number in range(ROWS):
        ref[pl.ds(rows * number, rows), :] = state[number]


def block_row(blocks, bins, width):
    lane = iota((1, width), 1)
    meta = jnp.zeros((1, width), F32)
    for b in range(bins):
        meta = jnp.where(lane == LANES + META + b, blocks[b].astype(F32), meta)
    return meta


def first_kernel(
    bins, device_total, blocks, live, device, x_ref, v_ref, f_ref, c_ref, m_ref, vol_ref,
    state_ref, motion_ref, speeds, meta, outbox, sem,
):
    rows = state_ref.shape[0] // ROWS
    quarters = rows // bins

    def relay(ref, count, kept, begin):
        for number in range(count):
            for s in range(rows):
                target = rows * (begin + number) + s
                kept[pl.ds(target, 1), :] = ref[pl.ds(number, 1), pl.ds(LANES * s, LANES)]

    def relay_flat(ref, number):
        for b in range(bins):
            alive = jnp.where(b < live[0], 1.0, 0.0)
            for q in range(quarters):
                s = quarters * b + q
                piece = ref[pl.ds(LANES * s, LANES)].reshape(1, LANES)
                state_ref[pl.ds(rows * number + s, 1), :] = piece * alive

    relay(v_ref, 3, motion_ref, 0)
    relay_flat(m_ref, MASS)
    motion = [motion_ref[pl.ds(rows * number, rows), :] for number in range(3)]
    send_speed(motion, state_ref[pl.ds(rows * MASS, rows), :], speeds, outbox, sem)

    @pl.when(live[0] >= 0)
    def _():
        relay(x_ref, 3, state_ref, POS)
        relay(f_ref, 9, state_ref, DEF)
        relay(c_ref, 9, motion_ref, 3)
        relay_flat(vol_ref, VOL)
        home = jnp.zeros((rows, LANES), F32)
        home_y, home_z = home, home
        row_bin = iota((rows, LANES), 0) // quarters
        for b in range(bins):
            block = blocks[b]
            block_y = block // BZ
            block_z = block - BZ * block_y
            home_y = jnp.where(row_bin == b, (4 * block_y).astype(F32), home_y)
            home_z = jnp.where(row_bin == b, (4 * block_z).astype(F32), home_z)
        anchors = (home + (4 * device).astype(F32), home_y, home_z)
        for axis in range(3):
            place = pl.ds(rows * axis, rows)
            state_ref[place, :] = state_ref[place, :] - anchors[axis]
            state_ref[pl.ds(rows * (TRAV + axis), rows), :] = home
        meta[...] = jnp.broadcast_to(block_row(blocks, bins, meta.shape[1]), meta.shape)

    pltpu.make_async_copy(outbox, speeds, sem).wait()


def scatter_kernel(
    bins, device_total, live, device, state_ref, motion_ref, meta, far, highs, lows, along,
    channels, across,
):
    rows = state_ref.shape[0] // ROWS
    motion = [motion_ref[pl.ds(rows * number, rows), :] for number in range(12)]
    to_grid(
        read_state(state_ref, rows), motion[0:3], motion[3:12], state_ref, device, bins, meta, far,
        highs, lows, along, channels, across,
    )


def place_own(own, low, middle, high, selector):
    own[0:16, :] = placed(low, selector)
    own[16:32, :] = placed(jnp.concatenate(middle, axis=1), selector)
    own[32:48, :] = placed(high, selector)


def first_rest_kernel(
    bins, device_total, live, device, meta, far, highs, lows, along, channels,
    near, own, geometry, home,
):
    low, middle, high = rest_of_grid(
        device, bins, meta, far, highs, lows, along, channels, near
    )
    width = bins * SLOT
    position = iota((1, width), 1)
    column_bin = position // SLOT
    column_node = position - SLOT * column_bin
    column_valid = (column_node < TILE) & (column_node % 8 < 6)
    own_blocks = block_numbers(meta[0:1, :], bins)
    column_block = jnp.zeros((1, width), F32)
    for b in range(bins):
        column_block = jnp.where(column_bin == b, own_blocks[b], column_block)
    column_y, column_z = node_key(column_block, column_node.astype(F32))
    column_key = jnp.where(column_valid, LANES * column_y + column_z, -1.0)
    selector = placing(own_blocks, column_key, bins)
    home[...] = selector
    place_own(own, low, middle, high, selector)
    sub = iota((8, width), 0)
    wide_y = jnp.broadcast_to(column_y, (8, width))
    wide_z = jnp.broadcast_to(column_z, (8, width))
    geometry[0:8, :] = jnp.broadcast_to(column_key, (8, width))
    geometry[8:16, :] = jnp.where(
        ((sub == 2) & (wide_y < 2.0)) | ((sub == 3) & (wide_z < 2.0)), 0.0, -BIG
    )
    geometry[16:24, :] = jnp.where(
        ((sub == 2) & (wide_y >= NGY - 2.0)) | ((sub == 3) & (wide_z >= NGZ - 2.0)), 0.0, BIG
    )


def rest_kernel(
    bins, device_total, live, device, meta, far, highs, lows, along, channels, home, near, own
):
    low, middle, high = rest_of_grid(
        device, bins, meta, far, highs, lows, along, channels, near
    )
    place_own(own, low, middle, high, home[...])


def second_kernel(
    bins, device_total, live, device, old_ref, speeds, own, geometry, highs, lows, along,
    near, outer, inner, state_ref, motion_ref, new_speeds, sides_ref, shuffle, outbox, sem,
):
    around = halos(near, outer, inner, device, device_total)
    key = geometry[0:1, :]
    sides = [placing(block_numbers(block[7:8, :], bins), key, bins) for block in around]
    for side in range(2):
        sides_ref[side] = sides[side]
    advance(
        live, bins, device_total, device, old_ref, speeds, own, geometry, highs, lows, along, around,
        sides, state_ref, motion_ref, new_speeds, shuffle, outbox, sem,
    )


def later_kernel(
    bins, device_total, live, device, old_ref, speeds, own, geometry, highs, lows, along,
    near, outer, inner, sides_ref, state_ref, motion_ref, new_speeds, shuffle, outbox, sem,
):
    around = halos(near, outer, inner, device, device_total)
    sides = [sides_ref[0], sides_ref[1]]
    advance(
        live, bins, device_total, device, old_ref, speeds, own, geometry, highs, lows, along, around,
        sides, state_ref, motion_ref, new_speeds, shuffle, outbox, sem,
    )


def advance(
    live, bins, device_total, device, old_ref, speeds, own, geometry, highs, lows, along, around,
    sides, state_ref, motion_ref, new_speeds, shuffle, outbox, sem,
):
    rows = state_ref.shape[0] // ROWS

    def started(velocity):
        send_speed(velocity, old_ref[pl.ds(rows * MASS, rows), :], new_speeds, outbox, sem)

    def finish(state, velocity, affine):
        write_state(state_ref, state)
        for number, value in enumerate(velocity + affine):
            motion_ref[pl.ds(rows * number, rows), :] = value

    to_particles(
        live, old_ref, device, bins, device_total, geometry, own, sides, speeds, around, highs,
        lows, along, shuffle, started, finish,
    )
    pltpu.make_async_copy(outbox, new_speeds, sem).wait()


def last_kernel(
    bins, device_total, live, device, old_ref, speeds, own, geometry, highs, lows, along,
    near, outer, inner, sides_ref, d_out, v_out, f_out, c_out, shuffle,
):
    rows = old_ref.shape[0] // ROWS
    quarters = rows // bins
    row_bin = iota((rows, LANES), 0) // quarters
    alive = row_bin < live[0]
    half = rows * LANES

    def finish(state, velocity, affine):
        results = (
            (d_out, state[TRAV : TRAV + 3]),
            (v_out, velocity),
            (f_out, state[DEF : DEF + 9]),
            (c_out, affine),
        )
        for ref, values in results:
            count = len(values)
            for number in range(count):
                value = jnp.where(alive, values[number], 0.0)
                for s in range(rows):
                    ref[pl.ds(number, 1), pl.ds(LANES * s, LANES)] = value[s : s + 1, :]
            total = ref.shape[1]
            ref[:, pl.ds(half, total - half)] = jnp.zeros((count, total - half), F32)

    to_particles(
        None, old_ref, device, bins, device_total, geometry, own, [sides_ref[0], sides_ref[1]], speeds,
        halos(near, outer, inner, device, device_total), highs, lows, along, shuffle,
        lambda velocity: None, finish,
    )


def local(positions, velocity, deformation, affine, particle_mass, volume, bin_block, live_count):
    slot_total = bin_block.shape[0]
    per_bin = positions.shape[1] // slot_total
    bins = slot_total // 2
    device_total = lax.axis_size("space")
    rows = bins * per_bin // LANES
    half = rows * LANES
    nodes = bins * TILE
    width = bins * SLOT
    message = ((16, -(-(nodes + LANES // 2) // LANES) * LANES), F32)
    speeds_shape = ((device_total, LANES), F32)
    held = [((ROWS * rows, LANES), F32), ((12 * rows, LANES), F32), speeds_shape]
    grid_held = [
        message,
        ((bins, 3 * TILE, per_bin), BF16),
        ((bins, 3 * TILE, per_bin), BF16),
        ((12 * rows, LANES), F32),
        ((4 * 8 * rows, LANES), F32),
    ]
    meta_shape = ((8, message[0][1]), F32)
    own_shape = ((48, width), F32)
    geometry_shape = ((24, width), F32)
    home_shape = ((nodes, width), BF16)
    sides_shape = ((2, nodes, width), BF16)
    smem = pl.BlockSpec(memory_space=pltpu.SMEM)
    vmem = pl.BlockSpec(memory_space=pltpu.VMEM)
    anywhere = pl.BlockSpec(memory_space=pl.ANY)
    shuffle = pltpu.VMEM((4 * 8 * rows, LANES), F32)
    sending = [pltpu.VMEM((device_total, LANES), F32), pltpu.SemaphoreType.DMA]
    bin_block = bin_block if INTERPRET else pltpu.with_memory_space_constraint(bin_block, pltpu.HBM)
    me = lax.axis_index("space").astype(jnp.int32).reshape(1)

    def stay(array, space=pltpu.VMEM):
        return array if INTERPRET else pltpu.with_memory_space_constraint(array, space)

    def call(body, scalars, arguments, outputs, scratch, in_specs=None, final=False):
        def kernel(*refs):
            count = len(scalars)
            body(bins, device_total, *refs[: count - 1], refs[count - 1][0], *refs[count:])

        extra = {}
        out_specs = tuple(anywhere if output == speeds_shape else vmem for output in outputs)
        if in_specs is None:
            in_specs = [vmem] * len(arguments)
            arguments = [stay(argument) for argument in arguments]
        else:
            arguments = [stay(argument, pltpu.HBM) for argument in arguments]
            out_specs = tuple(
                anywhere
                if output == speeds_shape
                else pl.BlockSpec(output[0], lambda i, rank=len(output[0]): (0,) * rank)
                for output in outputs
            )
            extra = {"grid": (1,)}
        make = jax.ShapeDtypeStruct if final or INTERPRET else pltpu.VMEM
        return pl.pallas_call(
            kernel,
            in_specs=[smem] * len(scalars) + in_specs,
            out_shape=tuple(
                pltpu.HBM(*output) if output == speeds_shape and not INTERPRET else make(*output)
                for output in outputs
            ),
            out_specs=out_specs,
            scratch_shapes=scratch,
            interpret=INTERPRET,
            compiler_params=pltpu.CompilerParams(vmem_limit_bytes=GRANT),
            **extra,
        )(*scalars, *arguments)

    def first_half(count):
        return pl.BlockSpec((count, half), lambda i: (0, 0))

    flat_half = pl.BlockSpec((half,), lambda i: (0,))
    length = device_total
    swap_pairs = [(i, i ^ 1) for i in range(length)]
    inner_pairs = [(i, i ^ 3) for i in range(length)]
    outer_pairs = [(i, i + 1) for i in range(3, length - 1, 4)]
    outer_pairs = outer_pairs + [(i, i + 3) for i in range(2, length - 3, 4)]
    outer_pairs = outer_pairs + [(0, 1), (length - 2, length - 1)]
    outer_pairs = outer_pairs + [(j, i) for i, j in outer_pairs]

    *results, meta = call(
        first_kernel,
        (bin_block, live_count, me),
        (positions, velocity, deformation, affine, particle_mass, volume),
        held + [meta_shape],
        sending,
        [first_half(3), first_half(3), first_half(9), first_half(9), flat_half, flat_half],
    )
    sides = ()
    for step in range(STEPS):
        state, motion, speeds = results[:3]
        sides = sides + tuple(results[3:])
        speeds = lax.all_to_all(speeds, "space", 0, 0, tiled=True)
        far, highs, lows, along, channels = call(
            scatter_kernel,
            (live_count, me),
            (state, motion, meta),
            grid_held,
            [pltpu.VMEM((12 * rows, LANES), F32)],
        )
        from_outer = lax.ppermute(far, "space", outer_pairs)
        from_inner = lax.ppermute(far, "space", inner_pairs)
        arguments = (meta, far, highs, lows, along, channels)
        if step == 0:
            near, own, geometry, home = call(
                first_rest_kernel,
                (live_count, me),
                arguments,
                [message, own_shape, geometry_shape, home_shape],
                [],
            )
        else:
            near, own = call(
                rest_kernel, (live_count, me), arguments + (home,), [message, own_shape], []
            )
        from_near = lax.ppermute(near, "space", swap_pairs)
        arguments = (
            state, speeds, own, geometry, highs, lows, along, from_near, from_outer, from_inner,
            *sides,
        )
        if step < STEPS - 1:
            results = call(
                second_kernel if step == 0 else later_kernel,
                (live_count, me),
                arguments,
                held + ([sides_shape] if step == 0 else []),
                [shuffle] + sending,
            )
    total = positions.shape[1]
    return call(
        last_kernel,
        (live_count, me),
        arguments,
        [((count, total), F32) for count in (3, 3, 9, 9)],
        [shuffle],
        final=True,
    )


def solution(mesh):
    in_specs = (
        P(None, "space"),
        P(None, "space"),
        P(None, "space"),
        P(None, "space"),
        P("space"),
        P("space"),
        P("space"),
        P("space"),
    )
    out_specs = (P(None, "space"), P(None, "space"), P(None, "space"), P(None, "space"))
    return jax.shard_map(local, mesh=mesh, in_specs=in_specs, out_specs=out_specs, check_vma=False)
```

```python
import jax
import jax.numpy as jnp
from jax import lax
from jax.experimental import pallas as pl
from jax.experimental.pallas import tpu as pltpu
from jax.sharding import PartitionSpec as P


BZ = 16
STEPS = 3
NGY = 66
NGZ = 66

mu_shear = 4.0
lame_first = 6.0
courant = 0.15
sound_speed = 3.7416573867739413
mass_floor = 0.05
gravity_x = 3.0
gravity_z = -9.0

LANES = 128
TILE = 48
SLOT = 64
META = 64
BIG = 3.0e38
GRANT = 8 * 2**20
F32 = jnp.float32
BF16 = jnp.bfloat16
INTERPRET = False

POS, DEF, MASS, VOL, TRAV = 0, 3, 12, 13, 14
ROWS = 17


def iota(shape, dim):
    return lax.broadcasted_iota(jnp.int32, shape, dim)


def split(value):
    high = value.astype(BF16)
    low = (value - high.astype(F32)).astype(BF16)
    return high, low


def dot_nt(a, b):
    return lax.dot_general(a, b, (((1,), (1,)), ((), ())), preferred_element_type=F32)


def dot_nn(a, b):
    return lax.dot_general(a, b, (((1,), (0,)), ((), ())), preferred_element_type=F32)


def spline(distance):
    magnitude = jnp.abs(distance)
    outer = jnp.maximum(1.5 - magnitude, 0.0)
    inner = jnp.maximum(0.5 - magnitude, 0.0)
    return 0.5 * outer * outer - 1.5 * inner * inner


def spread(ref, row, quarters):
    return jnp.concatenate(
        [ref[pl.ds(row + q, 8, stride=0), :] for q in range(quarters)], axis=1
    )


def dense_weights(position, ref):
    rows = position.shape[0]
    for a in range(6):
        offset = float(a) - position
        weight = spline(offset)
        ref[pl.ds(rows * a, rows), :] = weight
        ref[pl.ds(rows * (6 + a), rows), :] = weight * offset


def pair_weights(state_ref, across, row, span):
    rows = across.shape[0] // 12
    along_z = spread(state_ref, 2 * rows + row, span)
    third_node = iota(along_z.shape, 0)
    third_offset = third_node.astype(F32) - along_z
    third = jnp.where(third_node < 6, spline(third_offset), 0.0)
    third_moved = third * third_offset
    plain, moved_y, moved_z = [], [], []
    for a in range(6):
        second = spread(across, rows * a + row, span)
        second_moved = spread(across, rows * (6 + a) + row, span)
        plain.append(second * third)
        moved_y.append(second_moved * third)
        moved_z.append(second * third_moved)
    return [jnp.concatenate(part, axis=0) for part in (plain, moved_y, moved_z)]


def kirchhoff(deform):
    determinant = (
        deform[0] * (deform[4] * deform[8] - deform[5] * deform[7])
        - deform[1] * (deform[3] * deform[8] - deform[5] * deform[6])
        + deform[2] * (deform[3] * deform[7] - deform[4] * deform[6])
    )
    pressure = lame_first * (determinant - 1.0) * determinant
    stress = [None] * 9
    for r in range(3):
        for c in range(r, 3):
            product = (
                deform[3 * r] * deform[3 * c]
                + deform[3 * r + 1] * deform[3 * c + 1]
                + deform[3 * r + 2] * deform[3 * c + 2]
            )
            if r == c:
                stress[3 * r + c] = mu_shear * (product - 1.0) + pressure
            else:
                stress[3 * r + c] = mu_shear * product
                stress[3 * c + r] = stress[3 * r + c]
    return stress


def send_speed(velocity, mass, speeds, outbox, sem):
    speed = velocity[0] * velocity[0] + velocity[1] * velocity[1] + velocity[2] * velocity[2]
    speed = jnp.max(jnp.where(mass > 0.0, speed, 0.0), axis=0, keepdims=True)
    speed = jnp.max(speed, axis=1, keepdims=True)
    outbox[...] = jnp.broadcast_to(speed, outbox.shape)
    pltpu.make_async_copy(outbox, speeds, sem).start()


def halves(quarters):
    parts = 2 if quarters % 2 == 0 else 1
    span = quarters // parts
    return [(part * span, span, pl.ds(part * span * LANES, span * LANES)) for part in range(parts)]


def plane_sums(planes, row, span, channels, along, tables):
    rows = along.shape[0] // 12

    def channel(matrix):
        begin = 8 * (matrix * rows + row)
        return jnp.concatenate(
            [channels[pl.ds(begin + 8 * q, 8), :] for q in range(span)], axis=1
        )

    base, slope_x, slope_y, slope_z = [channel(matrix) for matrix in range(4)]
    pieces = ([], [], [])
    for a in planes:
        first = spread(along, rows * a + row, span)
        first_moved = spread(along, rows * (6 + a) + row, span)
        pieces[0].append(first * base + first_moved * slope_x)
        pieces[1].append(first * slope_y)
        pieces[2].append(first * slope_z)
    count = 8 * len(planes)
    total = None
    for piece, (right_high, right_low) in zip(pieces, tables):
        left_high, left_low = split(jnp.concatenate(piece, axis=0))
        both = dot_nt(jnp.concatenate([left_high, left_low], axis=0), right_high)
        product = both[0:count] + both[count : 2 * count] + dot_nt(left_high, right_low)
        total = product if total is None else total + product
    return total


def far_planes(device):
    return 4 * (device % 2)


def to_grid(
    state, velocity, affine, state_ref, device, bins, meta, far, highs, lows, along, channels, across
):
    rows = state[0].shape[0]
    quarters = rows // bins
    deform = state[DEF : DEF + 9]
    mass, volume = state[MASS], state[VOL]
    stress = kirchhoff(deform)
    scaled = 4.0 * volume
    span = 8 * rows
    zero = jnp.zeros((rows, LANES), F32)

    def put(matrix, row, value):
        channels[pl.ds(matrix * span + row, rows, stride=8), :] = value

    put(0, 0, mass)
    for c in range(3):
        put(0, 1 + c, mass * velocity[c])
        put(0, 4 + c, zero)
    put(0, 7, zero)
    for axis in range(3):
        put(1 + axis, 0, zero)
        put(1 + axis, 7, zero)
        for c in range(3):
            put(1 + axis, 1 + c, mass * affine[3 * c + axis])
            put(1 + axis, 4 + c, scaled * stress[3 * c + axis])
    dense_weights(state[0], along)
    dense_weights(state[1], across)
    base = far_planes(device)
    for b in range(bins):
        total = None
        for begin, width, lanes in halves(quarters):
            row = b * quarters + begin
            tables = []
            for kind, values in enumerate(pair_weights(state_ref, across, row, width)):
                high, low = split(values)
                highs[b, pl.ds(kind * TILE, TILE), lanes] = high
                lows[b, pl.ds(kind * TILE, TILE), lanes] = low
                tables.append((high, low))
            sums = plane_sums((base, base + 1), row, width, channels, along, tables)
            total = sums if total is None else total + sums
        far[:, TILE * b : TILE * (b + 1)] = total
    nodes = bins * TILE
    width = far.shape[1]
    far[:, nodes:width] = jnp.broadcast_to(meta[0:1, nodes:width], (16, width - nodes))


def rest_of_grid(device, bins, meta, far, highs, lows, along, channels, near):
    rows = along.shape[0] // 12
    quarters = rows // bins
    odd = device % 2 == 1
    base = 4 - far_planes(device)
    middle = []
    for b in range(bins):
        total = None
        for begin, width, lanes in halves(quarters):
            row = b * quarters + begin
            tables = [
                (highs[b, pl.ds(kind * TILE, TILE), lanes], lows[b, pl.ds(kind * TILE, TILE), lanes])
                for kind in range(3)
            ]
            sums = plane_sums((base, base + 1, 2, 3), row, width, channels, along, tables)
            total = sums if total is None else total + sums
        near[:, TILE * b : TILE * (b + 1)] = total[0:16]
        middle.append(total[16:32])
    nodes = bins * TILE
    width = near.shape[1]
    near[:, nodes:width] = jnp.broadcast_to(meta[0:1, nodes:width], (16, width - nodes))
    near_part, far_part = near[:, 0:nodes], far[:, 0:nodes]
    low = jnp.where(odd, near_part, far_part)
    high = jnp.where(odd, far_part, near_part)
    return low, middle, high


def node_key(block, node):
    block_y = jnp.floor((block + 0.5) * (1.0 / BZ))
    block_z = block - BZ * block_y
    node_y = jnp.floor((node + 0.5) * (1.0 / 8.0))
    node_z = node - 8.0 * node_y
    return 4.0 * block_y + node_y, 4.0 * block_z + node_z


def placing(source_block, column_key, bins):
    nodes = bins * TILE
    source = iota((nodes, 1), 0).astype(F32)
    source_bin = jnp.floor((source + 0.5) * (1.0 / TILE))
    source_node = source - TILE * source_bin
    block = jnp.zeros((nodes, 1), F32)
    for b in range(bins):
        block = jnp.where(source_bin == float(b), source_block[b], block)
    row_y, row_z = node_key(block, source_node)
    row_key = LANES * row_y + row_z
    used = source_node - 8.0 * jnp.floor((source_node + 0.5) * (1.0 / 8.0)) < 6.0
    row_key = jnp.where(used, row_key, -2.0)
    return jnp.where(row_key == column_key, 1.0, 0.0).astype(BF16)


def placed(values, selector):
    count = values.shape[0]
    high, low = split(values)
    result = dot_nn(jnp.concatenate([high, low], axis=0), selector)
    return result[0:count] + result[count : 2 * count]


def halos(near, outer, inner, device, device_total):
    odd = device % 2 == 1
    middle = (device + 1) % 4 >= 2
    near_block = near[...]
    far_block = jnp.where(middle, inner[...], outer[...])
    left_block = jnp.where(odd, near_block, far_block)
    right_block = jnp.where(odd, far_block, near_block)
    left_block = jnp.where(device > 0, left_block, 0.0)
    right_block = jnp.where(device + 1 < device_total, right_block, 0.0)
    return left_block, right_block


def block_numbers(row, bins):
    lane = iota((1, LANES), 1)
    return [
        jnp.max(jnp.where(lane == META + b, row[:, LANES : 2 * LANES], 0.0), axis=1, keepdims=True)
        for b in range(bins)
    ]


def to_particles(
    live, old_ref, device, bins, device_total, geometry, own, sides, speeds, blocks_around,
    highs, lows, along, shuffle, started, finish,
):
    rows = old_ref.shape[0] // ROWS
    quarters = rows // bins
    state = read_state(old_ref, rows)
    width = bins * SLOT
    nodes = bins * TILE
    fastest = jnp.max(speeds[...], axis=0, keepdims=True)
    fastest = jnp.max(fastest, axis=1, keepdims=True)
    time_step = courant / (jnp.sqrt(fastest) + sound_speed)

    around = []
    for side, block in enumerate(blocks_around):
        around.append(placed(block[:, 0:nodes], sides[side]))
    left, right = around

    sub = iota((8, width), 0)
    wide_valid = geometry[0:8, :] >= 0.0
    component = (sub >= 1) & (sub <= 3) & wide_valid
    floor_of = geometry[8:16, :]
    roof_of = geometry[16:24, :]
    pull = time_step * jnp.where(sub == 1, gravity_x, jnp.where(sub == 3, gravity_z, 0.0))
    plane_total = 4 * device_total
    motions = []
    for a in range(6):
        sums = own[8 * a : 8 * a + 8, :]
        if a < 2:
            sums = sums + left[8 * a : 8 * a + 8]
        if a >= 4:
            sums = sums + right[8 * a - 32 : 8 * a - 24]
        plane = 4 * device + a
        node_mass = jnp.maximum(jnp.broadcast_to(sums[0:1, :], (8, width)), mass_floor)
        per_step = pltpu.roll(sums, 5, 0)
        motion = (sums - time_step * per_step) / node_mass + pull
        lowest = jnp.where(plane < 2, 0.0, -BIG)
        highest = jnp.where(plane >= plane_total - 2, 0.0, BIG)
        motion = jnp.maximum(motion, jnp.where(sub == 1, lowest, floor_of))
        motion = jnp.minimum(motion, jnp.where(sub == 1, highest, roof_of))
        inside = jnp.where(plane < plane_total, 1, 0)
        motion = jnp.where(component & (inside > 0), motion, 0.0)
        motions.append(motion)
    paired = jnp.concatenate(
        [motions[2 * g] + pltpu.roll(motions[2 * g + 1], 4, 0) for g in range(3)], axis=0
    )

    span = 8 * rows
    blocks = []
    for b in range(bins):
        begin = (b * SLOT) // LANES * LANES
        block = paired[:, begin : begin + LANES]
        if b * SLOT > begin:
            block = pltpu.roll(block, LANES - (b * SLOT - begin), 1)
        block = block[:, 0:TILE]
        high = block.astype(BF16)
        kept = high.astype(F32)
        blocks.append((jnp.concatenate([kept, block - kept], axis=0).astype(BF16), high))

    def gather(kinds):
        for b in range(bins):
            stacked, high = blocks[b]
            count = high.shape[0]
            for first_quarter, wide, lanes in halves(quarters):
                row = b * quarters + first_quarter
                even = iota((8, wide * LANES), 0) < 4

                def pair_weights_of(begin):
                    return [
                        jnp.where(
                            even,
                            spread(along, rows * (begin + 2 * g) + row, wide),
                            spread(along, rows * (begin + 2 * g + 1) + row, wide),
                        )
                        for g in range(3)
                    ]

                weights = pair_weights_of(0)
                for kind in kinds:
                    right_high = highs[b, pl.ds(kind * TILE, TILE), lanes]
                    right_low = lows[b, pl.ds(kind * TILE, TILE), lanes]
                    product = dot_nn(stacked, right_high)
                    product = product[0:count] + product[count : 2 * count]
                    product = product + dot_nn(high, right_low)
                    groups = [product[8 * g : 8 * g + 8] for g in range(3)]
                    sums = [(kind, sum(w * group for w, group in zip(weights, groups)))]
                    if kind == 0:
                        moved = zip(pair_weights_of(6), groups)
                        sums.append((3, sum(w * group for w, group in moved)))
                    for target, value in sums:
                        for q in range(wide):
                            place = target * span + 8 * (row + q)
                            shuffle[pl.ds(place, 8), :] = value[:, LANES * q : LANES * (q + 1)]

    def take(kind, c):
        return (
            shuffle[pl.ds(kind * span + 1 + c, rows, stride=8), :]
            + shuffle[pl.ds(kind * span + 5 + c, rows, stride=8), :]
        )

    gather((0, 1, 2) if live is None else (0,))
    started([take(0, c) for c in range(3)])

    def rest():
        if live is not None:
            gather((1, 2))
        velocity = [take(0, c) for c in range(3)]
        affine = [None] * 9
        for c in range(3):
            affine[3 * c] = 4.0 * take(3, c)
            affine[3 * c + 1] = 4.0 * take(1, c)
            affine[3 * c + 2] = 4.0 * take(2, c)
        old = state[DEF : DEF + 9]
        deform = []
        for r in range(3):
            for c in range(3):
                change = (
                    affine[3 * r] * old[c]
                    + affine[3 * r + 1] * old[3 + c]
                    + affine[3 * r + 2] * old[6 + c]
                )
                deform.append(old[3 * r + c] + time_step * change)
        steps = [time_step * velocity[c] for c in range(3)]
        moved = [state[c] + steps[c] for c in range(3)]
        travelled = [state[TRAV + c] + steps[c] for c in range(3)]
        finish(moved + deform + [state[MASS], state[VOL]] + travelled, velocity, affine)

    if live is None:
        rest()
    else:
        pl.when(live[0] >= 0)(rest)


def read_state(ref, rows):
    return [ref[pl.ds(rows * number, rows), :] for number in range(ROWS)]


def write_state(ref, state):
    rows = state[0].shape[0]
    for number in range(ROWS):
        ref[pl.ds(rows * number, rows), :] = state[number]


def rows_of(begin, count, s, rows):
    if count == 1:
        return pl.ds(rows * begin + s, 1)
    return pl.ds(rows * begin + s, count, stride=rows)


def block_row(blocks, bins, width):
    lane = iota((1, width), 1)
    meta = jnp.zeros((1, width), F32)
    for b in range(bins):
        meta = jnp.where(lane == LANES + META + b, blocks[b].astype(F32), meta)
    return meta


def first_kernel(
    bins, device_total, live, device, blocks_in, x_in, v_in, f_in, c_in, m_in, vol_in,
    state_ref, motion_ref, speeds, meta, outbox, sem, blocks, x_ref, v_ref, f_ref, c_ref, m_ref,
    vol_ref, arrivals,
):
    rows = state_ref.shape[0] // ROWS
    quarters = rows // bins
    half = rows * LANES
    copies = []
    moves = (
        (v_in.at[:, pl.ds(0, half)], v_ref),
        (m_in.at[pl.ds(0, half)], m_ref),
        (blocks_in, blocks),
        (x_in.at[:, pl.ds(0, half)], x_ref),
        (f_in.at[:, pl.ds(0, half)], f_ref),
        (c_in.at[:, pl.ds(0, half)], c_ref),
        (vol_in.at[pl.ds(0, half)], vol_ref),
    )
    for number, (source, target) in enumerate(moves):
        copies.append(pltpu.make_async_copy(source, target, arrivals.at[number]))
        copies[number].start()
    copies[0].wait()
    copies[1].wait()

    def relay(ref, count, kept, begin):
        for s in range(rows):
            for start in range(0, count, 8):
                size = min(8, count - start)
                source = ref[pl.ds(start, size), pl.ds(LANES * s, LANES)]
                kept[rows_of(begin + start, size, s, rows), :] = source

    def relay_flat(ref, number):
        for b in range(bins):
            alive = jnp.where(b < live[0], 1.0, 0.0)
            for q in range(quarters):
                s = quarters * b + q
                piece = ref[pl.ds(LANES * s, LANES)].reshape(1, LANES)
                state_ref[pl.ds(rows * number + s, 1), :] = piece * alive

    fastest = jnp.zeros((1, LANES), F32)
    for b in range(bins):
        for s in range(quarters * b, quarters * (b + 1)):
            part = v_ref[:, pl.ds(LANES * s, LANES)]
            speed = jnp.sum(part * part, axis=0, keepdims=True)
            mass = m_ref[pl.ds(LANES * s, LANES)].reshape(1, LANES)
            counted = (mass > 0.0) & (b < live[0])
            fastest = jnp.maximum(fastest, jnp.where(counted, speed, 0.0))
    outbox[...] = jnp.broadcast_to(jnp.max(fastest, axis=1, keepdims=True), outbox.shape)
    pltpu.make_async_copy(outbox, speeds, sem).start()

    @pl.when(live[0] >= 0)
    def _():
        for copy in copies[2:]:
            copy.wait()
        relay(v_ref, 3, motion_ref, 0)
        relay_flat(m_ref, MASS)
        relay(x_ref, 3, state_ref, POS)
        relay(f_ref, 9, state_ref, DEF)
        relay(c_ref, 9, motion_ref, 3)
        relay_flat(vol_ref, VOL)
        home = jnp.zeros((rows, LANES), F32)
        home_y, home_z = home, home
        row_bin = iota((rows, LANES), 0) // quarters
        for b in range(bins):
            block = blocks[b]
            block_y = block // BZ
            block_z = block - BZ * block_y
            home_y = jnp.where(row_bin == b, (4 * block_y).astype(F32), home_y)
            home_z = jnp.where(row_bin == b, (4 * block_z).astype(F32), home_z)
        anchors = (home + (4 * device).astype(F32), home_y, home_z)
        for axis in range(3):
            place = pl.ds(rows * axis, rows)
            state_ref[place, :] = state_ref[place, :] - anchors[axis]
            state_ref[pl.ds(rows * (TRAV + axis), rows), :] = home
        meta[...] = jnp.broadcast_to(block_row(blocks, bins, meta.shape[1]), meta.shape)

    pltpu.make_async_copy(outbox, speeds, sem).wait()


def scatter_kernel(
    bins, device_total, live, device, state_ref, motion_ref, meta, far, highs, lows, along,
    channels, across,
):
    rows = state_ref.shape[0] // ROWS
    motion = [motion_ref[pl.ds(rows * number, rows), :] for number in range(12)]
    to_grid(
        read_state(state_ref, rows), motion[0:3], motion[3:12], state_ref, device, bins, meta, far,
        highs, lows, along, channels, across,
    )


def place_own(own, low, middle, high, selector):
    own[0:16, :] = placed(low, selector)
    own[16:32, :] = placed(jnp.concatenate(middle, axis=1), selector)
    own[32:48, :] = placed(high, selector)


def first_rest_kernel(
    bins, device_total, live, device, meta, far, highs, lows, along, channels,
    near, own, geometry, home,
):
    low, middle, high = rest_of_grid(
        device, bins, meta, far, highs, lows, along, channels, near
    )
    width = bins * SLOT
    position = iota((1, width), 1)
    column_bin = position // SLOT
    column_node = position - SLOT * column_bin
    column_valid = (column_node < TILE) & (column_node % 8 < 6)
    own_blocks = block_numbers(meta[0:1, :], bins)
    column_block = jnp.zeros((1, width), F32)
    for b in range(bins):
        column_block = jnp.where(column_bin == b, own_blocks[b], column_block)
    column_y, column_z = node_key(column_block, column_node.astype(F32))
    column_key = jnp.where(column_valid, LANES * column_y + column_z, -1.0)
    selector = placing(own_blocks, column_key, bins)
    home[...] = selector
    place_own(own, low, middle, high, selector)
    sub = iota((8, width), 0)
    wide_y = jnp.broadcast_to(column_y, (8, width))
    wide_z = jnp.broadcast_to(column_z, (8, width))
    geometry[0:8, :] = jnp.broadcast_to(column_key, (8, width))
    geometry[8:16, :] = jnp.where(
        ((sub == 2) & (wide_y < 2.0)) | ((sub == 3) & (wide_z < 2.0)), 0.0, -BIG
    )
    geometry[16:24, :] = jnp.where(
        ((sub == 2) & (wide_y >= NGY - 2.0)) | ((sub == 3) & (wide_z >= NGZ - 2.0)), 0.0, BIG
    )


def rest_kernel(
    bins, device_total, live, device, meta, far, highs, lows, along, channels, home, near, own
):
    low, middle, high = rest_of_grid(
        device, bins, meta, far, highs, lows, along, channels, near
    )
    place_own(own, low, middle, high, home[...])


def second_kernel(
    bins, device_total, live, device, old_ref, speeds, own, geometry, highs, lows, along,
    near, outer, inner, state_ref, motion_ref, new_speeds, sides_ref, shuffle, outbox, sem,
):
    around = halos(near, outer, inner, device, device_total)
    key = geometry[0:1, :]
    sides = [placing(block_numbers(block[7:8, :], bins), key, bins) for block in around]
    for side in range(2):
        sides_ref[side] = sides[side]
    advance(
        live, bins, device_total, device, old_ref, speeds, own, geometry, highs, lows, along, around,
        sides, state_ref, motion_ref, new_speeds, shuffle, outbox, sem,
    )


def later_kernel(
    bins, device_total, live, device, old_ref, speeds, own, geometry, highs, lows, along,
    near, outer, inner, sides_ref, state_ref, motion_ref, new_speeds, shuffle, outbox, sem,
):
    around = halos(near, outer, inner, device, device_total)
    sides = [sides_ref[0], sides_ref[1]]
    advance(
        live, bins, device_total, device, old_ref, speeds, own, geometry, highs, lows, along, around,
        sides, state_ref, motion_ref, new_speeds, shuffle, outbox, sem,
    )


def advance(
    live, bins, device_total, device, old_ref, speeds, own, geometry, highs, lows, along, around,
    sides, state_ref, motion_ref, new_speeds, shuffle, outbox, sem,
):
    rows = state_ref.shape[0] // ROWS

    def started(velocity):
        send_speed(velocity, old_ref[pl.ds(rows * MASS, rows), :], new_speeds, outbox, sem)

    def finish(state, velocity, affine):
        write_state(state_ref, state)
        for number, value in enumerate(velocity + affine):
            motion_ref[pl.ds(rows * number, rows), :] = value

    to_particles(
        live, old_ref, device, bins, device_total, geometry, own, sides, speeds, around, highs,
        lows, along, shuffle, started, finish,
    )
    pltpu.make_async_copy(outbox, new_speeds, sem).wait()


def last_kernel(
    bins, device_total, live, device, old_ref, speeds, own, geometry, highs, lows, along,
    near, outer, inner, sides_ref, d_out, v_out, f_out, c_out, shuffle, d_rows,
    v_rows, f_rows, c_rows,
):
    rows = old_ref.shape[0] // ROWS
    quarters = rows // bins
    row_bin = iota((rows, LANES), 0) // quarters
    alive = row_bin < live[0]
    half = rows * LANES

    def finish(state, velocity, affine):
        results = (
            (d_out, state[TRAV : TRAV + 3], d_rows),
            (v_out, velocity, v_rows),
            (f_out, state[DEF : DEF + 9], f_rows),
            (c_out, affine, c_rows),
        )
        for ref, values, finished in results:
            count = len(values)
            for number in range(count):
                finished[pl.ds(rows * number, rows), :] = jnp.where(alive, values[number], 0.0)
            for s in range(rows):
                for start in range(0, count, 8):
                    size = min(8, count - start)
                    value = finished[rows_of(start, size, s, rows), :]
                    ref[pl.ds(start, size), pl.ds(LANES * s, LANES)] = value
            total = ref.shape[1]
            ref[:, pl.ds(half, total - half)] = jnp.zeros((count, total - half), F32)

    to_particles(
        None, old_ref, device, bins, device_total, geometry, own, [sides_ref[0], sides_ref[1]], speeds,
        halos(near, outer, inner, device, device_total), highs, lows, along, shuffle,
        lambda velocity: None, finish,
    )


def local(positions, velocity, deformation, affine, particle_mass, volume, bin_block, live_count):
    slot_total = bin_block.shape[0]
    per_bin = positions.shape[1] // slot_total
    bins = slot_total // 2
    device_total = lax.axis_size("space")
    rows = bins * per_bin // LANES
    half = rows * LANES
    nodes = bins * TILE
    width = bins * SLOT
    message = ((16, -(-(nodes + LANES // 2) // LANES) * LANES), F32)
    speeds_shape = ((device_total, LANES), F32)
    held = [((ROWS * rows, LANES), F32), ((12 * rows, LANES), F32), speeds_shape]
    grid_held = [
        message,
        ((bins, 3 * TILE, per_bin), BF16),
        ((bins, 3 * TILE, per_bin), BF16),
        ((12 * rows, LANES), F32),
        ((4 * 8 * rows, LANES), F32),
    ]
    meta_shape = ((8, message[0][1]), F32)
    own_shape = ((48, width), F32)
    geometry_shape = ((24, width), F32)
    home_shape = ((nodes, width), BF16)
    sides_shape = ((2, nodes, width), BF16)
    smem = pl.BlockSpec(memory_space=pltpu.SMEM)
    vmem = pl.BlockSpec(memory_space=pltpu.VMEM)
    anywhere = pl.BlockSpec(memory_space=pl.ANY)
    shuffle = pltpu.VMEM((4 * 8 * rows, LANES), F32)
    sending = [pltpu.VMEM((device_total, LANES), F32), pltpu.SemaphoreType.DMA]
    me = lax.axis_index("space").astype(jnp.int32).reshape(1)

    def stay(array, space=pltpu.VMEM):
        return array if INTERPRET else pltpu.with_memory_space_constraint(array, space)

    def call(body, scalars, arguments, outputs, scratch, in_specs=None, final=False):
        def kernel(*refs):
            count = len(scalars)
            body(bins, device_total, *refs[: count - 1], refs[count - 1][0], *refs[count:])

        out_specs = tuple(anywhere if output == speeds_shape else vmem for output in outputs)
        if in_specs is None:
            in_specs = [vmem] * len(arguments)
            arguments = [stay(argument) for argument in arguments]
        else:
            arguments = [stay(argument, pltpu.HBM) for argument in arguments]
        make = jax.ShapeDtypeStruct if final or INTERPRET else pltpu.VMEM
        return pl.pallas_call(
            kernel,
            in_specs=[smem] * len(scalars) + in_specs,
            out_shape=tuple(
                pltpu.HBM(*output) if output == speeds_shape and not INTERPRET else make(*output)
                for output in outputs
            ),
            out_specs=out_specs,
            scratch_shapes=scratch,
            interpret=INTERPRET,
            compiler_params=pltpu.CompilerParams(vmem_limit_bytes=GRANT),
        )(*scalars, *arguments)

    length = device_total
    swap_pairs = [(i, i ^ 1) for i in range(length)]
    inner_pairs = [(i, i ^ 3) for i in range(length)]
    outer_pairs = [(i, i + 1) for i in range(3, length - 1, 4)]
    outer_pairs = outer_pairs + [(i, i + 3) for i in range(2, length - 3, 4)]
    outer_pairs = outer_pairs + [(0, 1), (length - 2, length - 1)]
    outer_pairs = outer_pairs + [(j, i) for i, j in outer_pairs]

    slot_rows = [pltpu.VMEM((count, half), F32) for count in (3, 3, 9, 9)]
    *results, meta = call(
        first_kernel,
        (live_count, me),
        (bin_block, positions, velocity, deformation, affine, particle_mass, volume),
        [*held, meta_shape],
        sending
        + [pltpu.SMEM((slot_total,), jnp.int32)]
        + slot_rows
        + [pltpu.VMEM((half,), F32), pltpu.VMEM((half,), F32), pltpu.SemaphoreType.DMA((7,))],
        [anywhere] * 7,
    )
    sides = ()
    for step in range(STEPS):
        state, motion, speeds = results[:3]
        sides = sides + tuple(results[3:])
        speeds = lax.all_to_all(speeds, "space", 0, 0, tiled=True)
        far, highs, lows, along, channels = call(
            scatter_kernel,
            (live_count, me),
            (state, motion, meta),
            grid_held,
            [pltpu.VMEM((12 * rows, LANES), F32)],
        )
        from_outer = lax.ppermute(far, "space", outer_pairs)
        from_inner = lax.ppermute(far, "space", inner_pairs)
        arguments = (meta, far, highs, lows, along, channels)
        if step == 0:
            near, own, geometry, home = call(
                first_rest_kernel,
                (live_count, me),
                arguments,
                [message, own_shape, geometry_shape, home_shape],
                [],
            )
        else:
            near, own = call(
                rest_kernel, (live_count, me), arguments + (home,), [message, own_shape], []
            )
        from_near = lax.ppermute(near, "space", swap_pairs)
        arguments = (
            state, speeds, own, geometry, highs, lows, along, from_near, from_outer, from_inner,
            *sides,
        )
        if step < STEPS - 1:
            results = call(
                second_kernel if step == 0 else later_kernel,
                (live_count, me),
                arguments,
                held + ([sides_shape] if step == 0 else []),
                [shuffle] + sending,
            )
    total = positions.shape[1]
    return call(
        last_kernel,
        (live_count, me),
        arguments,
        [((count, total), F32) for count in (3, 3, 9, 9)],
        [shuffle] + [pltpu.VMEM((count * rows, LANES), F32) for count in (3, 3, 9, 9)],
        final=True,
    )


def solution(mesh):
    in_specs = (
        P(None, "space"),
        P(None, "space"),
        P(None, "space"),
        P(None, "space"),
        P("space"),
        P("space"),
        P("space"),
        P("space"),
    )
    out_specs = (P(None, "space"), P(None, "space"), P(None, "space"), P(None, "space"))
    return jax.shard_map(local, mesh=mesh, in_specs=in_specs, out_specs=out_specs, check_vma=False)
```

```python
import jax
import jax.numpy as jnp
from jax import lax
from jax.experimental import pallas as pl
from jax.experimental.pallas import tpu as pltpu
from jax.sharding import PartitionSpec as P


BZ = 16
STEPS = 3
NGY = 66
NGZ = 66

mu_shear = 4.0
lame_first = 6.0
courant = 0.15
sound_speed = 3.7416573867739413
mass_floor = 0.05
gravity_x = 3.0
gravity_z = -9.0

LANES = 128
TILE = 48
SLOT = 64
META = 64
BIG = 3.0e38
GRANT = 8 * 2**20
F32 = jnp.float32
BF16 = jnp.bfloat16
INTERPRET = False

POS, DEF, MASS, VOL, TRAV = 0, 3, 12, 13, 14
ROWS = 17


def iota(shape, dim):
    return lax.broadcasted_iota(jnp.int32, shape, dim)


def split(value):
    high = value.astype(BF16)
    low = (value - high.astype(F32)).astype(BF16)
    return high, low


def dot_nt(a, b):
    return lax.dot_general(a, b, (((1,), (1,)), ((), ())), preferred_element_type=F32)


def dot_nn(a, b):
    return lax.dot_general(a, b, (((1,), (0,)), ((), ())), preferred_element_type=F32)


def spline(distance):
    magnitude = jnp.abs(distance)
    outer = jnp.maximum(1.5 - magnitude, 0.0)
    inner = jnp.maximum(0.5 - magnitude, 0.0)
    return 0.5 * outer * outer - 1.5 * inner * inner


def spread(ref, row, quarters):
    return jnp.concatenate(
        [ref[pl.ds(row + q, 8, stride=0), :] for q in range(quarters)], axis=1
    )


def dense_weights(position, ref):
    rows = position.shape[0]
    for a in range(6):
        offset = float(a) - position
        weight = spline(offset)
        ref[pl.ds(rows * a, rows), :] = weight
        ref[pl.ds(rows * (6 + a), rows), :] = weight * offset


def pair_weights(state_ref, across, row, span):
    rows = across.shape[0] // 12
    along_z = spread(state_ref, 2 * rows + row, span)
    third_node = iota(along_z.shape, 0)
    third_offset = third_node.astype(F32) - along_z
    third = jnp.where(third_node < 6, spline(third_offset), 0.0)
    third_moved = third * third_offset
    plain, moved_y, moved_z = [], [], []
    for a in range(6):
        second = spread(across, rows * a + row, span)
        second_moved = spread(across, rows * (6 + a) + row, span)
        plain.append(second * third)
        moved_y.append(second_moved * third)
        moved_z.append(second * third_moved)
    return [jnp.concatenate(part, axis=0) for part in (plain, moved_y, moved_z)]


def kirchhoff(deform):
    determinant = (
        deform[0] * (deform[4] * deform[8] - deform[5] * deform[7])
        - deform[1] * (deform[3] * deform[8] - deform[5] * deform[6])
        + deform[2] * (deform[3] * deform[7] - deform[4] * deform[6])
    )
    pressure = lame_first * (determinant - 1.0) * determinant
    stress = [None] * 9
    for r in range(3):
        for c in range(r, 3):
            product = (
                deform[3 * r] * deform[3 * c]
                + deform[3 * r + 1] * deform[3 * c + 1]
                + deform[3 * r + 2] * deform[3 * c + 2]
            )
            if r == c:
                stress[3 * r + c] = mu_shear * (product - 1.0) + pressure
            else:
                stress[3 * r + c] = mu_shear * product
                stress[3 * c + r] = stress[3 * r + c]
    return stress


def send_speed(velocity, mass, speeds, outbox, sem):
    speed = velocity[0] * velocity[0] + velocity[1] * velocity[1] + velocity[2] * velocity[2]
    speed = jnp.max(jnp.where(mass > 0.0, speed, 0.0), axis=0, keepdims=True)
    speed = jnp.max(speed, axis=1, keepdims=True)
    outbox[...] = jnp.broadcast_to(speed, outbox.shape)
    pltpu.make_async_copy(outbox, speeds, sem).start()


def halves(quarters):
    parts = 2 if quarters % 2 == 0 else 1
    span = quarters // parts
    return [(part * span, span, pl.ds(part * span * LANES, span * LANES)) for part in range(parts)]


def plane_sums(planes, row, span, channels, along, tables):
    rows = along.shape[0] // 12

    def channel(matrix):
        begin = 8 * (matrix * rows + row)
        return jnp.concatenate(
            [channels[pl.ds(begin + 8 * q, 8), :] for q in range(span)], axis=1
        )

    base, slope_x, slope_y, slope_z = [channel(matrix) for matrix in range(4)]
    pieces = ([], [], [])
    for a in planes:
        first = spread(along, rows * a + row, span)
        first_moved = spread(along, rows * (6 + a) + row, span)
        pieces[0].append(first * base + first_moved * slope_x)
        pieces[1].append(first * slope_y)
        pieces[2].append(first * slope_z)
    count = 8 * len(planes)
    total = None
    for piece, (right_high, right_low) in zip(pieces, tables):
        left_high, left_low = split(jnp.concatenate(piece, axis=0))
        both = dot_nt(jnp.concatenate([left_high, left_low], axis=0), right_high)
        product = both[0:count] + both[count : 2 * count] + dot_nt(left_high, right_low)
        total = product if total is None else total + product
    return total


def far_planes(device):
    return 4 * (device % 2)


def to_grid(
    state, velocity, affine, state_ref, device, bins, meta, far, highs, lows, along, channels, across
):
    rows = state[0].shape[0]
    quarters = rows // bins
    deform = state[DEF : DEF + 9]
    mass, volume = state[MASS], state[VOL]
    stress = kirchhoff(deform)
    scaled = 4.0 * volume
    span = 8 * rows
    zero = jnp.zeros((rows, LANES), F32)

    def put(matrix, row, value):
        channels[pl.ds(matrix * span + row, rows, stride=8), :] = value

    put(0, 0, mass)
    for c in range(3):
        put(0, 1 + c, mass * velocity[c])
        put(0, 4 + c, zero)
    put(0, 7, zero)
    for axis in range(3):
        put(1 + axis, 0, zero)
        put(1 + axis, 7, zero)
        for c in range(3):
            put(1 + axis, 1 + c, mass * affine[3 * c + axis])
            put(1 + axis, 4 + c, scaled * stress[3 * c + axis])
    dense_weights(state[0], along)
    dense_weights(state[1], across)
    base = far_planes(device)
    for b in range(bins):
        total = None
        for begin, width, lanes in halves(quarters):
            row = b * quarters + begin
            tables = []
            for kind, values in enumerate(pair_weights(state_ref, across, row, width)):
                high, low = split(values)
                highs[b, pl.ds(kind * TILE, TILE), lanes] = high
                lows[b, pl.ds(kind * TILE, TILE), lanes] = low
                tables.append((high, low))
            sums = plane_sums((base, base + 1), row, width, channels, along, tables)
            total = sums if total is None else total + sums
        far[:, TILE * b : TILE * (b + 1)] = total
    nodes = bins * TILE
    width = far.shape[1]
    far[:, nodes:width] = jnp.broadcast_to(meta[0:1, nodes:width], (16, width - nodes))


def rest_of_grid(device, bins, meta, far, highs, lows, along, channels, near):
    rows = along.shape[0] // 12
    quarters = rows // bins
    odd = device % 2 == 1
    base = 4 - far_planes(device)
    middle = []
    for b in range(bins):
        total = None
        for begin, width, lanes in halves(quarters):
            row = b * quarters + begin
            tables = [
                (highs[b, pl.ds(kind * TILE, TILE), lanes], lows[b, pl.ds(kind * TILE, TILE), lanes])
                for kind in range(3)
            ]
            sums = plane_sums((base, base + 1, 2, 3), row, width, channels, along, tables)
            total = sums if total is None else total + sums
        near[:, TILE * b : TILE * (b + 1)] = total[0:16]
        middle.append(total[16:32])
    nodes = bins * TILE
    width = near.shape[1]
    near[:, nodes:width] = jnp.broadcast_to(meta[0:1, nodes:width], (16, width - nodes))
    near_part, far_part = near[:, 0:nodes], far[:, 0:nodes]
    low = jnp.where(odd, near_part, far_part)
    high = jnp.where(odd, far_part, near_part)
    return low, middle, high


def node_key(block, node):
    block_y = jnp.floor((block + 0.5) * (1.0 / BZ))
    block_z = block - BZ * block_y
    node_y = jnp.floor((node + 0.5) * (1.0 / 8.0))
    node_z = node - 8.0 * node_y
    return 4.0 * block_y + node_y, 4.0 * block_z + node_z


def placing(source_block, column_key, bins):
    nodes = bins * TILE
    source = iota((nodes, 1), 0).astype(F32)
    source_bin = jnp.floor((source + 0.5) * (1.0 / TILE))
    source_node = source - TILE * source_bin
    block = jnp.zeros((nodes, 1), F32)
    for b in range(bins):
        block = jnp.where(source_bin == float(b), source_block[b], block)
    row_y, row_z = node_key(block, source_node)
    row_key = LANES * row_y + row_z
    used = source_node - 8.0 * jnp.floor((source_node + 0.5) * (1.0 / 8.0)) < 6.0
    row_key = jnp.where(used, row_key, -2.0)
    return jnp.where(row_key == column_key, 1.0, 0.0).astype(BF16)


def placed(values, selector):
    count = values.shape[0]
    high, low = split(values)
    result = dot_nn(jnp.concatenate([high, low], axis=0), selector)
    return result[0:count] + result[count : 2 * count]


def halos(near, outer, inner, device, device_total):
    odd = device % 2 == 1
    middle = (device + 1) % 4 >= 2
    near_block = near[...]
    far_block = jnp.where(middle, inner[...], outer[...])
    left_block = jnp.where(odd, near_block, far_block)
    right_block = jnp.where(odd, far_block, near_block)
    left_block = jnp.where(device > 0, left_block, 0.0)
    right_block = jnp.where(device + 1 < device_total, right_block, 0.0)
    return left_block, right_block


def block_numbers(row, bins):
    lane = iota((1, LANES), 1)
    return [
        jnp.max(jnp.where(lane == META + b, row[:, LANES : 2 * LANES], 0.0), axis=1, keepdims=True)
        for b in range(bins)
    ]


def to_particles(
    live, old_ref, device, bins, device_total, geometry, own, sides, speeds, blocks_around,
    highs, lows, along, shuffle, started, finish,
):
    rows = old_ref.shape[0] // ROWS
    quarters = rows // bins
    state = read_state(old_ref, rows)
    width = bins * SLOT
    nodes = bins * TILE
    fastest = jnp.max(speeds[...], axis=0, keepdims=True)
    fastest = jnp.max(fastest, axis=1, keepdims=True)
    time_step = courant / (jnp.sqrt(fastest) + sound_speed)

    around = []
    for side, block in enumerate(blocks_around):
        around.append(placed(block[:, 0:nodes], sides[side]))
    left, right = around

    sub = iota((8, width), 0)
    wide_valid = geometry[0:8, :] >= 0.0
    component = (sub >= 1) & (sub <= 3) & wide_valid
    floor_of = geometry[8:16, :]
    roof_of = geometry[16:24, :]
    pull = time_step * jnp.where(sub == 1, gravity_x, jnp.where(sub == 3, gravity_z, 0.0))
    plane_total = 4 * device_total
    motions = []
    for a in range(6):
        sums = own[8 * a : 8 * a + 8, :]
        if a < 2:
            sums = sums + left[8 * a : 8 * a + 8]
        if a >= 4:
            sums = sums + right[8 * a - 32 : 8 * a - 24]
        plane = 4 * device + a
        node_mass = jnp.maximum(jnp.broadcast_to(sums[0:1, :], (8, width)), mass_floor)
        per_step = pltpu.roll(sums, 5, 0)
        motion = (sums - time_step * per_step) / node_mass + pull
        lowest = jnp.where(plane < 2, 0.0, -BIG)
        highest = jnp.where(plane >= plane_total - 2, 0.0, BIG)
        motion = jnp.maximum(motion, jnp.where(sub == 1, lowest, floor_of))
        motion = jnp.minimum(motion, jnp.where(sub == 1, highest, roof_of))
        inside = jnp.where(plane < plane_total, 1, 0)
        motion = jnp.where(component & (inside > 0), motion, 0.0)
        motions.append(motion)
    paired = jnp.concatenate(
        [motions[2 * g] + pltpu.roll(motions[2 * g + 1], 4, 0) for g in range(3)], axis=0
    )

    span = 8 * rows
    blocks = []
    for b in range(bins):
        begin = (b * SLOT) // LANES * LANES
        block = paired[:, begin : begin + LANES]
        if b * SLOT > begin:
            block = pltpu.roll(block, LANES - (b * SLOT - begin), 1)
        block = block[:, 0:TILE]
        high = block.astype(BF16)
        kept = high.astype(F32)
        blocks.append((jnp.concatenate([kept, block - kept], axis=0).astype(BF16), high))

    def gather(kinds):
        for b in range(bins):
            stacked, high = blocks[b]
            count = high.shape[0]
            for first_quarter, wide, lanes in halves(quarters):
                row = b * quarters + first_quarter
                even = iota((8, wide * LANES), 0) < 4

                def pair_weights_of(begin):
                    return [
                        jnp.where(
                            even,
                            spread(along, rows * (begin + 2 * g) + row, wide),
                            spread(along, rows * (begin + 2 * g + 1) + row, wide),
                        )
                        for g in range(3)
                    ]

                weights = pair_weights_of(0)
                for kind in kinds:
                    right_high = highs[b, pl.ds(kind * TILE, TILE), lanes]
                    right_low = lows[b, pl.ds(kind * TILE, TILE), lanes]
                    product = dot_nn(stacked, right_high)
                    product = product[0:count] + product[count : 2 * count]
                    product = product + dot_nn(high, right_low)
                    groups = [product[8 * g : 8 * g + 8] for g in range(3)]
                    sums = [(kind, sum(w * group for w, group in zip(weights, groups)))]
                    if kind == 0:
                        moved = zip(pair_weights_of(6), groups)
                        sums.append((3, sum(w * group for w, group in moved)))
                    for target, value in sums:
                        for q in range(wide):
                            place = target * span + 8 * (row + q)
                            shuffle[pl.ds(place, 8), :] = value[:, LANES * q : LANES * (q + 1)]

    def take(kind, c):
        return (
            shuffle[pl.ds(kind * span + 1 + c, rows, stride=8), :]
            + shuffle[pl.ds(kind * span + 5 + c, rows, stride=8), :]
        )

    gather((0, 1, 2) if live is None else (0,))
    started([take(0, c) for c in range(3)])

    def rest():
        if live is not None:
            gather((1, 2))
        velocity = [take(0, c) for c in range(3)]
        affine = [None] * 9
        for c in range(3):
            affine[3 * c] = 4.0 * take(3, c)
            affine[3 * c + 1] = 4.0 * take(1, c)
            affine[3 * c + 2] = 4.0 * take(2, c)
        old = state[DEF : DEF + 9]
        deform = []
        for r in range(3):
            for c in range(3):
                change = (
                    affine[3 * r] * old[c]
                    + affine[3 * r + 1] * old[3 + c]
                    + affine[3 * r + 2] * old[6 + c]
                )
                deform.append(old[3 * r + c] + time_step * change)
        steps = [time_step * velocity[c] for c in range(3)]
        moved = [state[c] + steps[c] for c in range(3)]
        travelled = [state[TRAV + c] + steps[c] for c in range(3)]
        finish(moved + deform + [state[MASS], state[VOL]] + travelled, velocity, affine)

    if live is None:
        rest()
    else:
        pl.when(live[0] >= 0)(rest)


def read_state(ref, rows):
    return [ref[pl.ds(rows * number, rows), :] for number in range(ROWS)]


def write_state(ref, state):
    rows = state[0].shape[0]
    for number in range(ROWS):
        ref[pl.ds(rows * number, rows), :] = state[number]


def rows_of(begin, count, s, rows):
    if count == 1:
        return pl.ds(rows * begin + s, 1)
    return pl.ds(rows * begin + s, count, stride=rows)


def block_row(blocks, bins, width):
    lane = iota((1, width), 1)
    meta = jnp.zeros((1, width), F32)
    for b in range(bins):
        meta = jnp.where(lane == LANES + META + b, blocks[b].astype(F32), meta)
    return meta


def first_kernel(
    bins, device_total, live, device, blocks_in, x_in, v_in, f_in, c_in, m_in, vol_in,
    state_ref, motion_ref, speeds, meta, outbox, sem, blocks, x_ref, v_ref, f_ref, c_ref, m_ref,
    vol_ref, arrivals,
):
    rows = state_ref.shape[0] // ROWS
    quarters = rows // bins
    half = rows * LANES
    copies = []
    moves = (
        (v_in.at[:, pl.ds(0, half)], v_ref),
        (m_in.at[pl.ds(0, half)], m_ref),
        (blocks_in, blocks),
        (x_in.at[:, pl.ds(0, half)], x_ref),
        (f_in.at[:, pl.ds(0, half)], f_ref),
        (c_in.at[:, pl.ds(0, half)], c_ref),
        (vol_in.at[pl.ds(0, half)], vol_ref),
    )
    for number, (source, target) in enumerate(moves):
        copies.append(pltpu.make_async_copy(source, target, arrivals.at[number]))
        copies[number].start()
    copies[0].wait()
    copies[1].wait()

    def relay(ref, count, kept, begin):
        for s in range(rows):
            for start in range(0, count, 8):
                size = min(8, count - start)
                source = ref[pl.ds(start, size), pl.ds(LANES * s, LANES)]
                kept[rows_of(begin + start, size, s, rows), :] = source

    def relay_flat(ref, number):
        for b in range(bins):
            alive = jnp.where(b < live[0], 1.0, 0.0)
            for q in range(quarters):
                s = quarters * b + q
                piece = ref[pl.ds(LANES * s, LANES)].reshape(1, LANES)
                state_ref[pl.ds(rows * number + s, 1), :] = piece * alive

    fastest = jnp.zeros((1, LANES), F32)
    for b in range(bins):
        for s in range(quarters * b, quarters * (b + 1)):
            part = v_ref[:, pl.ds(LANES * s, LANES)]
            speed = jnp.sum(part * part, axis=0, keepdims=True)
            mass = m_ref[pl.ds(LANES * s, LANES)].reshape(1, LANES)
            counted = (mass > 0.0) & (b < live[0])
            fastest = jnp.maximum(fastest, jnp.where(counted, speed, 0.0))
    outbox[...] = jnp.broadcast_to(jnp.max(fastest, axis=1, keepdims=True), outbox.shape)
    pltpu.make_async_copy(outbox, speeds, sem).start()

    @pl.when(live[0] >= 0)
    def _():
        for copy in copies[2:]:
            copy.wait()
        relay(v_ref, 3, motion_ref, 0)
        relay_flat(m_ref, MASS)
        relay(x_ref, 3, state_ref, POS)
        relay(f_ref, 9, state_ref, DEF)
        relay(c_ref, 9, motion_ref, 3)
        relay_flat(vol_ref, VOL)
        home = jnp.zeros((rows, LANES), F32)
        home_y, home_z = home, home
        row_bin = iota((rows, LANES), 0) // quarters
        for b in range(bins):
            block = blocks[b]
            block_y = block // BZ
            block_z = block - BZ * block_y
            home_y = jnp.where(row_bin == b, (4 * block_y).astype(F32), home_y)
            home_z = jnp.where(row_bin == b, (4 * block_z).astype(F32), home_z)
        anchors = (home + (4 * device).astype(F32), home_y, home_z)
        for axis in range(3):
            place = pl.ds(rows * axis, rows)
            state_ref[place, :] = state_ref[place, :] - anchors[axis]
            state_ref[pl.ds(rows * (TRAV + axis), rows), :] = home
        meta[...] = jnp.broadcast_to(block_row(blocks, bins, meta.shape[1]), meta.shape)

    pltpu.make_async_copy(outbox, speeds, sem).wait()


def scatter_kernel(
    bins, device_total, live, device, state_ref, motion_ref, meta, far, highs, lows, along,
    channels, across,
):
    rows = state_ref.shape[0] // ROWS
    motion = [motion_ref[pl.ds(rows * number, rows), :] for number in range(12)]
    to_grid(
        read_state(state_ref, rows), motion[0:3], motion[3:12], state_ref, device, bins, meta, far,
        highs, lows, along, channels, across,
    )


def place_own(own, low, middle, high, selector):
    own[0:16, :] = placed(low, selector)
    own[16:32, :] = placed(jnp.concatenate(middle, axis=1), selector)
    own[32:48, :] = placed(high, selector)


def first_rest_kernel(
    bins, device_total, live, device, meta, far, highs, lows, along, channels,
    near, own, geometry, home,
):
    low, middle, high = rest_of_grid(
        device, bins, meta, far, highs, lows, along, channels, near
    )
    width = bins * SLOT
    position = iota((1, width), 1)
    column_bin = position // SLOT
    column_node = position - SLOT * column_bin
    column_valid = (column_node < TILE) & (column_node % 8 < 6)
    own_blocks = block_numbers(meta[0:1, :], bins)
    column_block = jnp.zeros((1, width), F32)
    for b in range(bins):
        column_block = jnp.where(column_bin == b, own_blocks[b], column_block)
    column_y, column_z = node_key(column_block, column_node.astype(F32))
    column_key = jnp.where(column_valid, LANES * column_y + column_z, -1.0)
    selector = placing(own_blocks, column_key, bins)
    home[...] = selector
    place_own(own, low, middle, high, selector)
    sub = iota((8, width), 0)
    wide_y = jnp.broadcast_to(column_y, (8, width))
    wide_z = jnp.broadcast_to(column_z, (8, width))
    geometry[0:8, :] = jnp.broadcast_to(column_key, (8, width))
    geometry[8:16, :] = jnp.where(
        ((sub == 2) & (wide_y < 2.0)) | ((sub == 3) & (wide_z < 2.0)), 0.0, -BIG
    )
    geometry[16:24, :] = jnp.where(
        ((sub == 2) & (wide_y >= NGY - 2.0)) | ((sub == 3) & (wide_z >= NGZ - 2.0)), 0.0, BIG
    )


def rest_kernel(
    bins, device_total, live, device, meta, far, highs, lows, along, channels, home, near, own
):
    low, middle, high = rest_of_grid(
        device, bins, meta, far, highs, lows, along, channels, near
    )
    place_own(own, low, middle, high, home[...])


def second_kernel(
    bins, device_total, live, device, meta, old_ref, speeds, own, geometry, highs, lows, along,
    near, outer, inner, state_ref, new_speeds, far, new_highs, new_lows, new_along, channels,
    sides_ref, across, outbox, sem,
):
    rows = state_ref.shape[0] // ROWS
    around = halos(near, outer, inner, device, device_total)
    key = geometry[0:1, :]
    sides = [placing(block_numbers(block[7:8, :], bins), key, bins) for block in around]
    for side in range(2):
        sides_ref[side] = sides[side]

    def started(velocity):
        send_speed(velocity, old_ref[pl.ds(rows * MASS, rows), :], new_speeds, outbox, sem)

    def finish(state, velocity, affine):
        write_state(state_ref, state)
        to_grid(
            state, velocity, affine, state_ref, device, bins, meta, far, new_highs, new_lows,
            new_along, channels, across,
        )

    to_particles(
        None, old_ref, device, bins, device_total, geometry, own, sides, speeds, around, highs,
        lows, along, channels, started, finish,
    )
    pltpu.make_async_copy(outbox, new_speeds, sem).wait()


def later_kernel(
    bins, device_total, live, device, old_ref, speeds, own, geometry, highs, lows, along,
    near, outer, inner, sides_ref, state_ref, motion_ref, new_speeds, shuffle, outbox, sem,
):
    around = halos(near, outer, inner, device, device_total)
    sides = [sides_ref[0], sides_ref[1]]
    advance(
        live, bins, device_total, device, old_ref, speeds, own, geometry, highs, lows, along, around,
        sides, state_ref, motion_ref, new_speeds, shuffle, outbox, sem,
    )


def advance(
    live, bins, device_total, device, old_ref, speeds, own, geometry, highs, lows, along, around,
    sides, state_ref, motion_ref, new_speeds, shuffle, outbox, sem,
):
    rows = state_ref.shape[0] // ROWS

    def started(velocity):
        send_speed(velocity, old_ref[pl.ds(rows * MASS, rows), :], new_speeds, outbox, sem)

    def finish(state, velocity, affine):
        write_state(state_ref, state)
        for number, value in enumerate(velocity + affine):
            motion_ref[pl.ds(rows * number, rows), :] = value

    to_particles(
        live, old_ref, device, bins, device_total, geometry, own, sides, speeds, around, highs,
        lows, along, shuffle, started, finish,
    )
    pltpu.make_async_copy(outbox, new_speeds, sem).wait()


def last_kernel(
    bins, device_total, live, device, old_ref, speeds, own, geometry, highs, lows, along,
    near, outer, inner, sides_ref, d_out, v_out, f_out, c_out, shuffle, d_rows,
    v_rows, f_rows, c_rows,
):
    rows = old_ref.shape[0] // ROWS
    quarters = rows // bins
    row_bin = iota((rows, LANES), 0) // quarters
    alive = row_bin < live[0]
    half = rows * LANES

    def finish(state, velocity, affine):
        results = (
            (d_out, state[TRAV : TRAV + 3], d_rows),
            (v_out, velocity, v_rows),
            (f_out, state[DEF : DEF + 9], f_rows),
            (c_out, affine, c_rows),
        )
        for ref, values, finished in results:
            count = len(values)
            for number in range(count):
                finished[pl.ds(rows * number, rows), :] = jnp.where(alive, values[number], 0.0)
            for s in range(rows):
                for start in range(0, count, 8):
                    size = min(8, count - start)
                    value = finished[rows_of(start, size, s, rows), :]
                    ref[pl.ds(start, size), pl.ds(LANES * s, LANES)] = value
            total = ref.shape[1]
            ref[:, pl.ds(half, total - half)] = jnp.zeros((count, total - half), F32)

    to_particles(
        None, old_ref, device, bins, device_total, geometry, own, [sides_ref[0], sides_ref[1]], speeds,
        halos(near, outer, inner, device, device_total), highs, lows, along, shuffle,
        lambda velocity: None, finish,
    )


def local(positions, velocity, deformation, affine, particle_mass, volume, bin_block, live_count):
    slot_total = bin_block.shape[0]
    per_bin = positions.shape[1] // slot_total
    bins = slot_total // 2
    device_total = lax.axis_size("space")
    rows = bins * per_bin // LANES
    half = rows * LANES
    nodes = bins * TILE
    width = bins * SLOT
    message = ((16, -(-(nodes + LANES // 2) // LANES) * LANES), F32)
    speeds_shape = ((device_total, LANES), F32)
    held = [((ROWS * rows, LANES), F32), ((12 * rows, LANES), F32), speeds_shape]
    grid_held = [
        message,
        ((bins, 3 * TILE, per_bin), BF16),
        ((bins, 3 * TILE, per_bin), BF16),
        ((12 * rows, LANES), F32),
        ((4 * 8 * rows, LANES), F32),
    ]
    meta_shape = ((8, message[0][1]), F32)
    own_shape = ((48, width), F32)
    geometry_shape = ((24, width), F32)
    home_shape = ((nodes, width), BF16)
    sides_shape = ((2, nodes, width), BF16)
    smem = pl.BlockSpec(memory_space=pltpu.SMEM)
    vmem = pl.BlockSpec(memory_space=pltpu.VMEM)
    anywhere = pl.BlockSpec(memory_space=pl.ANY)
    shuffle = pltpu.VMEM((4 * 8 * rows, LANES), F32)
    sending = [pltpu.VMEM((device_total, LANES), F32), pltpu.SemaphoreType.DMA]
    me = lax.axis_index("space").astype(jnp.int32).reshape(1)

    def stay(array, space=pltpu.VMEM):
        return array if INTERPRET else pltpu.with_memory_space_constraint(array, space)

    def call(body, scalars, arguments, outputs, scratch, in_specs=None, final=False):
        def kernel(*refs):
            count = len(scalars)
            body(bins, device_total, *refs[: count - 1], refs[count - 1][0], *refs[count:])

        out_specs = tuple(anywhere if output == speeds_shape else vmem for output in outputs)
        if in_specs is None:
            in_specs = [vmem] * len(arguments)
            arguments = [stay(argument) for argument in arguments]
        else:
            arguments = [stay(argument, pltpu.HBM) for argument in arguments]
        make = jax.ShapeDtypeStruct if final or INTERPRET else pltpu.VMEM
        return pl.pallas_call(
            kernel,
            in_specs=[smem] * len(scalars) + in_specs,
            out_shape=tuple(
                pltpu.HBM(*output) if output == speeds_shape and not INTERPRET else make(*output)
                for output in outputs
            ),
            out_specs=out_specs,
            scratch_shapes=scratch,
            interpret=INTERPRET,
            compiler_params=pltpu.CompilerParams(vmem_limit_bytes=GRANT),
        )(*scalars, *arguments)

    length = device_total
    swap_pairs = [(i, i ^ 1) for i in range(length)]
    inner_pairs = [(i, i ^ 3) for i in range(length)]
    outer_pairs = [(i, i + 1) for i in range(3, length - 1, 4)]
    outer_pairs = outer_pairs + [(i, i + 3) for i in range(2, length - 3, 4)]
    outer_pairs = outer_pairs + [(0, 1), (length - 2, length - 1)]
    outer_pairs = outer_pairs + [(j, i) for i, j in outer_pairs]

    slot_rows = [pltpu.VMEM((count, half), F32) for count in (3, 3, 9, 9)]
    *results, meta = call(
        first_kernel,
        (live_count, me),
        (bin_block, positions, velocity, deformation, affine, particle_mass, volume),
        [*held, meta_shape],
        sending
        + [pltpu.SMEM((slot_total,), jnp.int32)]
        + slot_rows
        + [pltpu.VMEM((half,), F32), pltpu.VMEM((half,), F32), pltpu.SemaphoreType.DMA((7,))],
        [anywhere] * 7,
    )
    across = pltpu.VMEM((12 * rows, LANES), F32)
    state, motion, speeds = results
    for step in range(STEPS):
        speeds = lax.all_to_all(speeds, "space", 0, 0, tiled=True)
        if step != 1:
            far, highs, lows, along, channels = call(
                scatter_kernel, (live_count, me), (state, motion, meta), grid_held, [across]
            )
        from_outer = lax.ppermute(far, "space", outer_pairs)
        from_inner = lax.ppermute(far, "space", inner_pairs)
        arguments = (meta, far, highs, lows, along, channels)
        if step == 0:
            near, own, geometry, home = call(
                first_rest_kernel,
                (live_count, me),
                arguments,
                [message, own_shape, geometry_shape, home_shape],
                [],
            )
        else:
            near, own = call(
                rest_kernel, (live_count, me), arguments + (home,), [message, own_shape], []
            )
        from_near = lax.ppermute(near, "space", swap_pairs)
        arguments = (
            state, speeds, own, geometry, highs, lows, along, from_near, from_outer, from_inner,
        )
        if step == 0:
            state, speeds, far, highs, lows, along, channels, sides = call(
                second_kernel,
                (live_count, me),
                (meta, *arguments),
                [held[0], speeds_shape, *grid_held, sides_shape],
                [across] + sending,
            )
        elif step < STEPS - 1:
            state, motion, speeds = call(
                later_kernel, (live_count, me), (*arguments, sides), held, [shuffle] + sending
            )
    total = positions.shape[1]
    return call(
        last_kernel,
        (live_count, me),
        (*arguments, sides),
        [((count, total), F32) for count in (3, 3, 9, 9)],
        [shuffle] + [pltpu.VMEM((count * rows, LANES), F32) for count in (3, 3, 9, 9)],
        final=True,
    )


def solution(mesh):
    in_specs = (
        P(None, "space"),
        P(None, "space"),
        P(None, "space"),
        P(None, "space"),
        P("space"),
        P("space"),
        P("space"),
        P("space"),
    )
    out_specs = (P(None, "space"), P(None, "space"), P(None, "space"), P(None, "space"))
    return jax.shard_map(local, mesh=mesh, in_specs=in_specs, out_specs=out_specs, check_vma=False)
```

```python
import jax
import jax.numpy as jnp
from jax import lax
from jax.experimental import pallas as pl
from jax.experimental.pallas import tpu as pltpu
from jax.sharding import PartitionSpec as P


BZ = 16
STEPS = 3
NGY = 66
NGZ = 66

mu_shear = 4.0
lame_first = 6.0
courant = 0.15
sound_speed = 3.7416573867739413
mass_floor = 0.05
gravity_x = 3.0
gravity_z = -9.0

LANES = 128
TILE = 48
SLOT = 64
META = 64
BIG = 3.0e38
GRANT = 8 * 2**20
F32 = jnp.float32
BF16 = jnp.bfloat16
INTERPRET = False

POS, DEF, MASS, VOL, TRAV = 0, 3, 12, 13, 14
ROWS = 17


def iota(shape, dim):
    return lax.broadcasted_iota(jnp.int32, shape, dim)


def split(value):
    high = value.astype(BF16)
    low = (value - high.astype(F32)).astype(BF16)
    return high, low


def dot_nt(a, b):
    return lax.dot_general(a, b, (((1,), (1,)), ((), ())), preferred_element_type=F32)


def dot_nn(a, b):
    return lax.dot_general(a, b, (((1,), (0,)), ((), ())), preferred_element_type=F32)


def spline(distance):
    magnitude = jnp.abs(distance)
    outer = jnp.maximum(1.5 - magnitude, 0.0)
    inner = jnp.maximum(0.5 - magnitude, 0.0)
    return 0.5 * outer * outer - 1.5 * inner * inner


def spread(ref, row, quarters):
    return jnp.concatenate(
        [ref[pl.ds(row + q, 8, stride=0), :] for q in range(quarters)], axis=1
    )


def dense_weights(position, ref):
    rows = position.shape[0]
    for a in range(6):
        offset = float(a) - position
        weight = spline(offset)
        ref[pl.ds(rows * a, rows), :] = weight
        ref[pl.ds(rows * (6 + a), rows), :] = weight * offset


def pair_weights(state_ref, across, row, span):
    rows = across.shape[0] // 12
    along_z = spread(state_ref, 2 * rows + row, span)
    third_node = iota(along_z.shape, 0)
    third_offset = third_node.astype(F32) - along_z
    third = jnp.where(third_node < 6, spline(third_offset), 0.0)
    third_moved = third * third_offset
    plain, moved_y, moved_z = [], [], []
    for a in range(6):
        second = spread(across, rows * a + row, span)
        second_moved = spread(across, rows * (6 + a) + row, span)
        plain.append(second * third)
        moved_y.append(second_moved * third)
        moved_z.append(second * third_moved)
    return [jnp.concatenate(part, axis=0) for part in (plain, moved_y, moved_z)]


def kirchhoff(deform):
    determinant = (
        deform[0] * (deform[4] * deform[8] - deform[5] * deform[7])
        - deform[1] * (deform[3] * deform[8] - deform[5] * deform[6])
        + deform[2] * (deform[3] * deform[7] - deform[4] * deform[6])
    )
    pressure = lame_first * (determinant - 1.0) * determinant
    stress = [None] * 9
    for r in range(3):
        for c in range(r, 3):
            product = (
                deform[3 * r] * deform[3 * c]
                + deform[3 * r + 1] * deform[3 * c + 1]
                + deform[3 * r + 2] * deform[3 * c + 2]
            )
            if r == c:
                stress[3 * r + c] = mu_shear * (product - 1.0) + pressure
            else:
                stress[3 * r + c] = mu_shear * product
                stress[3 * c + r] = stress[3 * r + c]
    return stress


def send_speed(velocity, mass, speeds, outbox, sem):
    speed = velocity[0] * velocity[0] + velocity[1] * velocity[1] + velocity[2] * velocity[2]
    speed = jnp.max(jnp.where(mass > 0.0, speed, 0.0), axis=0, keepdims=True)
    speed = jnp.max(speed, axis=1, keepdims=True)
    outbox[...] = jnp.broadcast_to(speed, outbox.shape)
    pltpu.make_async_copy(outbox, speeds, sem).start()


def halves(quarters):
    parts = 2 if quarters % 2 == 0 else 1
    span = quarters // parts
    return [(part * span, span, pl.ds(part * span * LANES, span * LANES)) for part in range(parts)]


def plane_sums(planes, row, span, channels, along, tables):
    rows = along.shape[0] // 12

    def channel(matrix):
        begin = 8 * (matrix * rows + row)
        return jnp.concatenate(
            [channels[pl.ds(begin + 8 * q, 8), :] for q in range(span)], axis=1
        )

    base, slope_x, slope_y, slope_z = [channel(matrix) for matrix in range(4)]
    pieces = ([], [], [])
    for a in planes:
        first = spread(along, rows * a + row, span)
        first_moved = spread(along, rows * (6 + a) + row, span)
        pieces[0].append(first * base + first_moved * slope_x)
        pieces[1].append(first * slope_y)
        pieces[2].append(first * slope_z)
    count = 8 * len(planes)
    total = None
    for piece, (right_high, right_low) in zip(pieces, tables):
        left_high, left_low = split(jnp.concatenate(piece, axis=0))
        both = dot_nt(jnp.concatenate([left_high, left_low], axis=0), right_high)
        product = both[0:count] + both[count : 2 * count] + dot_nt(left_high, right_low)
        total = product if total is None else total + product
    return total


def far_planes(device):
    return 4 * (device % 2)


def to_grid(
    state, velocity, affine, state_ref, device, bins, meta, far, highs, lows, along, channels, across
):
    rows = state[0].shape[0]
    quarters = rows // bins
    deform = state[DEF : DEF + 9]
    mass, volume = state[MASS], state[VOL]
    stress = kirchhoff(deform)
    scaled = 4.0 * volume
    span = 8 * rows
    zero = jnp.zeros((rows, LANES), F32)

    def put(matrix, row, value):
        channels[pl.ds(matrix * span + row, rows, stride=8), :] = value

    put(0, 0, mass)
    for c in range(3):
        put(0, 1 + c, mass * velocity[c])
        put(0, 4 + c, zero)
    put(0, 7, zero)
    for axis in range(3):
        put(1 + axis, 0, zero)
        put(1 + axis, 7, zero)
        for c in range(3):
            put(1 + axis, 1 + c, mass * affine[3 * c + axis])
            put(1 + axis, 4 + c, scaled * stress[3 * c + axis])
    dense_weights(state[0], along)
    dense_weights(state[1], across)
    base = far_planes(device)
    for b in range(bins):
        total = None
        for begin, width, lanes in halves(quarters):
            row = b * quarters + begin
            tables = []
            for kind, values in enumerate(pair_weights(state_ref, across, row, width)):
                high, low = split(values)
                highs[b, pl.ds(kind * TILE, TILE), lanes] = high
                lows[b, pl.ds(kind * TILE, TILE), lanes] = low
                tables.append((high, low))
            sums = plane_sums((base, base + 1), row, width, channels, along, tables)
            total = sums if total is None else total + sums
        far[:, TILE * b : TILE * (b + 1)] = total
    nodes = bins * TILE
    width = far.shape[1]
    far[:, nodes:width] = jnp.broadcast_to(meta[0:1, nodes:width], (16, width - nodes))


def rest_of_grid(device, bins, meta, far, highs, lows, along, channels, near):
    rows = along.shape[0] // 12
    quarters = rows // bins
    odd = device % 2 == 1
    base = 4 - far_planes(device)
    middle = []
    for b in range(bins):
        total = None
        for begin, width, lanes in halves(quarters):
            row = b * quarters + begin
            tables = [
                (highs[b, pl.ds(kind * TILE, TILE), lanes], lows[b, pl.ds(kind * TILE, TILE), lanes])
                for kind in range(3)
            ]
            sums = plane_sums((base, base + 1, 2, 3), row, width, channels, along, tables)
            total = sums if total is None else total + sums
        near[:, TILE * b : TILE * (b + 1)] = total[0:16]
        middle.append(total[16:32])
    nodes = bins * TILE
    width = near.shape[1]
    near[:, nodes:width] = jnp.broadcast_to(meta[0:1, nodes:width], (16, width - nodes))
    near_part, far_part = near[:, 0:nodes], far[:, 0:nodes]
    low = jnp.where(odd, near_part, far_part)
    high = jnp.where(odd, far_part, near_part)
    return low, middle, high


def node_key(block, node):
    block_y = jnp.floor((block + 0.5) * (1.0 / BZ))
    block_z = block - BZ * block_y
    node_y = jnp.floor((node + 0.5) * (1.0 / 8.0))
    node_z = node - 8.0 * node_y
    return 4.0 * block_y + node_y, 4.0 * block_z + node_z


def placing(source_block, column_key, bins):
    nodes = bins * TILE
    source = iota((nodes, 1), 0).astype(F32)
    source_bin = jnp.floor((source + 0.5) * (1.0 / TILE))
    source_node = source - TILE * source_bin
    block = jnp.zeros((nodes, 1), F32)
    for b in range(bins):
        block = jnp.where(source_bin == float(b), source_block[b], block)
    row_y, row_z = node_key(block, source_node)
    row_key = LANES * row_y + row_z
    used = source_node - 8.0 * jnp.floor((source_node + 0.5) * (1.0 / 8.0)) < 6.0
    row_key = jnp.where(used, row_key, -2.0)
    return jnp.where(row_key == column_key, 1.0, 0.0).astype(BF16)


def placed(values, selector):
    count = values.shape[0]
    high, low = split(values)
    result = dot_nn(jnp.concatenate([high, low], axis=0), selector)
    return result[0:count] + result[count : 2 * count]


def halos(near, outer, inner, device, device_total):
    odd = device % 2 == 1
    middle = (device + 1) % 4 >= 2
    near_block = near[...]
    far_block = jnp.where(middle, inner[...], outer[...])
    left_block = jnp.where(odd, near_block, far_block)
    right_block = jnp.where(odd, far_block, near_block)
    left_block = jnp.where(device > 0, left_block, 0.0)
    right_block = jnp.where(device + 1 < device_total, right_block, 0.0)
    return left_block, right_block


def block_numbers(row, bins):
    lane = iota((1, LANES), 1)
    return [
        jnp.max(jnp.where(lane == META + b, row[:, LANES : 2 * LANES], 0.0), axis=1, keepdims=True)
        for b in range(bins)
    ]


def to_particles(
    live, old_ref, device, bins, device_total, geometry, own, sides, speeds, blocks_around,
    highs, lows, along, shuffle, started, finish,
):
    rows = old_ref.shape[0] // ROWS
    quarters = rows // bins
    state = read_state(old_ref, rows)
    width = bins * SLOT
    nodes = bins * TILE
    fastest = jnp.max(speeds[...], axis=0, keepdims=True)
    fastest = jnp.where(iota((1, LANES), 1) < META, fastest, 0.0)
    fastest = jnp.max(fastest, axis=1, keepdims=True)
    time_step = courant / (jnp.sqrt(fastest) + sound_speed)

    around = []
    for side, block in enumerate(blocks_around):
        around.append(placed(block[:, 0:nodes], sides[side]))
    left, right = around

    sub = iota((8, width), 0)
    wide_valid = geometry[0:8, :] >= 0.0
    component = (sub >= 1) & (sub <= 3) & wide_valid
    floor_of = geometry[8:16, :]
    roof_of = geometry[16:24, :]
    pull = time_step * jnp.where(sub == 1, gravity_x, jnp.where(sub == 3, gravity_z, 0.0))
    plane_total = 4 * device_total
    motions = []
    for a in range(6):
        sums = own[8 * a : 8 * a + 8, :]
        if a < 2:
            sums = sums + left[8 * a : 8 * a + 8]
        if a >= 4:
            sums = sums + right[8 * a - 32 : 8 * a - 24]
        plane = 4 * device + a
        node_mass = jnp.maximum(jnp.broadcast_to(sums[0:1, :], (8, width)), mass_floor)
        per_step = pltpu.roll(sums, 5, 0)
        motion = (sums - time_step * per_step) / node_mass + pull
        lowest = jnp.where(plane < 2, 0.0, -BIG)
        highest = jnp.where(plane >= plane_total - 2, 0.0, BIG)
        motion = jnp.maximum(motion, jnp.where(sub == 1, lowest, floor_of))
        motion = jnp.minimum(motion, jnp.where(sub == 1, highest, roof_of))
        inside = jnp.where(plane < plane_total, 1, 0)
        motion = jnp.where(component & (inside > 0), motion, 0.0)
        motions.append(motion)
    paired = jnp.concatenate(
        [motions[2 * g] + pltpu.roll(motions[2 * g + 1], 4, 0) for g in range(3)], axis=0
    )

    span = 8 * rows
    blocks = []
    for b in range(bins):
        begin = (b * SLOT) // LANES * LANES
        block = paired[:, begin : begin + LANES]
        if b * SLOT > begin:
            block = pltpu.roll(block, LANES - (b * SLOT - begin), 1)
        block = block[:, 0:TILE]
        high = block.astype(BF16)
        kept = high.astype(F32)
        blocks.append((jnp.concatenate([kept, block - kept], axis=0).astype(BF16), high))

    def gather(kinds):
        for b in range(bins):
            stacked, high = blocks[b]
            count = high.shape[0]
            for first_quarter, wide, lanes in halves(quarters):
                row = b * quarters + first_quarter
                even = iota((8, wide * LANES), 0) < 4

                def pair_weights_of(begin):
                    return [
                        jnp.where(
                            even,
                            spread(along, rows * (begin + 2 * g) + row, wide),
                            spread(along, rows * (begin + 2 * g + 1) + row, wide),
                        )
                        for g in range(3)
                    ]

                weights = pair_weights_of(0)
                for kind in kinds:
                    right_high = highs[b, pl.ds(kind * TILE, TILE), lanes]
                    right_low = lows[b, pl.ds(kind * TILE, TILE), lanes]
                    product = dot_nn(stacked, right_high)
                    product = product[0:count] + product[count : 2 * count]
                    product = product + dot_nn(high, right_low)
                    groups = [product[8 * g : 8 * g + 8] for g in range(3)]
                    sums = [(kind, sum(w * group for w, group in zip(weights, groups)))]
                    if kind == 0:
                        moved = zip(pair_weights_of(6), groups)
                        sums.append((3, sum(w * group for w, group in moved)))
                    for target, value in sums:
                        for q in range(wide):
                            place = target * span + 8 * (row + q)
                            shuffle[pl.ds(place, 8), :] = value[:, LANES * q : LANES * (q + 1)]

    def take(kind, c):
        return (
            shuffle[pl.ds(kind * span + 1 + c, rows, stride=8), :]
            + shuffle[pl.ds(kind * span + 5 + c, rows, stride=8), :]
        )

    gather((0, 1, 2) if live is None else (0,))
    started([take(0, c) for c in range(3)])

    def rest():
        if live is not None:
            gather((1, 2))
        velocity = [take(0, c) for c in range(3)]
        affine = [None] * 9
        for c in range(3):
            affine[3 * c] = 4.0 * take(3, c)
            affine[3 * c + 1] = 4.0 * take(1, c)
            affine[3 * c + 2] = 4.0 * take(2, c)
        old = state[DEF : DEF + 9]
        deform = []
        for r in range(3):
            for c in range(3):
                change = (
                    affine[3 * r] * old[c]
                    + affine[3 * r + 1] * old[3 + c]
                    + affine[3 * r + 2] * old[6 + c]
                )
                deform.append(old[3 * r + c] + time_step * change)
        steps = [time_step * velocity[c] for c in range(3)]
        moved = [state[c] + steps[c] for c in range(3)]
        travelled = [state[TRAV + c] + steps[c] for c in range(3)]
        finish(moved + deform + [state[MASS], state[VOL]] + travelled, velocity, affine)

    if live is None:
        rest()
    else:
        pl.when(live[0] >= 0)(rest)


def read_state(ref, rows):
    return [ref[pl.ds(rows * number, rows), :] for number in range(ROWS)]


def write_state(ref, state):
    rows = state[0].shape[0]
    for number in range(ROWS):
        ref[pl.ds(rows * number, rows), :] = state[number]


def rows_of(begin, count, s, rows):
    if count == 1:
        return pl.ds(rows * begin + s, 1)
    return pl.ds(rows * begin + s, count, stride=rows)


def block_row(blocks, bins, width):
    lane = iota((1, width), 1)
    meta = jnp.zeros((1, width), F32)
    for b in range(bins):
        meta = jnp.where(lane == LANES + META + b, blocks[b].astype(F32), meta)
    return meta


def first_kernel(
    bins, device_total, live, device, blocks_in, x_in, v_in, f_in, c_in, m_in, vol_in,
    state_ref, motion_ref, speeds, meta, outbox, sem, blocks, x_ref, v_ref, f_ref, c_ref, m_ref,
    vol_ref, arrivals,
):
    rows = state_ref.shape[0] // ROWS
    quarters = rows // bins
    half = rows * LANES
    copies = []
    moves = (
        (v_in.at[:, pl.ds(0, half)], v_ref),
        (m_in.at[pl.ds(0, half)], m_ref),
        (blocks_in, blocks),
        (x_in.at[:, pl.ds(0, half)], x_ref),
        (f_in.at[:, pl.ds(0, half)], f_ref),
        (c_in.at[:, pl.ds(0, half)], c_ref),
        (vol_in.at[pl.ds(0, half)], vol_ref),
    )
    for number, (source, target) in enumerate(moves):
        copies.append(pltpu.make_async_copy(source, target, arrivals.at[number]))
        copies[number].start()
    copies[0].wait()
    copies[1].wait()

    def relay(ref, count, kept, begin):
        for s in range(rows):
            for start in range(0, count, 8):
                size = min(8, count - start)
                source = ref[pl.ds(start, size), pl.ds(LANES * s, LANES)]
                kept[rows_of(begin + start, size, s, rows), :] = source

    def relay_flat(ref, number):
        for b in range(bins):
            alive = jnp.where(b < live[0], 1.0, 0.0)
            for q in range(quarters):
                s = quarters * b + q
                piece = ref[pl.ds(LANES * s, LANES)].reshape(1, LANES)
                state_ref[pl.ds(rows * number + s, 1), :] = piece * alive

    fastest = jnp.zeros((1, LANES), F32)
    for b in range(bins):
        for s in range(quarters * b, quarters * (b + 1)):
            part = v_ref[:, pl.ds(LANES * s, LANES)]
            speed = jnp.sum(part * part, axis=0, keepdims=True)
            mass = m_ref[pl.ds(LANES * s, LANES)].reshape(1, LANES)
            counted = (mass > 0.0) & (b < live[0])
            fastest = jnp.maximum(fastest, jnp.where(counted, speed, 0.0))
    copies[2].wait()
    lane = iota((1, LANES), 1)
    fastest = jnp.broadcast_to(jnp.max(fastest, axis=1, keepdims=True), (1, LANES))
    for b in range(bins):
        fastest = jnp.where(lane == META + b, blocks[b].astype(F32), fastest)
    outbox[...] = jnp.broadcast_to(fastest, outbox.shape)
    pltpu.make_async_copy(outbox, speeds, sem).start()

    @pl.when(live[0] >= 0)
    def _():
        for copy in copies[3:]:
            copy.wait()
        relay(v_ref, 3, motion_ref, 0)
        relay_flat(m_ref, MASS)
        relay(x_ref, 3, state_ref, POS)
        relay(f_ref, 9, state_ref, DEF)
        relay(c_ref, 9, motion_ref, 3)
        relay_flat(vol_ref, VOL)
        home = jnp.zeros((rows, LANES), F32)
        home_y, home_z = home, home
        row_bin = iota((rows, LANES), 0) // quarters
        for b in range(bins):
            block = blocks[b]
            block_y = block // BZ
            block_z = block - BZ * block_y
            home_y = jnp.where(row_bin == b, (4 * block_y).astype(F32), home_y)
            home_z = jnp.where(row_bin == b, (4 * block_z).astype(F32), home_z)
        anchors = (home + (4 * device).astype(F32), home_y, home_z)
        for axis in range(3):
            place = pl.ds(rows * axis, rows)
            state_ref[place, :] = state_ref[place, :] - anchors[axis]
            state_ref[pl.ds(rows * (TRAV + axis), rows), :] = home
        meta[...] = jnp.broadcast_to(block_row(blocks, bins, meta.shape[1]), meta.shape)

    pltpu.make_async_copy(outbox, speeds, sem).wait()


def scatter_kernel(
    bins, device_total, live, device, state_ref, motion_ref, meta, far, highs, lows, along,
    channels, across,
):
    rows = state_ref.shape[0] // ROWS
    motion = [motion_ref[pl.ds(rows * number, rows), :] for number in range(12)]
    to_grid(
        read_state(state_ref, rows), motion[0:3], motion[3:12], state_ref, device, bins, meta, far,
        highs, lows, along, channels, across,
    )


def place_own(own, low, middle, high, selector):
    own[0:16, :] = placed(low, selector)
    own[16:32, :] = placed(jnp.concatenate(middle, axis=1), selector)
    own[32:48, :] = placed(high, selector)


def first_rest_kernel(
    bins, device_total, live, device, meta, far, highs, lows, along, channels,
    near, own, geometry, home,
):
    low, middle, high = rest_of_grid(
        device, bins, meta, far, highs, lows, along, channels, near
    )
    width = bins * SLOT
    position = iota((1, width), 1)
    column_bin = position // SLOT
    column_node = position - SLOT * column_bin
    column_valid = (column_node < TILE) & (column_node % 8 < 6)
    own_blocks = block_numbers(meta[0:1, :], bins)
    column_block = jnp.zeros((1, width), F32)
    for b in range(bins):
        column_block = jnp.where(column_bin == b, own_blocks[b], column_block)
    column_y, column_z = node_key(column_block, column_node.astype(F32))
    column_key = jnp.where(column_valid, LANES * column_y + column_z, -1.0)
    selector = placing(own_blocks, column_key, bins)
    home[...] = selector
    place_own(own, low, middle, high, selector)
    sub = iota((8, width), 0)
    wide_y = jnp.broadcast_to(column_y, (8, width))
    wide_z = jnp.broadcast_to(column_z, (8, width))
    geometry[0:8, :] = jnp.broadcast_to(column_key, (8, width))
    geometry[8:16, :] = jnp.where(
        ((sub == 2) & (wide_y < 2.0)) | ((sub == 3) & (wide_z < 2.0)), 0.0, -BIG
    )
    geometry[16:24, :] = jnp.where(
        ((sub == 2) & (wide_y >= NGY - 2.0)) | ((sub == 3) & (wide_z >= NGZ - 2.0)), 0.0, BIG
    )


def rest_kernel(
    bins, device_total, live, device, meta, far, highs, lows, along, channels, home, near, own
):
    low, middle, high = rest_of_grid(
        device, bins, meta, far, highs, lows, along, channels, near
    )
    place_own(own, low, middle, high, home[...])


def sides_kernel(bins, device_total, live, device, speeds, geometry, sides_ref):
    lane = iota((1, LANES), 1)
    key = geometry[0:1, :]
    left, right = jnp.maximum(device - 1, 0), jnp.minimum(device + 1, device_total - 1)
    for side, index in enumerate((left, right)):
        row = speeds[pl.ds(index, 1), :]
        numbers = [
            jnp.max(jnp.where(lane == META + b, row, 0.0), axis=1, keepdims=True)
            for b in range(bins)
        ]
        sides_ref[side] = placing(numbers, key, bins)


def second_kernel(
    bins, device_total, live, device, meta, old_ref, speeds, own, geometry, highs, lows, along,
    near, outer, inner, sides_ref, state_ref, new_speeds, far, new_highs, new_lows, new_along,
    channels, across, outbox, sem,
):
    rows = state_ref.shape[0] // ROWS
    around = halos(near, outer, inner, device, device_total)
    sides = [sides_ref[0], sides_ref[1]]

    def started(velocity):
        send_speed(velocity, old_ref[pl.ds(rows * MASS, rows), :], new_speeds, outbox, sem)

    def finish(state, velocity, affine):
        write_state(state_ref, state)
        to_grid(
            state, velocity, affine, state_ref, device, bins, meta, far, new_highs, new_lows,
            new_along, channels, across,
        )

    to_particles(
        None, old_ref, device, bins, device_total, geometry, own, sides, speeds, around, highs,
        lows, along, channels, started, finish,
    )
    pltpu.make_async_copy(outbox, new_speeds, sem).wait()


def later_kernel(
    bins, device_total, live, device, old_ref, speeds, own, geometry, highs, lows, along,
    near, outer, inner, sides_ref, state_ref, motion_ref, new_speeds, shuffle, outbox, sem,
):
    around = halos(near, outer, inner, device, device_total)
    sides = [sides_ref[0], sides_ref[1]]
    advance(
        live, bins, device_total, device, old_ref, speeds, own, geometry, highs, lows, along, around,
        sides, state_ref, motion_ref, new_speeds, shuffle, outbox, sem,
    )


def advance(
    live, bins, device_total, device, old_ref, speeds, own, geometry, highs, lows, along, around,
    sides, state_ref, motion_ref, new_speeds, shuffle, outbox, sem,
):
    rows = state_ref.shape[0] // ROWS

    def started(velocity):
        send_speed(velocity, old_ref[pl.ds(rows * MASS, rows), :], new_speeds, outbox, sem)

    def finish(state, velocity, affine):
        write_state(state_ref, state)
        for number, value in enumerate(velocity + affine):
            motion_ref[pl.ds(rows * number, rows), :] = value

    to_particles(
        live, old_ref, device, bins, device_total, geometry, own, sides, speeds, around, highs,
        lows, along, shuffle, started, finish,
    )
    pltpu.make_async_copy(outbox, new_speeds, sem).wait()


def last_kernel(
    bins, device_total, live, device, old_ref, speeds, own, geometry, highs, lows, along,
    near, outer, inner, sides_ref, d_out, v_out, f_out, c_out, shuffle, d_rows,
    v_rows, f_rows, c_rows,
):
    rows = old_ref.shape[0] // ROWS
    quarters = rows // bins
    row_bin = iota((rows, LANES), 0) // quarters
    alive = row_bin < live[0]
    half = rows * LANES

    def finish(state, velocity, affine):
        results = (
            (d_out, state[TRAV : TRAV + 3], d_rows),
            (v_out, velocity, v_rows),
            (f_out, state[DEF : DEF + 9], f_rows),
            (c_out, affine, c_rows),
        )
        for ref, values, finished in results:
            count = len(values)
            for number in range(count):
                finished[pl.ds(rows * number, rows), :] = jnp.where(alive, values[number], 0.0)
            for s in range(rows):
                for start in range(0, count, 8):
                    size = min(8, count - start)
                    value = finished[rows_of(start, size, s, rows), :]
                    ref[pl.ds(start, size), pl.ds(LANES * s, LANES)] = value
            total = ref.shape[1]
            ref[:, pl.ds(half, total - half)] = jnp.zeros((count, total - half), F32)

    to_particles(
        None, old_ref, device, bins, device_total, geometry, own, [sides_ref[0], sides_ref[1]], speeds,
        halos(near, outer, inner, device, device_total), highs, lows, along, shuffle,
        lambda velocity: None, finish,
    )


def local(positions, velocity, deformation, affine, particle_mass, volume, bin_block, live_count):
    slot_total = bin_block.shape[0]
    per_bin = positions.shape[1] // slot_total
    bins = slot_total // 2
    device_total = lax.axis_size("space")
    rows = bins * per_bin // LANES
    half = rows * LANES
    nodes = bins * TILE
    width = bins * SLOT
    message = ((16, -(-(nodes + LANES // 2) // LANES) * LANES), F32)
    speeds_shape = ((device_total, LANES), F32)
    held = [((ROWS * rows, LANES), F32), ((12 * rows, LANES), F32), speeds_shape]
    grid_held = [
        message,
        ((bins, 3 * TILE, per_bin), BF16),
        ((bins, 3 * TILE, per_bin), BF16),
        ((12 * rows, LANES), F32),
        ((4 * 8 * rows, LANES), F32),
    ]
    meta_shape = ((8, message[0][1]), F32)
    own_shape = ((48, width), F32)
    geometry_shape = ((24, width), F32)
    home_shape = ((nodes, width), BF16)
    sides_shape = ((2, nodes, width), BF16)
    smem = pl.BlockSpec(memory_space=pltpu.SMEM)
    vmem = pl.BlockSpec(memory_space=pltpu.VMEM)
    anywhere = pl.BlockSpec(memory_space=pl.ANY)
    shuffle = pltpu.VMEM((4 * 8 * rows, LANES), F32)
    sending = [pltpu.VMEM((device_total, LANES), F32), pltpu.SemaphoreType.DMA]
    me = lax.axis_index("space").astype(jnp.int32).reshape(1)

    def stay(array, space=pltpu.VMEM):
        return array if INTERPRET else pltpu.with_memory_space_constraint(array, space)

    def call(body, scalars, arguments, outputs, scratch, in_specs=None, final=False):
        def kernel(*refs):
            count = len(scalars)
            body(bins, device_total, *refs[: count - 1], refs[count - 1][0], *refs[count:])

        out_specs = tuple(anywhere if output == speeds_shape else vmem for output in outputs)
        if in_specs is None:
            in_specs = [vmem] * len(arguments)
            arguments = [stay(argument) for argument in arguments]
        else:
            arguments = [stay(argument, pltpu.HBM) for argument in arguments]
        make = jax.ShapeDtypeStruct if final or INTERPRET else pltpu.VMEM
        return pl.pallas_call(
            kernel,
            in_specs=[smem] * len(scalars) + in_specs,
            out_shape=tuple(
                pltpu.HBM(*output) if output == speeds_shape and not INTERPRET else make(*output)
                for output in outputs
            ),
            out_specs=out_specs,
            scratch_shapes=scratch,
            interpret=INTERPRET,
            compiler_params=pltpu.CompilerParams(vmem_limit_bytes=GRANT),
        )(*scalars, *arguments)

    length = device_total
    swap_pairs = [(i, i ^ 1) for i in range(length)]
    inner_pairs = [(i, i ^ 3) for i in range(length)]
    outer_pairs = [(i, i + 1) for i in range(3, length - 1, 4)]
    outer_pairs = outer_pairs + [(i, i + 3) for i in range(2, length - 3, 4)]
    outer_pairs = outer_pairs + [(0, 1), (length - 2, length - 1)]
    outer_pairs = outer_pairs + [(j, i) for i, j in outer_pairs]

    slot_rows = [pltpu.VMEM((count, half), F32) for count in (3, 3, 9, 9)]
    *results, meta = call(
        first_kernel,
        (live_count, me),
        (bin_block, positions, velocity, deformation, affine, particle_mass, volume),
        [*held, meta_shape],
        sending
        + [pltpu.SMEM((slot_total,), jnp.int32)]
        + slot_rows
        + [pltpu.VMEM((half,), F32), pltpu.VMEM((half,), F32), pltpu.SemaphoreType.DMA((7,))],
        [anywhere] * 7,
    )
    across = pltpu.VMEM((12 * rows, LANES), F32)
    state, motion, speeds = results
    for step in range(STEPS):
        speeds = lax.all_to_all(speeds, "space", 0, 0, tiled=True)
        if step != 1:
            far, highs, lows, along, channels = call(
                scatter_kernel, (live_count, me), (state, motion, meta), grid_held, [across]
            )
        from_outer = lax.ppermute(far, "space", outer_pairs)
        from_inner = lax.ppermute(far, "space", inner_pairs)
        arguments = (meta, far, highs, lows, along, channels)
        if step == 0:
            near, own, geometry, home = call(
                first_rest_kernel,
                (live_count, me),
                arguments,
                [message, own_shape, geometry_shape, home_shape],
                [],
            )
        else:
            near, own = call(
                rest_kernel, (live_count, me), arguments + (home,), [message, own_shape], []
            )
        from_near = lax.ppermute(near, "space", swap_pairs)
        arguments = (
            state, speeds, own, geometry, highs, lows, along, from_near, from_outer, from_inner,
        )
        if step == 0:
            (sides,) = call(sides_kernel, (live_count, me), (speeds, geometry), [sides_shape], [])
            state, speeds, far, highs, lows, along, channels = call(
                second_kernel,
                (live_count, me),
                (meta, *arguments, sides),
                [held[0], speeds_shape, *grid_held],
                [across] + sending,
            )
        elif step < STEPS - 1:
            state, motion, speeds = call(
                later_kernel, (live_count, me), (*arguments, sides), held, [shuffle] + sending
            )
    total = positions.shape[1]
    return call(
        last_kernel,
        (live_count, me),
        (*arguments, sides),
        [((count, total), F32) for count in (3, 3, 9, 9)],
        [shuffle] + [pltpu.VMEM((count * rows, LANES), F32) for count in (3, 3, 9, 9)],
        final=True,
    )


def solution(mesh):
    in_specs = (
        P(None, "space"),
        P(None, "space"),
        P(None, "space"),
        P(None, "space"),
        P("space"),
        P("space"),
        P("space"),
        P("space"),
    )
    out_specs = (P(None, "space"), P(None, "space"), P(None, "space"), P(None, "space"))
    return jax.shard_map(local, mesh=mesh, in_specs=in_specs, out_specs=out_specs, check_vma=False)
```

```python
import jax
import jax.numpy as jnp
from jax import lax
from jax.experimental import pallas as pl
from jax.experimental.pallas import tpu as pltpu
from jax.sharding import PartitionSpec as P


BZ = 16
STEPS = 3
NGY = 66
NGZ = 66

mu_shear = 4.0
lame_first = 6.0
courant = 0.15
sound_speed = 3.7416573867739413
mass_floor = 0.05
gravity_x = 3.0
gravity_z = -9.0

LANES = 128
TILE = 48
SLOT = 64
META = 64
BIG = 3.0e38
GRANT = 8 * 2**20
F32 = jnp.float32
BF16 = jnp.bfloat16
INTERPRET = False

POS, DEF, MASS, VOL, TRAV = 0, 3, 12, 13, 14
ROWS = 17


def iota(shape, dim):
    return lax.broadcasted_iota(jnp.int32, shape, dim)


def split(value):
    high = value.astype(BF16)
    low = (value - high.astype(F32)).astype(BF16)
    return high, low


def dot_nt(a, b):
    return lax.dot_general(a, b, (((1,), (1,)), ((), ())), preferred_element_type=F32)


def dot_nn(a, b):
    return lax.dot_general(a, b, (((1,), (0,)), ((), ())), preferred_element_type=F32)


def spline(distance):
    magnitude = jnp.abs(distance)
    outer = jnp.maximum(1.5 - magnitude, 0.0)
    inner = jnp.maximum(0.5 - magnitude, 0.0)
    return 0.5 * outer * outer - 1.5 * inner * inner


def spread(ref, row, quarters):
    return jnp.concatenate(
        [ref[pl.ds(row + q, 8, stride=0), :] for q in range(quarters)], axis=1
    )


def dense_weights(position, ref):
    rows = position.shape[0]
    for a in range(6):
        offset = float(a) - position
        weight = spline(offset)
        ref[pl.ds(rows * a, rows), :] = weight
        ref[pl.ds(rows * (6 + a), rows), :] = weight * offset


def pair_weights(state_ref, across, row, span):
    rows = across.shape[0] // 12
    along_z = spread(state_ref, 2 * rows + row, span)
    third_node = iota(along_z.shape, 0)
    third_offset = third_node.astype(F32) - along_z
    third = jnp.where(third_node < 6, spline(third_offset), 0.0)
    third_moved = third * third_offset
    plain, moved_y, moved_z = [], [], []
    for a in range(6):
        second = spread(across, rows * a + row, span)
        second_moved = spread(across, rows * (6 + a) + row, span)
        plain.append(second * third)
        moved_y.append(second_moved * third)
        moved_z.append(second * third_moved)
    return [jnp.concatenate(part, axis=0) for part in (plain, moved_y, moved_z)]


def kirchhoff(deform):
    determinant = (
        deform[0] * (deform[4] * deform[8] - deform[5] * deform[7])
        - deform[1] * (deform[3] * deform[8] - deform[5] * deform[6])
        + deform[2] * (deform[3] * deform[7] - deform[4] * deform[6])
    )
    pressure = lame_first * (determinant - 1.0) * determinant
    stress = [None] * 9
    for r in range(3):
        for c in range(r, 3):
            product = (
                deform[3 * r] * deform[3 * c]
                + deform[3 * r + 1] * deform[3 * c + 1]
                + deform[3 * r + 2] * deform[3 * c + 2]
            )
            if r == c:
                stress[3 * r + c] = mu_shear * (product - 1.0) + pressure
            else:
                stress[3 * r + c] = mu_shear * product
                stress[3 * c + r] = stress[3 * r + c]
    return stress


def send_speed(velocity, mass, speeds, outbox, sem):
    speed = velocity[0] * velocity[0] + velocity[1] * velocity[1] + velocity[2] * velocity[2]
    speed = jnp.max(jnp.where(mass > 0.0, speed, 0.0), axis=0, keepdims=True)
    speed = jnp.max(speed, axis=1, keepdims=True)
    outbox[...] = jnp.broadcast_to(speed, outbox.shape)
    pltpu.make_async_copy(outbox, speeds, sem).start()


def halves(quarters):
    parts = 2 if quarters % 2 == 0 else 1
    span = quarters // parts
    return [(part * span, span, pl.ds(part * span * LANES, span * LANES)) for part in range(parts)]


def plane_sums(planes, row, span, channels, along, tables):
    rows = along.shape[0] // 12

    def channel(matrix):
        begin = 8 * (matrix * rows + row)
        return jnp.concatenate(
            [channels[pl.ds(begin + 8 * q, 8), :] for q in range(span)], axis=1
        )

    base, slope_x, slope_y, slope_z = [channel(matrix) for matrix in range(4)]
    pieces = ([], [], [])
    for a in planes:
        first = spread(along, rows * a + row, span)
        first_moved = spread(along, rows * (6 + a) + row, span)
        pieces[0].append(first * base + first_moved * slope_x)
        pieces[1].append(first * slope_y)
        pieces[2].append(first * slope_z)
    count = 8 * len(planes)
    total = None
    for piece, (right_high, right_low) in zip(pieces, tables):
        left_high, left_low = split(jnp.concatenate(piece, axis=0))
        both = dot_nt(jnp.concatenate([left_high, left_low], axis=0), right_high)
        product = both[0:count] + both[count : 2 * count] + dot_nt(left_high, right_low)
        total = product if total is None else total + product
    return total


def far_planes(device):
    return 4 * (device % 2)


def to_grid(
    state, velocity, affine, state_ref, device, bins, meta, far, highs, lows, along, channels, across
):
    rows = state[0].shape[0]
    quarters = rows // bins
    deform = state[DEF : DEF + 9]
    mass, volume = state[MASS], state[VOL]
    stress = kirchhoff(deform)
    scaled = 4.0 * volume
    span = 8 * rows
    zero = jnp.zeros((rows, LANES), F32)

    def put(matrix, row, value):
        channels[pl.ds(matrix * span + row, rows, stride=8), :] = value

    put(0, 0, mass)
    for c in range(3):
        put(0, 1 + c, mass * velocity[c])
        put(0, 4 + c, zero)
    put(0, 7, zero)
    for axis in range(3):
        put(1 + axis, 0, zero)
        put(1 + axis, 7, zero)
        for c in range(3):
            put(1 + axis, 1 + c, mass * affine[3 * c + axis])
            put(1 + axis, 4 + c, scaled * stress[3 * c + axis])
    dense_weights(state[0], along)
    dense_weights(state[1], across)
    base = far_planes(device)
    for b in range(bins):
        total = None
        for begin, width, lanes in halves(quarters):
            row = b * quarters + begin
            tables = []
            for kind, values in enumerate(pair_weights(state_ref, across, row, width)):
                high, low = split(values)
                highs[b, pl.ds(kind * TILE, TILE), lanes] = high
                lows[b, pl.ds(kind * TILE, TILE), lanes] = low
                tables.append((high, low))
            sums = plane_sums((base, base + 1), row, width, channels, along, tables)
            total = sums if total is None else total + sums
        far[:, TILE * b : TILE * (b + 1)] = total
    nodes = bins * TILE
    width = far.shape[1]
    far[:, nodes:width] = jnp.broadcast_to(meta[0:1, nodes:width], (16, width - nodes))


def rest_of_grid(device, bins, meta, far, highs, lows, along, channels, near):
    rows = along.shape[0] // 12
    quarters = rows // bins
    odd = device % 2 == 1
    base = 4 - far_planes(device)
    middle = []
    for b in range(bins):
        total = None
        for begin, width, lanes in halves(quarters):
            row = b * quarters + begin
            tables = [
                (highs[b, pl.ds(kind * TILE, TILE), lanes], lows[b, pl.ds(kind * TILE, TILE), lanes])
                for kind in range(3)
            ]
            sums = plane_sums((base, base + 1, 2, 3), row, width, channels, along, tables)
            total = sums if total is None else total + sums
        near[:, TILE * b : TILE * (b + 1)] = total[0:16]
        middle.append(total[16:32])
    nodes = bins * TILE
    width = near.shape[1]
    near[:, nodes:width] = jnp.broadcast_to(meta[0:1, nodes:width], (16, width - nodes))
    near_part, far_part = near[:, 0:nodes], far[:, 0:nodes]
    low = jnp.where(odd, near_part, far_part)
    high = jnp.where(odd, far_part, near_part)
    return low, middle, high


def node_key(block, node):
    block_y = jnp.floor((block + 0.5) * (1.0 / BZ))
    block_z = block - BZ * block_y
    node_y = jnp.floor((node + 0.5) * (1.0 / 8.0))
    node_z = node - 8.0 * node_y
    return 4.0 * block_y + node_y, 4.0 * block_z + node_z


def placing(source_block, column_key, bins):
    nodes = bins * TILE
    source = iota((nodes, 1), 0).astype(F32)
    source_bin = jnp.floor((source + 0.5) * (1.0 / TILE))
    source_node = source - TILE * source_bin
    block = jnp.zeros((nodes, 1), F32)
    for b in range(bins):
        block = jnp.where(source_bin == float(b), source_block[b], block)
    row_y, row_z = node_key(block, source_node)
    row_key = LANES * row_y + row_z
    used = source_node - 8.0 * jnp.floor((source_node + 0.5) * (1.0 / 8.0)) < 6.0
    row_key = jnp.where(used, row_key, -2.0)
    return jnp.where(row_key == column_key, 1.0, 0.0).astype(BF16)


def placed(values, selector):
    count = values.shape[0]
    high, low = split(values)
    result = dot_nn(jnp.concatenate([high, low], axis=0), selector)
    return result[0:count] + result[count : 2 * count]


def halos(near, outer, inner, device, device_total):
    odd = device % 2 == 1
    middle = (device + 1) % 4 >= 2
    near_block = near[...]
    far_block = jnp.where(middle, inner[...], outer[...])
    left_block = jnp.where(odd, near_block, far_block)
    right_block = jnp.where(odd, far_block, near_block)
    left_block = jnp.where(device > 0, left_block, 0.0)
    right_block = jnp.where(device + 1 < device_total, right_block, 0.0)
    return left_block, right_block


def block_numbers(row, bins):
    lane = iota((1, LANES), 1)
    return [
        jnp.max(jnp.where(lane == META + b, row[:, LANES : 2 * LANES], 0.0), axis=1, keepdims=True)
        for b in range(bins)
    ]


def to_particles(
    live, old_ref, device, bins, device_total, geometry, own, sides, speeds, blocks_around,
    highs, lows, along, shuffle, started, finish, whole=False,
):
    rows = old_ref.shape[0] // ROWS
    quarters = rows // bins
    state = read_state(old_ref, rows)
    width = bins * SLOT
    nodes = bins * TILE
    fastest = jnp.max(speeds[...], axis=0, keepdims=True)
    fastest = jnp.where(iota((1, LANES), 1) < META, fastest, 0.0)
    fastest = jnp.max(fastest, axis=1, keepdims=True)
    time_step = courant / (jnp.sqrt(fastest) + sound_speed)

    around = []
    for side, block in enumerate(blocks_around):
        around.append(placed(block[:, 0:nodes], sides[side]))
    left, right = around

    sub = iota((8, width), 0)
    wide_valid = geometry[0:8, :] >= 0.0
    component = (sub >= 1) & (sub <= 3) & wide_valid
    floor_of = geometry[8:16, :]
    roof_of = geometry[16:24, :]
    pull = time_step * jnp.where(sub == 1, gravity_x, jnp.where(sub == 3, gravity_z, 0.0))
    plane_total = 4 * device_total
    motions = []
    for a in range(6):
        sums = own[8 * a : 8 * a + 8, :]
        if a < 2:
            sums = sums + left[8 * a : 8 * a + 8]
        if a >= 4:
            sums = sums + right[8 * a - 32 : 8 * a - 24]
        plane = 4 * device + a
        node_mass = jnp.maximum(jnp.broadcast_to(sums[0:1, :], (8, width)), mass_floor)
        per_step = pltpu.roll(sums, 5, 0)
        motion = (sums - time_step * per_step) / node_mass + pull
        lowest = jnp.where(plane < 2, 0.0, -BIG)
        highest = jnp.where(plane >= plane_total - 2, 0.0, BIG)
        motion = jnp.maximum(motion, jnp.where(sub == 1, lowest, floor_of))
        motion = jnp.minimum(motion, jnp.where(sub == 1, highest, roof_of))
        inside = jnp.where(plane < plane_total, 1, 0)
        motion = jnp.where(component & (inside > 0), motion, 0.0)
        motions.append(motion)
    paired = jnp.concatenate(
        [motions[2 * g] + pltpu.roll(motions[2 * g + 1], 4, 0) for g in range(3)], axis=0
    )

    span = 8 * rows
    blocks = []
    for b in range(bins):
        begin = (b * SLOT) // LANES * LANES
        block = paired[:, begin : begin + LANES]
        if b * SLOT > begin:
            block = pltpu.roll(block, LANES - (b * SLOT - begin), 1)
        block = block[:, 0:TILE]
        high = block.astype(BF16)
        kept = high.astype(F32)
        blocks.append((jnp.concatenate([kept, block - kept], axis=0).astype(BF16), high))

    def gather(kinds):
        for b in range(bins):
            stacked, high = blocks[b]
            count = high.shape[0]
            for first_quarter, wide, lanes in halves(quarters):
                row = b * quarters + first_quarter
                even = iota((8, wide * LANES), 0) < 4

                def pair_weights_of(begin):
                    return [
                        jnp.where(
                            even,
                            spread(along, rows * (begin + 2 * g) + row, wide),
                            spread(along, rows * (begin + 2 * g + 1) + row, wide),
                        )
                        for g in range(3)
                    ]

                weights = pair_weights_of(0)
                for kind in kinds:
                    right_high = highs[b, pl.ds(kind * TILE, TILE), lanes]
                    right_low = lows[b, pl.ds(kind * TILE, TILE), lanes]
                    product = dot_nn(stacked, right_high)
                    product = product[0:count] + product[count : 2 * count]
                    product = product + dot_nn(high, right_low)
                    groups = [product[8 * g : 8 * g + 8] for g in range(3)]
                    sums = [(kind, sum(w * group for w, group in zip(weights, groups)))]
                    if kind == 0:
                        moved = zip(pair_weights_of(6), groups)
                        sums.append((3, sum(w * group for w, group in moved)))
                    for target, value in sums:
                        for q in range(wide):
                            place = target * span + 8 * (row + q)
                            shuffle[pl.ds(place, 8), :] = value[:, LANES * q : LANES * (q + 1)]

    def take(kind, c):
        return (
            shuffle[pl.ds(kind * span + 1 + c, rows, stride=8), :]
            + shuffle[pl.ds(kind * span + 5 + c, rows, stride=8), :]
        )

    whole = whole or live is None
    gather((0, 1, 2) if whole else (0,))
    started([take(0, c) for c in range(3)])

    def rest():
        if not whole:
            gather((1, 2))
        velocity = [take(0, c) for c in range(3)]
        affine = [None] * 9
        for c in range(3):
            affine[3 * c] = 4.0 * take(3, c)
            affine[3 * c + 1] = 4.0 * take(1, c)
            affine[3 * c + 2] = 4.0 * take(2, c)
        old = state[DEF : DEF + 9]
        deform = []
        for r in range(3):
            for c in range(3):
                change = (
                    affine[3 * r] * old[c]
                    + affine[3 * r + 1] * old[3 + c]
                    + affine[3 * r + 2] * old[6 + c]
                )
                deform.append(old[3 * r + c] + time_step * change)
        steps = [time_step * velocity[c] for c in range(3)]
        moved = [state[c] + steps[c] for c in range(3)]
        travelled = [state[TRAV + c] + steps[c] for c in range(3)]
        finish(moved + deform + [state[MASS], state[VOL]] + travelled, velocity, affine)

    if live is None:
        rest()
    else:
        pl.when(live[0] >= 0)(rest)


def read_state(ref, rows):
    return [ref[pl.ds(rows * number, rows), :] for number in range(ROWS)]


def write_state(ref, state):
    rows = state[0].shape[0]
    for number in range(ROWS):
        ref[pl.ds(rows * number, rows), :] = state[number]


def rows_of(begin, count, s, rows):
    if count == 1:
        return pl.ds(rows * begin + s, 1)
    return pl.ds(rows * begin + s, count, stride=rows)


def block_row(blocks, bins, width):
    lane = iota((1, width), 1)
    meta = jnp.zeros((1, width), F32)
    for b in range(bins):
        meta = jnp.where(lane == LANES + META + b, blocks[b].astype(F32), meta)
    return meta


def first_kernel(
    bins, device_total, live, device, blocks_in, x_in, v_in, f_in, c_in, m_in, vol_in,
    state_ref, motion_ref, speeds, meta, outbox, sem, blocks, x_ref, v_ref, f_ref, c_ref, m_ref,
    vol_ref, arrivals,
):
    rows = state_ref.shape[0] // ROWS
    quarters = rows // bins
    half = rows * LANES
    copies = []
    moves = (
        (v_in.at[:, pl.ds(0, half)], v_ref),
        (m_in.at[pl.ds(0, half)], m_ref),
        (blocks_in, blocks),
        (x_in.at[:, pl.ds(0, half)], x_ref),
        (f_in.at[:, pl.ds(0, half)], f_ref),
        (c_in.at[:, pl.ds(0, half)], c_ref),
        (vol_in.at[pl.ds(0, half)], vol_ref),
    )
    for number, (source, target) in enumerate(moves):
        copies.append(pltpu.make_async_copy(source, target, arrivals.at[number]))
        copies[number].start()
    copies[0].wait()
    copies[1].wait()

    def relay(ref, count, kept, begin):
        for s in range(rows):
            for start in range(0, count, 8):
                size = min(8, count - start)
                source = ref[pl.ds(start, size), pl.ds(LANES * s, LANES)]
                kept[rows_of(begin + start, size, s, rows), :] = source

    def relay_flat(ref, number):
        for b in range(bins):
            alive = jnp.where(b < live[0], 1.0, 0.0)
            for q in range(quarters):
                s = quarters * b + q
                piece = ref[pl.ds(LANES * s, LANES)].reshape(1, LANES)
                state_ref[pl.ds(rows * number + s, 1), :] = piece * alive

    fastest = jnp.zeros((1, LANES), F32)
    for b in range(bins):
        for s in range(quarters * b, quarters * (b + 1)):
            part = v_ref[:, pl.ds(LANES * s, LANES)]
            speed = jnp.sum(part * part, axis=0, keepdims=True)
            mass = m_ref[pl.ds(LANES * s, LANES)].reshape(1, LANES)
            counted = (mass > 0.0) & (b < live[0])
            fastest = jnp.maximum(fastest, jnp.where(counted, speed, 0.0))
    copies[2].wait()
    lane = iota((1, LANES), 1)
    fastest = jnp.broadcast_to(jnp.max(fastest, axis=1, keepdims=True), (1, LANES))
    for b in range(bins):
        fastest = jnp.where(lane == META + b, blocks[b].astype(F32), fastest)
    outbox[...] = jnp.broadcast_to(fastest, outbox.shape)
    pltpu.make_async_copy(outbox, speeds, sem).start()

    @pl.when(live[0] >= 0)
    def _():
        for copy in copies[3:]:
            copy.wait()
        relay(v_ref, 3, motion_ref, 0)
        relay_flat(m_ref, MASS)
        relay(x_ref, 3, state_ref, POS)
        relay(f_ref, 9, state_ref, DEF)
        relay(c_ref, 9, motion_ref, 3)
        relay_flat(vol_ref, VOL)
        home = jnp.zeros((rows, LANES), F32)
        home_y, home_z = home, home
        row_bin = iota((rows, LANES), 0) // quarters
        for b in range(bins):
            block = blocks[b]
            block_y = block // BZ
            block_z = block - BZ * block_y
            home_y = jnp.where(row_bin == b, (4 * block_y).astype(F32), home_y)
            home_z = jnp.where(row_bin == b, (4 * block_z).astype(F32), home_z)
        anchors = (home + (4 * device).astype(F32), home_y, home_z)
        for axis in range(3):
            place = pl.ds(rows * axis, rows)
            state_ref[place, :] = state_ref[place, :] - anchors[axis]
            state_ref[pl.ds(rows * (TRAV + axis), rows), :] = home
        meta[...] = jnp.broadcast_to(block_row(blocks, bins, meta.shape[1]), meta.shape)

    pltpu.make_async_copy(outbox, speeds, sem).wait()


def scatter_kernel(
    bins, device_total, live, device, state_ref, motion_ref, meta, far, highs, lows, along,
    channels, across,
):
    rows = state_ref.shape[0] // ROWS
    motion = [motion_ref[pl.ds(rows * number, rows), :] for number in range(12)]
    to_grid(
        read_state(state_ref, rows), motion[0:3], motion[3:12], state_ref, device, bins, meta, far,
        highs, lows, along, channels, across,
    )


def place_own(own, low, middle, high, selector):
    own[0:16, :] = placed(low, selector)
    own[16:32, :] = placed(jnp.concatenate(middle, axis=1), selector)
    own[32:48, :] = placed(high, selector)


def first_rest_kernel(
    bins, device_total, live, device, meta, far, highs, lows, along, channels,
    near, own, geometry, home,
):
    low, middle, high = rest_of_grid(
        device, bins, meta, far, highs, lows, along, channels, near
    )
    width = bins * SLOT
    position = iota((1, width), 1)
    column_bin = position // SLOT
    column_node = position - SLOT * column_bin
    column_valid = (column_node < TILE) & (column_node % 8 < 6)
    own_blocks = block_numbers(meta[0:1, :], bins)
    column_block = jnp.zeros((1, width), F32)
    for b in range(bins):
        column_block = jnp.where(column_bin == b, own_blocks[b], column_block)
    column_y, column_z = node_key(column_block, column_node.astype(F32))
    column_key = jnp.where(column_valid, LANES * column_y + column_z, -1.0)
    selector = placing(own_blocks, column_key, bins)
    home[...] = selector
    place_own(own, low, middle, high, selector)
    sub = iota((8, width), 0)
    wide_y = jnp.broadcast_to(column_y, (8, width))
    wide_z = jnp.broadcast_to(column_z, (8, width))
    geometry[0:8, :] = jnp.broadcast_to(column_key, (8, width))
    geometry[8:16, :] = jnp.where(
        ((sub == 2) & (wide_y < 2.0)) | ((sub == 3) & (wide_z < 2.0)), 0.0, -BIG
    )
    geometry[16:24, :] = jnp.where(
        ((sub == 2) & (wide_y >= NGY - 2.0)) | ((sub == 3) & (wide_z >= NGZ - 2.0)), 0.0, BIG
    )


def rest_kernel(
    bins, device_total, live, device, meta, far, highs, lows, along, channels, home, near, own
):
    low, middle, high = rest_of_grid(
        device, bins, meta, far, highs, lows, along, channels, near
    )
    place_own(own, low, middle, high, home[...])


def sides_kernel(bins, device_total, live, device, speeds, geometry, sides_ref):
    lane = iota((1, LANES), 1)
    key = geometry[0:1, :]
    left, right = jnp.maximum(device - 1, 0), jnp.minimum(device + 1, device_total - 1)
    for side, index in enumerate((left, right)):
        row = speeds[pl.ds(index, 1), :]
        numbers = [
            jnp.max(jnp.where(lane == META + b, row, 0.0), axis=1, keepdims=True)
            for b in range(bins)
        ]
        sides_ref[side] = placing(numbers, key, bins)


def second_kernel(
    bins, device_total, live, device, meta, old_ref, speeds, own, geometry, highs, lows, along,
    near, outer, inner, sides_ref, state_ref, new_speeds, far, new_highs, new_lows, new_along,
    channels, across, outbox, sem,
):
    rows = state_ref.shape[0] // ROWS
    around = halos(near, outer, inner, device, device_total)
    sides = [sides_ref[0], sides_ref[1]]

    def started(velocity):
        send_speed(velocity, old_ref[pl.ds(rows * MASS, rows), :], new_speeds, outbox, sem)

    def finish(state, velocity, affine):
        write_state(state_ref, state)
        to_grid(
            state, velocity, affine, state_ref, device, bins, meta, far, new_highs, new_lows,
            new_along, channels, across,
        )

    to_particles(
        live, old_ref, device, bins, device_total, geometry, own, sides, speeds, around, highs,
        lows, along, channels, started, finish, whole=True,
    )
    pltpu.make_async_copy(outbox, new_speeds, sem).wait()


def later_kernel(
    bins, device_total, live, device, old_ref, speeds, own, geometry, highs, lows, along,
    near, outer, inner, sides_ref, state_ref, motion_ref, new_speeds, shuffle, outbox, sem,
):
    around = halos(near, outer, inner, device, device_total)
    sides = [sides_ref[0], sides_ref[1]]
    advance(
        live, bins, device_total, device, old_ref, speeds, own, geometry, highs, lows, along, around,
        sides, state_ref, motion_ref, new_speeds, shuffle, outbox, sem,
    )


def advance(
    live, bins, device_total, device, old_ref, speeds, own, geometry, highs, lows, along, around,
    sides, state_ref, motion_ref, new_speeds, shuffle, outbox, sem,
):
    rows = state_ref.shape[0] // ROWS

    def started(velocity):
        send_speed(velocity, old_ref[pl.ds(rows * MASS, rows), :], new_speeds, outbox, sem)

    def finish(state, velocity, affine):
        write_state(state_ref, state)
        for number, value in enumerate(velocity + affine):
            motion_ref[pl.ds(rows * number, rows), :] = value

    to_particles(
        live, old_ref, device, bins, device_total, geometry, own, sides, speeds, around, highs,
        lows, along, shuffle, started, finish,
    )
    pltpu.make_async_copy(outbox, new_speeds, sem).wait()


def last_kernel(
    bins, device_total, live, device, old_ref, speeds, own, geometry, highs, lows, along,
    near, outer, inner, sides_ref, d_out, v_out, f_out, c_out, shuffle, d_rows,
    v_rows, f_rows, c_rows,
):
    rows = old_ref.shape[0] // ROWS
    quarters = rows // bins
    row_bin = iota((rows, LANES), 0) // quarters
    alive = row_bin < live[0]
    half = rows * LANES

    def finish(state, velocity, affine):
        results = (
            (d_out, state[TRAV : TRAV + 3], d_rows),
            (v_out, velocity, v_rows),
            (f_out, state[DEF : DEF + 9], f_rows),
            (c_out, affine, c_rows),
        )
        for ref, values, finished in results:
            count = len(values)
            for number in range(count):
                finished[pl.ds(rows * number, rows), :] = jnp.where(alive, values[number], 0.0)
            for s in range(rows):
                for start in range(0, count, 8):
                    size = min(8, count - start)
                    value = finished[rows_of(start, size, s, rows), :]
                    ref[pl.ds(start, size), pl.ds(LANES * s, LANES)] = value
            total = ref.shape[1]
            ref[:, pl.ds(half, total - half)] = jnp.zeros((count, total - half), F32)

    to_particles(
        None, old_ref, device, bins, device_total, geometry, own, [sides_ref[0], sides_ref[1]], speeds,
        halos(near, outer, inner, device, device_total), highs, lows, along, shuffle,
        lambda velocity: None, finish,
    )


def local(positions, velocity, deformation, affine, particle_mass, volume, bin_block, live_count):
    slot_total = bin_block.shape[0]
    per_bin = positions.shape[1] // slot_total
    bins = slot_total // 2
    device_total = lax.axis_size("space")
    rows = bins * per_bin // LANES
    half = rows * LANES
    nodes = bins * TILE
    width = bins * SLOT
    message = ((16, -(-(nodes + LANES // 2) // LANES) * LANES), F32)
    speeds_shape = ((device_total, LANES), F32)
    held = [((ROWS * rows, LANES), F32), ((12 * rows, LANES), F32), speeds_shape]
    grid_held = [
        message,
        ((bins, 3 * TILE, per_bin), BF16),
        ((bins, 3 * TILE, per_bin), BF16),
        ((12 * rows, LANES), F32),
        ((4 * 8 * rows, LANES), F32),
    ]
    meta_shape = ((8, message[0][1]), F32)
    own_shape = ((48, width), F32)
    geometry_shape = ((24, width), F32)
    home_shape = ((nodes, width), BF16)
    sides_shape = ((2, nodes, width), BF16)
    smem = pl.BlockSpec(memory_space=pltpu.SMEM)
    vmem = pl.BlockSpec(memory_space=pltpu.VMEM)
    anywhere = pl.BlockSpec(memory_space=pl.ANY)
    shuffle = pltpu.VMEM((4 * 8 * rows, LANES), F32)
    sending = [pltpu.VMEM((device_total, LANES), F32), pltpu.SemaphoreType.DMA]
    me = lax.axis_index("space").astype(jnp.int32).reshape(1)

    def stay(array, space=pltpu.VMEM):
        return array if INTERPRET else pltpu.with_memory_space_constraint(array, space)

    def call(body, scalars, arguments, outputs, scratch, in_specs=None, final=False):
        def kernel(*refs):
            count = len(scalars)
            body(bins, device_total, *refs[: count - 1], refs[count - 1][0], *refs[count:])

        out_specs = tuple(anywhere if output == speeds_shape else vmem for output in outputs)
        if in_specs is None:
            in_specs = [vmem] * len(arguments)
            arguments = [stay(argument) for argument in arguments]
        else:
            arguments = [stay(argument, pltpu.HBM) for argument in arguments]
        make = jax.ShapeDtypeStruct if final or INTERPRET else pltpu.VMEM
        return pl.pallas_call(
            kernel,
            in_specs=[smem] * len(scalars) + in_specs,
            out_shape=tuple(
                pltpu.HBM(*output) if output == speeds_shape and not INTERPRET else make(*output)
                for output in outputs
            ),
            out_specs=out_specs,
            scratch_shapes=scratch,
            interpret=INTERPRET,
            compiler_params=pltpu.CompilerParams(vmem_limit_bytes=GRANT),
        )(*scalars, *arguments)

    length = device_total
    swap_pairs = [(i, i ^ 1) for i in range(length)]
    inner_pairs = [(i, i ^ 3) for i in range(length)]
    outer_pairs = [(i, i + 1) for i in range(3, length - 1, 4)]
    outer_pairs = outer_pairs + [(i, i + 3) for i in range(2, length - 3, 4)]
    outer_pairs = outer_pairs + [(0, 1), (length - 2, length - 1)]
    outer_pairs = outer_pairs + [(j, i) for i, j in outer_pairs]

    slot_rows = [pltpu.VMEM((count, half), F32) for count in (3, 3, 9, 9)]
    *results, meta = call(
        first_kernel,
        (live_count, me),
        (bin_block, positions, velocity, deformation, affine, particle_mass, volume),
        [*held, meta_shape],
        sending
        + [pltpu.SMEM((slot_total,), jnp.int32)]
        + slot_rows
        + [pltpu.VMEM((half,), F32), pltpu.VMEM((half,), F32), pltpu.SemaphoreType.DMA((7,))],
        [anywhere] * 7,
    )
    across = pltpu.VMEM((12 * rows, LANES), F32)
    state, motion, speeds = results
    for step in range(STEPS):
        speeds = lax.all_to_all(speeds, "space", 0, 0, tiled=True)
        if step != 1:
            far, highs, lows, along, channels = call(
                scatter_kernel, (live_count, me), (state, motion, meta), grid_held, [across]
            )
        from_outer = lax.ppermute(far, "space", outer_pairs)
        from_inner = lax.ppermute(far, "space", inner_pairs)
        arguments = (meta, far, highs, lows, along, channels)
        if step == 0:
            near, own, geometry, home = call(
                first_rest_kernel,
                (live_count, me),
                arguments,
                [message, own_shape, geometry_shape, home_shape],
                [],
            )
        else:
            near, own = call(
                rest_kernel, (live_count, me), arguments + (home,), [message, own_shape], []
            )
        from_near = lax.ppermute(near, "space", swap_pairs)
        arguments = (
            state, speeds, own, geometry, highs, lows, along, from_near, from_outer, from_inner,
        )
        if step == 0:
            (sides,) = call(sides_kernel, (live_count, me), (speeds, geometry), [sides_shape], [])
            state, speeds, far, highs, lows, along, channels = call(
                second_kernel,
                (live_count, me),
                (meta, *arguments, sides),
                [held[0], speeds_shape, *grid_held],
                [across] + sending,
            )
        elif step < STEPS - 1:
            state, motion, speeds = call(
                later_kernel, (live_count, me), (*arguments, sides), held, [shuffle] + sending
            )
    total = positions.shape[1]
    return call(
        last_kernel,
        (live_count, me),
        (*arguments, sides),
        [((count, total), F32) for count in (3, 3, 9, 9)],
        [shuffle] + [pltpu.VMEM((count * rows, LANES), F32) for count in (3, 3, 9, 9)],
        final=True,
    )


def solution(mesh):
    in_specs = (
        P(None, "space"),
        P(None, "space"),
        P(None, "space"),
        P(None, "space"),
        P("space"),
        P("space"),
        P("space"),
        P("space"),
    )
    out_specs = (P(None, "space"), P(None, "space"), P(None, "space"), P(None, "space"))
    return jax.shard_map(local, mesh=mesh, in_specs=in_specs, out_specs=out_specs, check_vma=False)
```
